32 devices in a mesh: dp: 16 (over z, x, core), tensor: 2 (over y).
Axes of the slice: x: 2, y: 2, z: 4, core: 2. Of those that a mesh axis runs over, the one named last changes fastest.
Arguments:
- tokens: bfloat16 [2048, 1024], P(('dp', 'tensor')), may hold values from -6 to 6
- out_grad: bfloat16 [2048, 1024], P(('dp', 'tensor')), may hold values from -6 to 6
- lengths: int32 [16, 6], P('dp'), may hold values from 1 to 64, 128 in all within a row
- routes: int32 [2048, 8], P('dp'), may hold values from 0 to 31, all different within a row; in each aligned block of 128 rows (0 to 127, 128 to 255, ...) at most 48 rows name the same one
- attn_gain: float32 [1024], replicated, may hold values from 0.25 to 1.75
- w_query: bfloat16 [1024, 1024], P('dp', 'tensor'), may hold values from -0.1875 to 0.1875
- w_key: bfloat16 [1024, 512], P('dp', 'tensor'), may hold values from -0.1875 to 0.1875
- w_value: bfloat16 [1024, 512], P('dp', 'tensor'), may hold values from -0.1875 to 0.1875
- w_out: bfloat16 [1024, 1024], P('dp', 'tensor'), may hold values from -3 to 3
- ffn_gain: float32 [1024], replicated, may hold values from 0.25 to 1.75
- w_router: float32 [1024, 32], replicated, may hold values from -0.1875 to 0.1875
- w_gate: bfloat16 [32, 1024, 512], P(None, 'dp', 'tensor'), may hold values from -0.1875 to 0.1875
- w_up: bfloat16 [32, 1024, 512], P(None, 'dp', 'tensor'), may hold values from -0.1875 to 0.1875
- w_down: bfloat16 [32, 1024, 512], P(None, 'dp', 'tensor'), may hold values from -3 to 3
Outputs:
- block_out: bfloat16 [2048, 1024], P(('dp', 'tensor'))
- tokens_grad: float32 [2048, 1024], P(('dp', 'tensor'))
- attn_gain_grad: float32 [1024], replicated
- w_query_grad: float32 [1024, 1024], P('dp', 'tensor')
- w_key_grad: float32 [1024, 512], P('dp', 'tensor')
- w_value_grad: float32 [1024, 512], P('dp', 'tensor')
- w_out_grad: float32 [1024, 1024], P('dp', 'tensor')
- ffn_gain_grad: float32 [1024], replicated
- w_router_grad: float32 [1024, 32], replicated
- w_gate_grad: float32 [32, 1024, 512], P(None, 'dp', 'tensor')
- w_up_grad: float32 [32, 1024, 512], P(None, 'dp', 'tensor')
- w_down_grad: float32 [32, 1024, 512], P(None, 'dp', 'tensor')
The draws below stay inside these ranges and needn't reach their ends.
Inputs may be any that keep to these rules, and one draw needn't show every extreme that they name: Each group's lengths sum to 128. `routes`: each row names 8 different experts; within the rows of one dp group no expert is named more than 48 times.
All inputs are finite; a program needn't handle non-finite values.
Results may differ from the reference program's by a relative error of at most 0.012.
The reference program's roundings to bfloat16 on the way count: a program that leaves them out, or rounds other values in their place, can miss the bound.
Values may be sent and summed in bfloat16 or wider, within the bound.
A program may use at most 128 MiB of HBM per device.

```python
import math
import jax
import jax.numpy as jnp
import numpy as np
from jax import lax

D = 1024
HEADS = 16
KV_HEADS = 8
EXPERTS = 32
FFE = 512
TOPK = 8
TOK_DEV = 128
SEQS = 6
HEAD_DIM = 64
MAXLEN = 64
MOST = 48
GROUPS = 16
TOKENS = 2048
N_TENSOR = 2


def levels(own_key, extent, cuts, least, largest):
    factor_of, own = 1.0, jax.random.fold_in(own_key, 6)
    for axis_at, parts in cuts:
        steps = jnp.exp(jax.random.uniform(jax.random.fold_in(own, axis_at), (parts,), jnp.float32, least / len(cuts), largest / len(cuts)))
        factor_of = factor_of * jnp.repeat(steps, extent[axis_at] // parts).reshape([-1 if axis == axis_at else 1 for axis in range(len(extent))])
    return factor_of


def length_profile(amount, total, most, slope):
    portions = [(1 << 20) // math.isqrt(rank ** slope) + 1 for rank in range(2, amount + 1)]
    spare, counts = total - most - (amount - 1), [1] * (amount - 1)
    while spare > 0:
        movable = [i for i in range(amount - 1) if counts[i] < most]
        pool, left = sum([portions[i] for i in movable]), spare
        for i in movable:
            more = min(most - counts[i], max(1, left * portions[i] // pool), spare)
            counts[i] = counts[i] + more
            spare = spare - more
    return np.array([most] + counts)


def uneven_parts(rng, count, total, bound, slope):
    if count == 2:
        one = jax.random.randint(rng, (), max(1, total - bound), min(bound, total - 1) + 1)
        return jnp.stack([one, total - one])
    sizes = jnp.asarray(length_profile(count, total, bound, slope), jnp.int32)
    couples = (count - 1) // 2
    source_of, sink = sizes[1:1 + 2 * couples:2], sizes[2:2 + 2 * couples:2]
    margin = jnp.minimum(source_of - 1, bound - sink)
    moved = jax.random.randint(jax.random.fold_in(rng, 1), (couples,), 0, 1 << 20) % (margin + 1)
    sizes = sizes.at[1:1 + 2 * couples:2].set(source_of - moved).at[2:2 + 2 * couples:2].set(sink + moved)
    return sizes[jax.random.permutation(jax.random.fold_in(rng, 2), count)]


def shared_out(key, own, number, rows, amount, top, most, slope):
    ranking = jax.random.permutation(key, amount)
    heavy_load, common = load_shares(amount, rows * top, most, slope, True), load_shares(amount, rows * top, most, slope, False)
    places = jnp.arange(amount)

    def named(tallies, turn):
        used = int((tallies > 0).sum())
        fixed = max(1, used // 4)
        passed = fixed + (places - fixed + turn * (used - fixed)) % max(1, amount - fixed)
        return jnp.zeros((amount,), jnp.int32).at[ranking[jnp.where(places < fixed, places, passed)]].set(jnp.asarray(tallies, jnp.int32))

    tallies = jnp.where(number % 4 == 0, named(heavy_load, number // 4), named(common, number - number // 4 - 1))
    mixed = jax.random.permutation(jax.random.fold_in(own, 3), amount)
    donor, sink = mixed[0:amount // 2 * 2:2], mixed[1:amount // 2 * 2:2]
    slack = jnp.minimum(tallies[donor] - 1, most - tallies[sink]) // 2
    slack = jnp.where((donor == ranking[0]) | (sink == ranking[0]) | (tallies[sink] == 0), 0, jnp.maximum(slack, 0))
    passed = jax.random.randint(jax.random.fold_in(own, 4), (amount // 2,), 0, 1 << 20) % (slack + 1)
    tallies = tallies.at[donor].add(-passed).at[sink].add(passed)
    labels = jnp.searchsorted(jnp.cumsum(tallies), jnp.arange(rows * top), side="right").astype(jnp.int32)
    grid = labels.reshape(top, rows).T
    grid = grid[jax.random.permutation(jax.random.fold_in(own, 1), rows)]
    turn = jax.random.randint(jax.random.fold_in(own, 2), (rows, 1), 0, top)
    return jnp.take_along_axis(grid, (jnp.arange(top)[None, :] + turn) % top, axis=1)


def load_shares(count, total, most, lean, full):
    portions = [(1 << 20) // math.isqrt(rank ** lean) + 1 for rank in range(1, count + 1)]
    largest = most if full else min(most, max(-(-total // count), total * portions[0] // sum(portions)))
    least = 1 if total - largest >= count - 1 else 0
    counts, rest = [largest] + [least] * (count - 1), total - largest - least * (count - 1)
    while rest > 0:
        movable = [i for i in range(1, count) if counts[i] < largest] or [i for i in range(1, count) if counts[i] < most]
        pool, left = sum([portions[i] for i in movable]), rest
        for i in movable:
            more = min(most - counts[i], max(1, left * portions[i] // pool), rest)
            counts[i] = counts[i] + more
            rest = rest - more
    return np.array(counts)


def scatter_about(stream_key, extent, scale, reach, split=(), kind=jnp.bfloat16):
    result = scale * jax.random.normal(stream_key, extent, jnp.float32)
    if split:
        result = result * levels(stream_key, extent, split, -0.22, 0.18)
    return jnp.clip(result, -reach, reach).astype(kind)


def setup_inputs(seed: int = 0) -> dict:
    key_list = jax.random.split(jax.random.key(seed), 15)
    tokens = scatter_about(key_list[0], (TOKENS, D), 1.0, 6.0, ((0, 32),))
    out_grad = scatter_about(key_list[1], (TOKENS, D), 1.0, 6.0, ((0, 32),))
    lengths = jax.vmap(lambda own: uneven_parts(own, SEQS, TOK_DEV, MAXLEN, 2))(jax.random.split(key_list[2], GROUPS)).reshape((GROUPS, SEQS)).astype(jnp.int32)
    routes_keys = jax.random.split(jax.random.fold_in(key_list[3], 1), TOKENS // TOK_DEV)
    routes_turns = jax.random.permutation(jax.random.fold_in(key_list[3], 3), TOKENS // TOK_DEV)
    routes = jax.vmap(lambda own, number: shared_out(jax.random.fold_in(key_list[3], 2), own, number, TOK_DEV, EXPERTS, TOPK, MOST, 2))(routes_keys, routes_turns).reshape((TOKENS, TOPK))
    attn_gain = jnp.clip(1.0 + 0.15 * jax.random.normal(key_list[4], (D,), jnp.float32), 0.25, 1.75)
    w_query = scatter_about(key_list[5], (D, HEADS * HEAD_DIM), D ** -0.5, 0.1875, ((0, 16), (1, 2)))
    w_key = scatter_about(key_list[6], (D, KV_HEADS * HEAD_DIM), D ** -0.5, 0.1875, ((0, 16), (1, 2)))
    w_value = scatter_about(key_list[7], (D, KV_HEADS * HEAD_DIM), D ** -0.5, 0.1875, ((0, 16), (1, 2)))
    w_out = scatter_about(key_list[8], (D, HEADS * HEAD_DIM), 4 ** -0.5, 3.0, ((0, 16), (1, 2)))
    ffn_gain = jnp.clip(1.0 + 0.15 * jax.random.normal(key_list[9], (D,), jnp.float32), 0.25, 1.75)
    w_router = scatter_about(key_list[10], (D, EXPERTS), D ** -0.5, 0.1875, (), jnp.float32)
    w_gate = scatter_about(key_list[11], (EXPERTS, D, FFE), D ** -0.5, 0.1875, ((1, 16), (2, 2)))
    w_up = scatter_about(key_list[12], (EXPERTS, D, FFE), D ** -0.5, 0.1875, ((1, 16), (2, 2)))
    w_down = scatter_about(key_list[13], (EXPERTS, D, FFE), 0.5, 3.0, ((1, 16), (2, 2)))
    return dict(tokens=tokens, out_grad=out_grad, lengths=lengths, routes=routes, attn_gain=attn_gain, w_query=w_query, w_key=w_key, w_value=w_value, w_out=w_out, ffn_gain=ffn_gain, w_router=w_router, w_gate=w_gate, w_up=w_up, w_down=w_down)


eps_norm = 1e-06
residual_scale = 0.22
score_scale = 0.015625
rope_base = 10000.0
masked_score = -1e+30

def to_bf16(array_in):
    return lax.optimization_barrier(array_in.astype(jnp.bfloat16))

def norm_forward(row_block, gain_vec):
    rscale = lax.rsqrt(lax.optimization_barrier(jnp.mean(row_block * row_block, axis=1, keepdims=True)) + eps_norm)
    unit_rows = row_block * rscale
    return (unit_rows, rscale, (unit_rows * gain_vec).astype(jnp.bfloat16))

def norm_backward(gradient, unit_rows, rscale, gain_vec):
    unit_grad = gradient * gain_vec
    back_rows = rscale * (unit_grad - unit_rows * lax.optimization_barrier(jnp.mean(unit_grad * unit_rows, axis=1, keepdims=True)))
    return (back_rows, lax.optimization_barrier(jnp.sum(gradient * unit_rows, axis=0)))

def seq_layout(seq_lengths, row_count):
    seq_ends = jnp.cumsum(seq_lengths).astype(jnp.int32)
    starts = seq_ends - seq_lengths
    places = jnp.arange(row_count, dtype=jnp.int32)
    segment = lax.optimization_barrier(jnp.sum((places[:, None] >= seq_ends[None, :]).astype(jnp.int32), axis=1))
    member = segment[:, None] == jnp.arange(seq_lengths.shape[0], dtype=jnp.int32)[None, :]
    offset = lax.optimization_barrier(jnp.sum(jnp.where(member, starts[None, :], 0), axis=1)).astype(jnp.int32)
    allowed = (segment[:, None] == segment[None, :]) & (places[None, :] <= places[:, None])
    return (places - offset, allowed)

def rope_tables(position, head_width):
    frequency = rope_base ** (-(jnp.arange(head_width // 2, dtype=jnp.float32) * 2.0) / head_width)
    angles = position.astype(jnp.float32)[:, None] * frequency[None, :]
    cosine = jnp.concatenate([jnp.cos(angles), jnp.cos(angles)], axis=1)[:, None, :]
    sine_table = jnp.concatenate([jnp.sin(angles), jnp.sin(angles)], axis=1)[:, None, :]
    return (cosine, sine_table)

def rotate(vectors, cosine, sine_table):
    half_width = vectors.shape[-1] // 2
    first_half = vectors[..., :half_width]
    second_half = vectors[..., half_width:]
    return vectors * cosine + jnp.concatenate([-second_half, first_half], axis=-1) * sine_table

def unrotate(gradient, cosine, sine_table):
    half_width = gradient.shape[-1] // 2
    first_half = gradient[..., :half_width]
    second_half = gradient[..., half_width:]
    return gradient * cosine + jnp.concatenate([second_half, -first_half], axis=-1) * sine_table

def score_block(query_heads, key_heads, allowed):
    row_count, head_count, head_width = query_heads.shape
    kv_count = key_heads.shape[1]
    grouped = query_heads.astype(jnp.float32).reshape(row_count, kv_count, head_count // kv_count, head_width)
    scores = jnp.einsum('igrd,jgd->grij', grouped, key_heads.astype(jnp.float32)) * score_scale
    return (grouped, jnp.where(allowed[None, None], scores, masked_score))

def attend(query_heads, key_heads, value_heads, allowed):
    row_count, head_count, head_width = query_heads.shape
    grouped, scores = score_block(query_heads, key_heads, allowed)
    row_max = lax.optimization_barrier(jnp.max(scores, axis=-1, keepdims=True))
    log_total = row_max + jnp.log(lax.optimization_barrier(jnp.sum(jnp.exp(scores - row_max), axis=-1, keepdims=True)))
    prob_bf = to_bf16(jnp.exp(scores - log_total)).astype(jnp.float32)
    mixed_out = jnp.einsum('grij,jgd->igrd', prob_bf, value_heads.astype(jnp.float32))
    return (mixed_out.reshape(row_count, head_count * head_width).astype(jnp.bfloat16), log_total)

def attend_back(query_heads, key_heads, value_heads, allowed, log_total, mixed_grad):
    row_count, head_count, head_width = query_heads.shape
    kv_count = key_heads.shape[1]
    grouped, scores = score_block(query_heads, key_heads, allowed)
    prob_full = jnp.exp(scores - log_total)
    grad_heads = mixed_grad.astype(jnp.float32).reshape(row_count, kv_count, head_count // kv_count, head_width)
    dprobs = jnp.einsum('igrd,jgd->grij', grad_heads, value_heads.astype(jnp.float32))
    row_delta = lax.optimization_barrier(jnp.sum(prob_full * dprobs, axis=-1, keepdims=True))
    dscores = to_bf16(prob_full * (dprobs - row_delta)).astype(jnp.float32)
    dquery = jnp.einsum('grij,jgd->igrd', dscores, key_heads.astype(jnp.float32)) * score_scale
    key_grad = jnp.einsum('grij,igrd->jgd', dscores, grouped) * score_scale
    prob_bf = to_bf16(prob_full).astype(jnp.float32)
    dvalues = jnp.einsum('grij,igrd->jgd', prob_bf, grad_heads)
    return (dquery.reshape(row_count, head_count, head_width), key_grad, dvalues)

def group_pass(params, x_rows, grad_rows, seq_lengths, route_ids):
    attn_gain, w_query, w_key, w_value, w_out, ffn_gain, w_router, gate_full, up_full, down_full = params
    row_count = x_rows.shape[0]
    half_ff = FFE // N_TENSOR
    tokens_f32 = x_rows.astype(jnp.float32)
    position, allowed = seq_layout(seq_lengths, row_count)
    cosine, sine_table = rope_tables(position, HEAD_DIM)
    unit_first, scale_first, normed_first = norm_forward(tokens_f32, attn_gain)
    query_heads = rotate(jnp.dot(normed_first, w_query, preferred_element_type=jnp.float32).reshape(row_count, HEADS, HEAD_DIM), cosine, sine_table).astype(jnp.bfloat16)
    key_heads = rotate(jnp.dot(normed_first, w_key, preferred_element_type=jnp.float32).reshape(row_count, KV_HEADS, HEAD_DIM), cosine, sine_table).astype(jnp.bfloat16)
    value_heads = jnp.dot(normed_first, w_value, preferred_element_type=jnp.float32).astype(jnp.bfloat16).reshape(row_count, KV_HEADS, HEAD_DIM)
    mixed_out, log_total = attend(query_heads, key_heads, value_heads, allowed)
    hidden = tokens_f32 + residual_scale * jnp.dot(mixed_out, w_out.T, preferred_element_type=jnp.float32)
    unit_second, scale_second, normed_second = norm_forward(hidden, ffn_gain)
    expert_ids = jnp.arange(EXPERTS, dtype=jnp.int32)
    picked = route_ids[:, :, None] == expert_ids[None, None, :]
    logits = jnp.dot(normed_second.astype(jnp.float32), w_router, precision=lax.Precision.HIGHEST)
    chosen = lax.optimization_barrier(jnp.sum(jnp.where(picked, logits[:, None, :], 0.0), axis=2))
    gate_probs = jax.nn.softmax(chosen, axis=1)
    flat_ids = route_ids.reshape(-1)
    onehot = (flat_ids[:, None] == expert_ids[None, :]).astype(jnp.int32)
    ordinal = lax.optimization_barrier(jnp.sum((jnp.cumsum(onehot, axis=0) - 1) * onehot, axis=1))
    slot_index = (flat_ids * MOST + ordinal).astype(jnp.int32)
    token_of = jnp.arange(row_count * TOPK, dtype=jnp.int32) // TOPK
    rows_in = jnp.zeros((EXPERTS * MOST, D), jnp.bfloat16).at[slot_index].set(normed_second[token_of])
    rows_in = rows_in.reshape(EXPERTS, MOST, D).astype(jnp.float32)
    gate_pre = jnp.einsum('ecd,edf->ecf', rows_in, gate_full)
    up_pre = jnp.einsum('ecd,edf->ecf', rows_in, up_full)
    sigmoid_gate = jax.nn.sigmoid(gate_pre)
    activated = gate_pre * sigmoid_gate
    inner_act = to_bf16(activated * up_pre).astype(jnp.float32)
    down_split = down_full.reshape(EXPERTS, D, N_TENSOR, half_ff)
    out_split = to_bf16(jnp.einsum('ecnf,ednf->necd', inner_act.reshape(EXPERTS, MOST, N_TENSOR, half_ff), down_split)).astype(jnp.float32)
    routed = out_split.reshape(N_TENSOR, EXPERTS * MOST, D)[:, slot_index]
    routed_sum = lax.optimization_barrier(jnp.sum(routed, axis=0)).reshape(row_count, TOPK, D)
    moe_out = lax.optimization_barrier(jnp.sum(gate_probs[:, :, None] * routed_sum, axis=1))
    block_rows = (hidden + residual_scale * moe_out).astype(jnp.bfloat16)
    out_f32 = grad_rows.astype(jnp.float32)
    moe_grad = to_bf16(residual_scale * out_f32).astype(jnp.float32)
    gate_grad = lax.optimization_barrier(jnp.sum(moe_grad[:, None, :] * routed_sum, axis=2))
    route_grad = to_bf16(gate_probs[:, :, None] * moe_grad[:, None, :]).astype(jnp.float32)
    grad_in = jnp.zeros((EXPERTS * MOST, D), jnp.float32).at[slot_index].set(route_grad.reshape(row_count * TOPK, D))
    grad_in = grad_in.reshape(EXPERTS, MOST, D)
    inner_grad = jnp.einsum('ecd,edf->ecf', grad_in, down_full)
    gate_pre_grad = to_bf16(inner_grad * up_pre * sigmoid_gate * (1.0 + gate_pre * (1.0 - sigmoid_gate))).astype(jnp.float32)
    up_pre_grad = to_bf16(inner_grad * activated).astype(jnp.float32)
    gate_split = gate_full.reshape(EXPERTS, D, N_TENSOR, half_ff)
    up_split = up_full.reshape(EXPERTS, D, N_TENSOR, half_ff)
    back_split = jnp.einsum('ecnf,ednf->necd', gate_pre_grad.reshape(EXPERTS, MOST, N_TENSOR, half_ff), gate_split)
    back_split = back_split + jnp.einsum('ecnf,ednf->necd', up_pre_grad.reshape(EXPERTS, MOST, N_TENSOR, half_ff), up_split)
    back_split = to_bf16(back_split).astype(jnp.float32)
    routed_back = back_split.reshape(N_TENSOR, EXPERTS * MOST, D)[:, slot_index].reshape(N_TENSOR, row_count, TOPK, D)
    expert_back = lax.optimization_barrier(jnp.sum(routed_back, axis=(0, 2)))
    w_gate_grad = jnp.einsum('ecd,ecf->edf', rows_in, gate_pre_grad)
    w_up_grad = jnp.einsum('ecd,ecf->edf', rows_in, up_pre_grad)
    w_down_grad = jnp.einsum('ecd,ecf->edf', grad_in, inner_act)
    chosen_grad = gate_probs * (gate_grad - lax.optimization_barrier(jnp.sum(gate_probs * gate_grad, axis=1, keepdims=True)))
    logits_grad = lax.optimization_barrier(jnp.sum(jnp.where(picked, chosen_grad[:, :, None], 0.0), axis=1))
    second_grad = expert_back + jnp.dot(logits_grad, w_router.T, precision=lax.Precision.HIGHEST)
    w_router_grad = jnp.dot(normed_second.astype(jnp.float32).T, logits_grad, precision=lax.Precision.HIGHEST)
    hidden_back, ffn_gain_grad = norm_backward(second_grad, unit_second, scale_second, ffn_gain)
    hidden_grad = out_f32 + hidden_back
    attn_grad = (residual_scale * hidden_grad).astype(jnp.bfloat16)
    mixed_grad = jnp.dot(attn_grad, w_out, preferred_element_type=jnp.float32).astype(jnp.bfloat16)
    w_out_grad = jnp.dot(attn_grad.T, mixed_out, preferred_element_type=jnp.float32)
    dquery, key_grad, dvalues = attend_back(query_heads, key_heads, value_heads, allowed, log_total, mixed_grad)
    query_grad = unrotate(dquery, cosine, sine_table).astype(jnp.bfloat16).reshape(row_count, HEADS * HEAD_DIM)
    keys_grad = unrotate(key_grad, cosine, sine_table).astype(jnp.bfloat16).reshape(row_count, KV_HEADS * HEAD_DIM)
    value_grad = dvalues.astype(jnp.bfloat16).reshape(row_count, KV_HEADS * HEAD_DIM)
    w_query_grad = jnp.dot(normed_first.T, query_grad, preferred_element_type=jnp.float32)
    w_key_grad = jnp.dot(normed_first.T, keys_grad, preferred_element_type=jnp.float32)
    w_value_grad = jnp.dot(normed_first.T, value_grad, preferred_element_type=jnp.float32)
    first_grad = jnp.dot(query_grad, w_query.T, preferred_element_type=jnp.float32)
    first_grad = first_grad + jnp.dot(keys_grad, w_key.T, preferred_element_type=jnp.float32)
    first_grad = first_grad + jnp.dot(value_grad, w_value.T, preferred_element_type=jnp.float32)
    tokens_back, attn_gain_grad = norm_backward(first_grad, unit_first, scale_first, attn_gain)
    tokens_grad = hidden_grad + tokens_back
    grads = (attn_gain_grad, w_query_grad, w_key_grad, w_value_grad, w_out_grad, ffn_gain_grad, w_router_grad, w_gate_grad, w_up_grad, w_down_grad)
    return (block_rows, tokens_grad, grads)

def reference(tokens, out_grad, lengths, routes, attn_gain, w_query, w_key, w_value, w_out, ffn_gain, w_router, w_gate, w_up, w_down):
    params = (attn_gain, w_query, w_key, w_value, w_out, ffn_gain, w_router, w_gate.astype(jnp.float32), w_up.astype(jnp.float32), w_down.astype(jnp.float32))
    group_count = lengths.shape[0]
    row_count = tokens.shape[0] // group_count
    inputs = (tokens.reshape(group_count, row_count, D), out_grad.reshape(group_count, row_count, D), lengths, routes.reshape(group_count, row_count, TOPK))
    zero_totals = (jnp.zeros((D,), jnp.float32), jnp.zeros(w_query.shape, jnp.float32), jnp.zeros(w_key.shape, jnp.float32), jnp.zeros(w_value.shape, jnp.float32), jnp.zeros(w_out.shape, jnp.float32), jnp.zeros((D,), jnp.float32), jnp.zeros(w_router.shape, jnp.float32), jnp.zeros(w_gate.shape, jnp.float32), jnp.zeros(w_up.shape, jnp.float32), jnp.zeros(w_down.shape, jnp.float32))

    def group_step(totals_acc, group_item):
        block_rows, tokens_grad, grads = group_pass(params, group_item[0], group_item[1], group_item[2], group_item[3])
        return (jax.tree.map(jnp.add, totals_acc, grads), (block_rows, tokens_grad))
    totals, (block_all, grad_all) = lax.scan(group_step, zero_totals, inputs)
    return (block_all.reshape(-1, D), grad_all.reshape(-1, D), totals[0], totals[1], totals[2], totals[3], totals[4], totals[5], totals[6], totals[7], totals[8], totals[9])
```

```python
import functools

import jax
import jax.numpy as jnp
from jax import lax
from jax.experimental import pallas as pl
from jax.experimental.pallas import tpu as pltpu
from jax.sharding import PartitionSpec as P

EXPERTS = 32
TOPK = 8
HEAD_DIM = 64


eps_norm = 1e-06
residual_scale = 0.22
score_scale = 0.015625
rope_base = 10000.0
masked_score = -1e30


def norm_forward(row_block, gain_vec):
    rscale = lax.rsqrt(jnp.mean(row_block * row_block, axis=1, keepdims=True) + eps_norm)
    unit_rows = row_block * rscale
    return (unit_rows, rscale, (unit_rows * gain_vec).astype(jnp.bfloat16))


def norm_backward(gradient, unit_rows, rscale, gain_vec):
    unit_grad = gradient * gain_vec
    back_rows = rscale * (
        unit_grad - unit_rows * jnp.mean(unit_grad * unit_rows, axis=1, keepdims=True)
    )
    return (back_rows, jnp.sum(gradient * unit_rows, axis=0))


def seq_layout(seq_lengths, row_count):
    order = jnp.arange(seq_lengths.shape[0], dtype=jnp.int32)
    seq_ends = jnp.sum(jnp.where(order[:, None] <= order[None, :], seq_lengths[:, None], 0), axis=0)
    starts = seq_ends - seq_lengths
    places = jnp.arange(row_count, dtype=jnp.int32)
    segment = jnp.sum((places[:, None] >= seq_ends[None, :]).astype(jnp.int32), axis=1)
    member = segment[:, None] == jnp.arange(seq_lengths.shape[0], dtype=jnp.int32)[None, :]
    offset = jnp.sum(jnp.where(member, starts[None, :], 0), axis=1)
    allowed = (segment[:, None] == segment[None, :]) & (places[None, :] <= places[:, None])
    return (places - offset, allowed)


def rope_tables(position, head_width):
    frequency = rope_base ** (-(jnp.arange(head_width // 2, dtype=jnp.float32) * 2.0) / head_width)
    angles = position.astype(jnp.float32)[:, None] * frequency[None, :]
    cosine = jnp.concatenate([jnp.cos(angles), jnp.cos(angles)], axis=1)[:, None, :]
    sine_table = jnp.concatenate([jnp.sin(angles), jnp.sin(angles)], axis=1)[:, None, :]
    return (cosine, sine_table)


def rotate(vectors, cosine, sine_table):
    half_width = vectors.shape[-1] // 2
    first_half = vectors[..., :half_width]
    second_half = vectors[..., half_width:]
    return vectors * cosine + jnp.concatenate([-second_half, first_half], axis=-1) * sine_table


def unrotate(gradient, cosine, sine_table):
    half_width = gradient.shape[-1] // 2
    first_half = gradient[..., :half_width]
    second_half = gradient[..., half_width:]
    return gradient * cosine + jnp.concatenate([second_half, -first_half], axis=-1) * sine_table


def score_block(query_heads, key_heads, allowed):
    row_count, head_count, head_width = query_heads.shape
    kv_count = key_heads.shape[1]
    grouped = query_heads.reshape(row_count, kv_count, head_count // kv_count, head_width)
    scores = (
        jnp.einsum("igrd,jgd->grij", grouped, key_heads, preferred_element_type=jnp.float32)
        * score_scale
    )
    return (grouped, jnp.where(allowed[None, None], scores, masked_score))


def attend(query_heads, key_heads, value_heads, allowed):
    row_count, head_count, head_width = query_heads.shape
    grouped, scores = score_block(query_heads, key_heads, allowed)
    row_max = jnp.max(scores, axis=-1, keepdims=True)
    log_total = row_max + jnp.log(jnp.sum(jnp.exp(scores - row_max), axis=-1, keepdims=True))
    prob_bf = jnp.exp(scores - log_total).astype(jnp.bfloat16)
    mixed_out = jnp.einsum(
        "grij,jgd->igrd", prob_bf, value_heads, preferred_element_type=jnp.float32
    )
    return (mixed_out.reshape(row_count, head_count * head_width).astype(jnp.bfloat16), log_total)


def attend_back(query_heads, key_heads, value_heads, allowed, log_total, mixed_grad):
    row_count, head_count, head_width = query_heads.shape
    kv_count = key_heads.shape[1]
    grouped, scores = score_block(query_heads, key_heads, allowed)
    prob_full = jnp.exp(scores - log_total)
    grad_heads = mixed_grad.reshape(row_count, kv_count, head_count // kv_count, head_width)
    dprobs = jnp.einsum(
        "igrd,jgd->grij", grad_heads, value_heads, preferred_element_type=jnp.float32
    )
    row_delta = jnp.sum(prob_full * dprobs, axis=-1, keepdims=True)
    dscores = (prob_full * (dprobs - row_delta)).astype(jnp.bfloat16)
    dquery = (
        jnp.einsum("grij,jgd->igrd", dscores, key_heads, preferred_element_type=jnp.float32)
        * score_scale
    )
    key_grad = (
        jnp.einsum("grij,igrd->jgd", dscores, grouped, preferred_element_type=jnp.float32)
        * score_scale
    )
    dvalues = jnp.einsum(
        "grij,igrd->jgd",
        prob_full.astype(jnp.bfloat16),
        grad_heads,
        preferred_element_type=jnp.float32,
    )
    return (dquery.reshape(row_count, head_count, head_width), key_grad, dvalues)


def spread_rows(row_block):
    return lax.all_gather(row_block, "tensor", axis=0, tiled=True)


def narrow(partial_rows):
    if lax.axis_size("tensor") != 2:
        return lax.psum_scatter(partial_rows, "tensor", scatter_dimension=0, tiled=True)
    half = partial_rows.shape[0] // 2
    mine = lax.axis_index("tensor")
    away = lax.dynamic_slice_in_dim(partial_rows, (1 - mine) * half, half, 0)
    kept = lax.dynamic_slice_in_dim(partial_rows, mine * half, half, 0)
    return kept + lax.ppermute(away, "tensor", [(0, 1), (1, 0)])


def split_three(values):
    high = lax.reduce_precision(values, 8, 7)
    rest = values - high
    middle = lax.reduce_precision(rest, 8, 7)
    return [part.astype(jnp.bfloat16) for part in (high, middle, rest - middle)]


def dot_f32(left, right, dims):
    return lax.dot_general(left, right, (dims, ((), ())), preferred_element_type=jnp.float32)


def exact_dot(rows_bf, values, dims):
    width = values.shape[1]
    product = dot_f32(rows_bf, jnp.concatenate(split_three(values), axis=1), dims)
    return product[:, :width] + (product[:, width : 2 * width] + product[:, 2 * width :])


def gather_dp(rows, groups):
    return lax.all_gather(rows, "dp", axis=0, tiled=True, axis_index_groups=groups)


def scatter_dp(rows, groups):
    return lax.psum_scatter(
        rows, "dp", scatter_dimension=0, tiled=True, axis_index_groups=groups
    )


def gather_weights(packed):
    return lax.all_gather(packed, "dp", axis=0, tiled=True)


def scatter_weights(packed):
    return lax.psum_scatter(packed, "dp", scatter_dimension=0, tiled=True)


def share_kernel(x_ref, o_ref, send_sem, recv_sem, own_sem):
    width = lax.axis_size("tensor")
    count = lax.axis_size("dp") * width
    me = lax.axis_index("dp") * width + lax.axis_index("tensor")
    barrier = pltpu.get_barrier_semaphore()

    def place(k):
        peer = lax.rem(me + k, count)
        return (lax.div(peer, width), lax.rem(peer, width))

    def greet(k, carry):
        pl.semaphore_signal(
            barrier, inc=1, device_id=place(k), device_id_type=pl.DeviceIdType.MESH
        )
        return carry

    def copy(k, slot):
        return pltpu.make_async_remote_copy(
            src_ref=x_ref,
            dst_ref=o_ref.at[slot],
            send_sem=send_sem.at[k],
            recv_sem=recv_sem.at[k],
            device_id=place(k),
            device_id_type=pl.DeviceIdType.MESH,
        )

    def start(k, carry):
        copy(k, me).start()
        return carry

    def finish(k, carry):
        copy(k, me).wait_send()
        copy(k, lax.rem(me - k + count, count)).wait_recv()
        return carry

    lax.fori_loop(1, count, greet, 0)
    pl.semaphore_wait(barrier, count - 1)
    own = pltpu.make_async_copy(x_ref, o_ref.at[me], own_sem)
    own.start()
    lax.fori_loop(1, count, start, 0)
    lax.fori_loop(1, count, finish, 0)
    own.wait()


def share(block):
    count = lax.axis_size("dp") * lax.axis_size("tensor")
    return pl.pallas_call(
        share_kernel,
        out_shape=jax.ShapeDtypeStruct((count,) + block.shape, block.dtype),
        in_specs=[pl.BlockSpec(memory_space=pltpu.VMEM)],
        out_specs=pl.BlockSpec(memory_space=pltpu.VMEM),
        scratch_shapes=[
            pltpu.SemaphoreType.DMA((count,)),
            pltpu.SemaphoreType.DMA((count,)),
            pltpu.SemaphoreType.DMA,
        ],
        compiler_params=pltpu.CompilerParams(collective_id=0, has_side_effects=True),
        name="share",
    )(block)


MESH = pl.DeviceIdType.MESH


def greet_plane(count):
    me, side = lax.axis_index("dp"), lax.axis_index("tensor")
    barrier = pltpu.get_barrier_semaphore()

    def greet(k, carry):
        pl.semaphore_signal(
            barrier, inc=1, device_id=(lax.rem(me + k, count), side), device_id_type=MESH
        )
        return carry

    lax.fori_loop(1, count, greet, 0)
    pl.semaphore_wait(barrier, count - 1)


def far_first(i, count):
    return count // 2 + (1 - 2 * lax.rem(i, 2)) * lax.div(i + 1, 2)


def swap_kernel(home, count, holders, rows, *refs):
    ins, outs, (send_sem, recv_sem, own_sem) = refs[:3], refs[3:6], refs[6:]
    me, side = lax.axis_index("dp"), lax.axis_index("tensor")

    def of_expert(ref, peer):
        return ref.at[pl.ds(peer * holders, holders)]

    def of_rows(ref, peer):
        return ref.at[:, pl.ds(peer * rows, rows)]

    pick, put = (of_rows, of_expert) if home else (of_expert, of_rows)

    def copy(w, k, owner):
        peer = lax.rem(me + k, count)
        return pltpu.make_async_remote_copy(
            src_ref=pick(ins[w], peer),
            dst_ref=put(outs[w], owner),
            send_sem=send_sem.at[w, k],
            recv_sem=recv_sem.at[w, k],
            device_id=(peer, side),
            device_id_type=MESH,
        )

    greet_plane(count)

    def start(i, carry):
        for w in range(3):
            copy(w, far_first(i, count), me).start()
        return carry

    lax.fori_loop(0, count - 1, start, 0)
    own = [
        pltpu.make_async_copy(pick(ins[w], me), put(outs[w], me), own_sem.at[w]) for w in range(3)
    ]
    for each in own:
        each.start()

    def finish(i, carry):
        k = far_first(i, count)
        for w in range(3):
            copy(w, k, me).wait_send()
            copy(w, k, lax.rem(me - k + count, count)).wait_recv()
        return carry

    lax.fori_loop(0, count - 1, finish, 0)
    for each in own:
        each.wait()


def swap(arrays, home, collective_id):
    count = lax.axis_size("dp")
    first, second, width = arrays[0].shape
    if home:
        holders, rows = first, second // count
        shape = (holders * count, rows, width)
    else:
        holders, rows = first // count, second
        shape = (holders, rows * count, width)
    return pl.pallas_call(
        functools.partial(swap_kernel, home, count, holders, rows),
        out_shape=[jax.ShapeDtypeStruct(shape, a.dtype) for a in arrays],
        in_specs=[pl.BlockSpec(memory_space=pl.ANY)] * 3,
        out_specs=[pl.BlockSpec(memory_space=pl.ANY)] * 3,
        scratch_shapes=[
            pltpu.SemaphoreType.DMA((3, count)),
            pltpu.SemaphoreType.DMA((3, count)),
            pltpu.SemaphoreType.DMA((3,)),
        ],
        compiler_params=pltpu.CompilerParams(
            collective_id=collective_id, has_side_effects=True
        ),
        name="send_home" if home else "fetch",
    )(*arrays)


def local(
    tokens,
    out_grad,
    lengths,
    routes,
    attn_gain,
    w_query,
    w_key,
    w_value,
    w_out,
    ffn_gain,
    w_router,
    w_gate,
    w_up,
    w_down,
):
    local_rows = tokens.shape[0]
    row_count = routes.shape[0]
    model_width = tokens.shape[1]
    dp_count = lax.axis_size("dp")
    replicas = max(1, dp_count // EXPERTS)
    holders = max(1, EXPERTS // dp_count)
    clusters = EXPERTS // holders
    half_ff = w_gate.shape[2]
    heads_here = w_query.shape[1] // HEAD_DIM
    kv_here = w_key.shape[1] // HEAD_DIM
    own_row = lax.axis_index("tensor") * local_rows
    groups = (
        None
        if replicas == 1
        else [[r * clusters + c for c in range(clusters)] for r in range(replicas)]
    )
    q_cols, k_cols = w_query.shape[1], w_key.shape[1]
    cuts = (q_cols, q_cols + k_cols, q_cols + 2 * k_cols)
    packed_attn = gather_weights(jnp.concatenate([w_query, w_key, w_value, w_out], axis=1))
    full_qkv = packed_attn[:, : cuts[2]]
    full_out = packed_attn[:, cuts[2] :]

    def spread_out(weight):
        grouped = weight.reshape(clusters, holders, weight.shape[1], half_ff)
        return jnp.broadcast_to(grouped[None], (replicas,) + grouped.shape).reshape(
            dp_count, holders, weight.shape[1], half_ff
        )

    def fetch(weight):
        moved = lax.all_to_all(spread_out(weight), "dp", split_axis=0, concat_axis=2, tiled=True)
        return moved.reshape(holders, model_width, half_ff)

    if replicas == 1:
        local_gate, local_up, local_down = swap([w_gate, w_up, w_down], False, 1)
    else:
        local_gate, local_up, local_down = fetch(w_gate), fetch(w_up), fetch(w_down)
    tokens_f32 = tokens.astype(jnp.float32)
    out_f32 = out_grad.astype(jnp.float32)
    position, allowed = seq_layout(lengths[0], row_count)
    cosine, sine_table = rope_tables(position, HEAD_DIM)
    unit_first, scale_first, normed_first = norm_forward(tokens_f32, attn_gain)
    both = spread_rows(
        jnp.concatenate(
            [normed_first, (residual_scale * out_f32).astype(jnp.bfloat16)], axis=1
        )
    )
    wide_first = both[:, :model_width]
    tagged = jnp.concatenate(
        [
            both[:, model_width:],
            jnp.pad(routes.astype(jnp.bfloat16), ((0, 0), (0, 128 - TOPK))),
        ],
        axis=1,
    )
    tagged_all = gather_dp(tagged, groups)
    moe_all = tagged_all[:, :model_width]
    routes_all = tagged_all[:, model_width : model_width + TOPK].astype(jnp.int32)
    qkv = jnp.dot(wide_first, full_qkv, preferred_element_type=jnp.float32)
    query_heads = rotate(
        qkv[:, : cuts[0]].reshape(row_count, heads_here, HEAD_DIM), cosine, sine_table
    ).astype(jnp.bfloat16)
    key_heads = rotate(
        qkv[:, cuts[0] : cuts[1]].reshape(row_count, kv_here, HEAD_DIM), cosine, sine_table
    ).astype(jnp.bfloat16)
    value_heads = qkv[:, cuts[1] :].astype(jnp.bfloat16).reshape(row_count, kv_here, HEAD_DIM)
    mixed_out, log_total = attend(query_heads, key_heads, value_heads, allowed)
    hidden = tokens_f32 + residual_scale * narrow(dot_f32(mixed_out, full_out, ((1,), (1,))))
    unit_second, scale_second, normed_second = norm_forward(hidden, ffn_gain)
    rows_all = gather_dp(spread_rows(normed_second), groups)

    expert_ids = jnp.arange(EXPERTS, dtype=jnp.int32)

    def gate_of(rows_bf, row_routes):
        picked = row_routes[:, :, None] == expert_ids[None, None, :]
        logits = exact_dot(rows_bf, w_router, ((1,), (0,)))
        named = jnp.any(picked, axis=1)
        masked = jnp.where(named, logits, -jnp.inf)
        raised = jnp.exp(masked - jnp.max(masked, axis=1, keepdims=True))
        return picked, named, raised / jnp.sum(raised, axis=1, keepdims=True)

    _, named_all, gates_all = gate_of(rows_all, routes_all)
    first_expert = lax.axis_index("dp") % clusters * holders
    out_part = back_part = gate_slots = 0.0
    grads = []
    for h in range(holders):
        gate = lax.dynamic_slice_in_dim(gates_all, first_expert + h, 1, 1)
        here = lax.dynamic_slice_in_dim(named_all, first_expert + h, 1, 1)
        gate_pre = dot_f32(rows_all, local_gate[h], ((1,), (0,)))
        up_pre = dot_f32(rows_all, local_up[h], ((1,), (0,)))
        sigmoid_gate = jax.nn.sigmoid(gate_pre)
        activated = gate_pre * sigmoid_gate
        inner_act = (activated * up_pre).astype(jnp.bfloat16)
        produced = dot_f32(inner_act, local_down[h], ((1,), (1,))).astype(jnp.bfloat16)
        produced = produced.astype(jnp.float32)
        out_part = out_part + jnp.where(here, gate * produced, 0.0)
        moe_f32 = moe_all.astype(jnp.float32)
        gate_part = jnp.sum(moe_f32 * produced, axis=1, keepdims=True)
        gate_slots = gate_slots + jnp.where(routes_all == first_expert + h, gate_part, 0.0)
        route_grad = jnp.where(here, gate * moe_f32, 0.0).astype(jnp.bfloat16)
        inner_grad = dot_f32(route_grad, local_down[h], ((1,), (0,)))
        gate_pre_grad = (
            inner_grad * up_pre * sigmoid_gate * (1.0 + gate_pre * (1.0 - sigmoid_gate))
        ).astype(jnp.bfloat16)
        up_pre_grad = (inner_grad * activated).astype(jnp.bfloat16)
        back = dot_f32(gate_pre_grad, local_gate[h], ((1,), (1,))) + dot_f32(
            up_pre_grad, local_up[h], ((1,), (1,))
        )
        back_part = back_part + back.astype(jnp.bfloat16).astype(jnp.float32)
        grads.append(
            (
                dot_f32(rows_all, gate_pre_grad, ((0,), (0,))).astype(jnp.bfloat16),
                dot_f32(rows_all, up_pre_grad, ((0,), (0,))).astype(jnp.bfloat16),
                dot_f32(route_grad, inner_act, ((0,), (0,))).astype(jnp.bfloat16),
            )
        )
    slot_parts = split_three(gate_slots)
    pad = jnp.zeros((rows_all.shape[0], 128 - 3 * TOPK), jnp.bfloat16)
    home = scatter_dp(
        jnp.concatenate(
            [back_part.astype(jnp.bfloat16)] + slot_parts + [pad, out_part.astype(jnp.bfloat16)],
            axis=1,
        ),
        groups,
    ).astype(jnp.float32)
    back_home = home[:, : model_width + 128]
    out_home = home[:, model_width + 128 :]
    slots = back_home[:, model_width:]
    gate_half = slots[:, :TOPK] + slots[:, TOPK : 2 * TOPK] + slots[:, 2 * TOPK : 3 * TOPK]
    own_back = narrow(
        jnp.concatenate(
            [back_home[:, :model_width], jnp.pad(gate_half, ((0, 0), (0, 128 - TOPK)))], axis=1
        )
    )
    expert_back = own_back[:, :model_width]
    gate_grad = own_back[:, model_width : model_width + TOPK]
    block_rows = (hidden + residual_scale * narrow(out_home)).astype(jnp.bfloat16)

    if replicas == 1:
        stacks = [jnp.stack([grads[h][i] for h in range(holders)]) for i in range(3)]
        moved_home = [g.astype(jnp.float32) for g in swap(stacks, True, 2)]

    def send_home(index):
        if replicas == 1:
            return moved_home[index]
        stacked = jnp.stack([grads[h][index] for h in range(holders)])
        moved = lax.all_to_all(stacked[None], "dp", split_axis=2, concat_axis=0, tiled=True)
        return jnp.sum(
            moved.astype(jnp.float32).reshape(
                replicas, clusters * holders, moved.shape[2], half_ff
            ),
            axis=0,
        )

    own_routes = lax.dynamic_slice_in_dim(routes, own_row, local_rows, 0)
    picked_own, _, gates_dense = gate_of(normed_second, own_routes)
    gates_own = jnp.sum(jnp.where(picked_own, gates_dense[:, None, :], 0.0), axis=2)
    chosen_grad = gates_own * (gate_grad - jnp.sum(gates_own * gate_grad, axis=1, keepdims=True))
    logits_grad = jnp.sum(jnp.where(picked_own, chosen_grad[:, :, None], 0.0), axis=1)
    second_grad = expert_back + jnp.dot(logits_grad, w_router.T, precision=lax.Precision.HIGHEST)
    hidden_back, ffn_gain_grad = norm_backward(second_grad, unit_second, scale_second, ffn_gain)
    hidden_grad = out_f32 + hidden_back
    attn_grad = spread_rows((residual_scale * hidden_grad).astype(jnp.bfloat16))
    mixed_grad = jnp.dot(attn_grad, full_out, preferred_element_type=jnp.float32).astype(
        jnp.bfloat16
    )
    out_w_grad = dot_f32(attn_grad, mixed_out, ((0,), (0,)))
    dquery, key_grad, dvalues = attend_back(
        query_heads, key_heads, value_heads, allowed, log_total, mixed_grad
    )
    query_grad = (
        unrotate(dquery, cosine, sine_table)
        .astype(jnp.bfloat16)
        .reshape(row_count, heads_here * HEAD_DIM)
    )
    keys_grad = (
        unrotate(key_grad, cosine, sine_table)
        .astype(jnp.bfloat16)
        .reshape(row_count, kv_here * HEAD_DIM)
    )
    value_grad = dvalues.astype(jnp.bfloat16).reshape(row_count, kv_here * HEAD_DIM)
    qkv_grad = jnp.concatenate([query_grad, keys_grad, value_grad], axis=1)
    qkv_w_grad = dot_f32(wide_first, qkv_grad, ((0,), (0,)))
    packed_grad = scatter_weights(
        jnp.concatenate([qkv_w_grad, out_w_grad], axis=1).astype(jnp.bfloat16)
    ).astype(jnp.float32)
    first_grad = narrow(dot_f32(qkv_grad, full_qkv, ((1,), (1,))))
    tokens_back, attn_gain_grad = norm_backward(first_grad, unit_first, scale_first, attn_gain)
    tokens_grad = hidden_grad + tokens_back
    if replicas == 1:
        tall = local_rows * EXPERTS // 128
        wide = model_width // 128
        shared = share(
            jnp.concatenate(
                [
                    logits_grad.reshape(tall, 128),
                    attn_gain_grad.reshape(wide, 128),
                    ffn_gain_grad.reshape(wide, 128),
                ],
                axis=0,
            )
        )
        logits_grad_all = shared[:, :tall].reshape(rows_all.shape[0], EXPERTS)
        router_total = exact_dot(rows_all, logits_grad_all, ((0,), (0,)))
        gains = jnp.sum(shared[:, tall:], axis=0).reshape(2, model_width)
        attn_gain_total, ffn_gain_total = gains[0], gains[1]
    else:
        attn_gain_total, ffn_gain_total, router_total = lax.psum(
            (
                attn_gain_grad,
                ffn_gain_grad,
                exact_dot(normed_second, logits_grad, ((0,), (0,))),
            ),
            ("dp", "tensor"),
        )
    return (
        block_rows,
        tokens_grad,
        attn_gain_total,
        packed_grad[:, : cuts[0]],
        packed_grad[:, cuts[0] : cuts[1]],
        packed_grad[:, cuts[1] : cuts[2]],
        packed_grad[:, cuts[2] :],
        ffn_gain_total,
        router_total,
        send_home(0),
        send_home(1),
        send_home(2),
    )


def solution(mesh):
    placed = (
        P(("dp", "tensor"), None),
        P(("dp", "tensor"), None),
        P("dp", None),
        P("dp", None),
        P(),
        P("dp", "tensor"),
        P("dp", "tensor"),
        P("dp", "tensor"),
        P("dp", "tensor"),
        P(),
        P(),
        P(None, "dp", "tensor"),
        P(None, "dp", "tensor"),
        P(None, "dp", "tensor"),
    )
    return jax.shard_map(
        local,
        mesh=mesh,
        in_specs=placed,
        out_specs=(
            P(("dp", "tensor"), None),
            P(("dp", "tensor"), None),
            P(),
            P("dp", "tensor"),
            P("dp", "tensor"),
            P("dp", "tensor"),
            P("dp", "tensor"),
            P(),
            P(),
            P(None, "dp", "tensor"),
            P(None, "dp", "tensor"),
            P(None, "dp", "tensor"),
        ),
        check_vma=False,
    )
```

```python
import functools

import jax
import jax.numpy as jnp
from jax import lax
from jax.experimental import pallas as pl
from jax.experimental.pallas import tpu as pltpu
from jax.sharding import PartitionSpec as P

EXPERTS = 32
TOPK = 8
HEAD_DIM = 64


eps_norm = 1e-06
residual_scale = 0.22
score_scale = 0.015625
rope_base = 10000.0
masked_score = -1e30


def norm_forward(row_block, gain_vec):
    rscale = lax.rsqrt(jnp.mean(row_block * row_block, axis=1, keepdims=True) + eps_norm)
    unit_rows = row_block * rscale
    return (unit_rows, rscale, (unit_rows * gain_vec).astype(jnp.bfloat16))


def norm_backward(gradient, unit_rows, rscale, gain_vec):
    unit_grad = gradient * gain_vec
    back_rows = rscale * (
        unit_grad - unit_rows * jnp.mean(unit_grad * unit_rows, axis=1, keepdims=True)
    )
    return (back_rows, jnp.sum(gradient * unit_rows, axis=0))


def seq_layout(seq_lengths, row_count):
    order = jnp.arange(seq_lengths.shape[0], dtype=jnp.int32)
    seq_ends = jnp.sum(jnp.where(order[:, None] <= order[None, :], seq_lengths[:, None], 0), axis=0)
    starts = seq_ends - seq_lengths
    places = jnp.arange(row_count, dtype=jnp.int32)
    segment = jnp.sum((places[:, None] >= seq_ends[None, :]).astype(jnp.int32), axis=1)
    member = segment[:, None] == jnp.arange(seq_lengths.shape[0], dtype=jnp.int32)[None, :]
    offset = jnp.sum(jnp.where(member, starts[None, :], 0), axis=1)
    allowed = (segment[:, None] == segment[None, :]) & (places[None, :] <= places[:, None])
    return (places - offset, allowed)


def rope_tables(position, head_width):
    frequency = rope_base ** (-(jnp.arange(head_width // 2, dtype=jnp.float32) * 2.0) / head_width)
    angles = position.astype(jnp.float32)[:, None] * frequency[None, :]
    cosine = jnp.concatenate([jnp.cos(angles), jnp.cos(angles)], axis=1)[:, None, :]
    sine_table = jnp.concatenate([jnp.sin(angles), jnp.sin(angles)], axis=1)[:, None, :]
    return (cosine, sine_table)


def rotate(vectors, cosine, sine_table):
    half_width = vectors.shape[-1] // 2
    first_half = vectors[..., :half_width]
    second_half = vectors[..., half_width:]
    return vectors * cosine + jnp.concatenate([-second_half, first_half], axis=-1) * sine_table


def unrotate(gradient, cosine, sine_table):
    half_width = gradient.shape[-1] // 2
    first_half = gradient[..., :half_width]
    second_half = gradient[..., half_width:]
    return gradient * cosine + jnp.concatenate([second_half, -first_half], axis=-1) * sine_table


def score_block(query_heads, key_heads, allowed):
    row_count, head_count, head_width = query_heads.shape
    kv_count = key_heads.shape[1]
    grouped = query_heads.reshape(row_count, kv_count, head_count // kv_count, head_width)
    scores = (
        jnp.einsum("igrd,jgd->grij", grouped, key_heads, preferred_element_type=jnp.float32)
        * score_scale
    )
    return (grouped, jnp.where(allowed[None, None], scores, masked_score))


def attend(query_heads, key_heads, value_heads, allowed):
    row_count, head_count, head_width = query_heads.shape
    grouped, scores = score_block(query_heads, key_heads, allowed)
    row_max = jnp.max(scores, axis=-1, keepdims=True)
    log_total = row_max + jnp.log(jnp.sum(jnp.exp(scores - row_max), axis=-1, keepdims=True))
    prob_bf = jnp.exp(scores - log_total).astype(jnp.bfloat16)
    mixed_out = jnp.einsum(
        "grij,jgd->igrd", prob_bf, value_heads, preferred_element_type=jnp.float32
    )
    return (mixed_out.reshape(row_count, head_count * head_width).astype(jnp.bfloat16), log_total)


def attend_back(query_heads, key_heads, value_heads, allowed, log_total, mixed_grad):
    row_count, head_count, head_width = query_heads.shape
    kv_count = key_heads.shape[1]
    grouped, scores = score_block(query_heads, key_heads, allowed)
    prob_full = jnp.exp(scores - log_total)
    grad_heads = mixed_grad.reshape(row_count, kv_count, head_count // kv_count, head_width)
    dprobs = jnp.einsum(
        "igrd,jgd->grij", grad_heads, value_heads, preferred_element_type=jnp.float32
    )
    row_delta = jnp.sum(prob_full * dprobs, axis=-1, keepdims=True)
    dscores = (prob_full * (dprobs - row_delta)).astype(jnp.bfloat16)
    dquery = (
        jnp.einsum("grij,jgd->igrd", dscores, key_heads, preferred_element_type=jnp.float32)
        * score_scale
    )
    key_grad = (
        jnp.einsum("grij,igrd->jgd", dscores, grouped, preferred_element_type=jnp.float32)
        * score_scale
    )
    dvalues = jnp.einsum(
        "grij,igrd->jgd",
        prob_full.astype(jnp.bfloat16),
        grad_heads,
        preferred_element_type=jnp.float32,
    )
    return (dquery.reshape(row_count, head_count, head_width), key_grad, dvalues)


def spread_rows(row_block):
    return lax.all_gather(row_block, "tensor", axis=0, tiled=True)


def narrow(partial_rows):
    if lax.axis_size("tensor") != 2:
        return lax.psum_scatter(partial_rows, "tensor", scatter_dimension=0, tiled=True)
    half = partial_rows.shape[0] // 2
    mine = lax.axis_index("tensor")
    away = lax.dynamic_slice_in_dim(partial_rows, (1 - mine) * half, half, 0)
    kept = lax.dynamic_slice_in_dim(partial_rows, mine * half, half, 0)
    return kept + lax.ppermute(away, "tensor", [(0, 1), (1, 0)])


def split_three(values):
    high = lax.reduce_precision(values, 8, 7)
    rest = values - high
    middle = lax.reduce_precision(rest, 8, 7)
    return [part.astype(jnp.bfloat16) for part in (high, middle, rest - middle)]


def dot_f32(left, right, dims):
    return lax.dot_general(left, right, (dims, ((), ())), preferred_element_type=jnp.float32)


def exact_dot(rows_bf, values, dims):
    width = values.shape[1]
    product = dot_f32(rows_bf, jnp.concatenate(split_three(values), axis=1), dims)
    return product[:, :width] + (product[:, width : 2 * width] + product[:, 2 * width :])


def gather_dp(rows, groups):
    return lax.all_gather(rows, "dp", axis=0, tiled=True, axis_index_groups=groups)


def scatter_dp(rows, groups):
    return lax.psum_scatter(
        rows, "dp", scatter_dimension=0, tiled=True, axis_index_groups=groups
    )


def gather_weights(packed):
    return lax.all_gather(packed, "dp", axis=0, tiled=True)


def scatter_weights(packed):
    return lax.psum_scatter(packed, "dp", scatter_dimension=0, tiled=True)


MESH = pl.DeviceIdType.MESH
WEIGHT = {"core": 1, "x": 2, "z0": 4, "z1": 8}
DIMS = ("z1", "z0", "x", "t")
ORDERS = (("x", "t", "z0", "z1"), ("t", "z0", "x", "z1"), ("z0", "x", "z1", "t"))


def bit_of(me, weight):
    return lax.rem(lax.div(me, weight), 2)


def partner(name):
    me, side = lax.axis_index("dp"), lax.axis_index("tensor")
    if name == "t":
        return (me, 1 - side)
    return (me + WEIGHT[name] * (1 - 2 * bit_of(me, WEIGHT[name])), side)


def greet_plane(count, others=()):
    me, side = lax.axis_index("dp"), lax.axis_index("tensor")
    barrier = pltpu.get_barrier_semaphore()

    def greet(k, carry):
        pl.semaphore_signal(
            barrier, inc=1, device_id=(lax.rem(me + k, count), side), device_id_type=MESH
        )
        return carry

    lax.fori_loop(1, count, greet, 0)
    for place in others:
        pl.semaphore_signal(barrier, inc=1, device_id=place, device_id_type=MESH)
    pl.semaphore_wait(barrier, count - 1 + len(others))


def far_first(i, count):
    return count // 2 + (1 - 2 * lax.rem(i, 2)) * lax.div(i + 1, 2)


class Swap:
    def __init__(self, home, count, ins, outs, send_sem, recv_sem, own_sem):
        self.home, self.count = home, count
        self.ins, self.outs = ins, outs
        self.sems = (send_sem, recv_sem, own_sem)
        if home:
            self.holders, self.rows = ins[0].shape[0], ins[0].shape[1] // count
        else:
            self.holders, self.rows = ins[0].shape[0] // count, ins[0].shape[1]

    def pick(self, ref, peer, home):
        if home:
            return ref.at[:, pl.ds(peer * self.rows, self.rows)]
        return ref.at[pl.ds(peer * self.holders, self.holders)]

    def copy(self, w, k, owner):
        me, side = lax.axis_index("dp"), lax.axis_index("tensor")
        peer = lax.rem(me + k, self.count)
        return pltpu.make_async_remote_copy(
            src_ref=self.pick(self.ins[w], peer, self.home),
            dst_ref=self.pick(self.outs[w], owner, not self.home),
            send_sem=self.sems[0].at[w, k],
            recv_sem=self.sems[1].at[w, k],
            device_id=(peer, side),
            device_id_type=MESH,
        )

    def own(self, w):
        me = lax.axis_index("dp")
        return pltpu.make_async_copy(
            self.pick(self.ins[w], me, self.home),
            self.pick(self.outs[w], me, not self.home),
            self.sems[2].at[w],
        )

    def start(self):
        def step(i, carry):
            for w in range(3):
                self.copy(w, far_first(i, self.count), lax.axis_index("dp")).start()
            return carry

        lax.fori_loop(0, self.count - 1, step, 0)
        for w in range(3):
            self.own(w).start()

    def finish(self):
        me = lax.axis_index("dp")

        def step(i, carry):
            k = far_first(i, self.count)
            for w in range(3):
                self.copy(w, k, me).wait_send()
                self.copy(w, k, lax.rem(me - k + self.count, self.count)).wait_recv()
            return carry

        lax.fori_loop(0, self.count - 1, step, 0)
        for w in range(3):
            self.own(w).wait()

    @staticmethod
    def sems(count):
        return [
            pltpu.SemaphoreType.DMA((3, count)),
            pltpu.SemaphoreType.DMA((3, count)),
            pltpu.SemaphoreType.DMA((3,)),
        ]


def fetch_kernel(count, *refs):
    job = Swap(False, count, refs[:3], refs[3:6], *refs[6:])
    greet_plane(count)
    job.start()
    job.finish()


def fetch_experts(arrays):
    count = lax.axis_size("dp")
    experts, rows, width = arrays[0].shape
    return pl.pallas_call(
        functools.partial(fetch_kernel, count),
        out_shape=[
            jax.ShapeDtypeStruct((experts // count, rows * count, width), a.dtype) for a in arrays
        ],
        in_specs=[pl.BlockSpec(memory_space=pl.ANY)] * 3,
        out_specs=[pl.BlockSpec(memory_space=pl.ANY)] * 3,
        scratch_shapes=Swap.sems(count),
        compiler_params=pltpu.CompilerParams(collective_id=1, has_side_effects=True),
        name="fetch_experts",
    )(*arrays)


class Sum:
    def __init__(self, pieces, ins, outs, accs, bufs, send_sem, recv_sem):
        me, side = lax.axis_index("dp"), lax.axis_index("tensor")
        self.pieces, self.ins, self.outs, self.accs, self.bufs = pieces, ins, outs, accs, bufs
        self.send_sem, self.recv_sem = send_sem, recv_sem
        self.core = bit_of(me, 1)
        self.whole = "t" in pieces[0][3]
        self.last = len(pieces[0][3])
        self.mine = {
            "z1": bit_of(me, 8),
            "z0": bit_of(me, 4),
            "x": bit_of(me, 2),
            "t": side if self.whole else 0,
        }

    def exchange(self, i, s):
        which, first, width, order = self.pieces[i]
        columns = pl.ds(first, width)
        if s == 0:
            src = self.ins[which].at[:, :, :, 1 - self.core, :, :, columns]
            place = partner("core")
        else:
            done, now = order[: s - 1], order[s - 1]
            index = []
            for d in DIMS:
                if d in done:
                    index.append(pl.ds(self.mine[d], 1))
                elif d == now:
                    index.append(pl.ds(1 - self.mine[d], 1))
                else:
                    index.append(slice(None))
            src = self.accs[which].at[tuple(index) + (slice(None), columns)]
            place = partner(now)
        return pltpu.make_async_remote_copy(
            src_ref=src,
            dst_ref=self.bufs[i * (self.last + 1) + s],
            send_sem=self.send_sem.at[i, s],
            recv_sem=self.recv_sem.at[i, s],
            device_id=place,
            device_id_type=MESH,
        )

    def add(self, i, s):
        which, first, width, order = self.pieces[i]
        buf = self.bufs[i * (self.last + 1) + s]
        columns = pl.ds(first, width)
        if s == self.last:
            at = tuple(self.mine[d] for d in DIMS) + (slice(None), columns)
            self.outs[which][:, columns] = self.accs[which][at].astype(jnp.float32) + buf[
                0, 0, 0, 0
            ].astype(jnp.float32)
            return
        free = [d for d in DIMS if d in order[s:]]

        def step(b, carry):
            at, frm = dict(self.mine), {d: 0 for d in DIMS}
            left = b
            for d in reversed(free):
                at[d] = frm[d] = lax.rem(left, 2)
                left = lax.div(left, 2)
            at = tuple(at[d] for d in DIMS)
            if s == 0:
                have = self.ins[which][at[:3] + (self.core, at[3], slice(None), columns)]
            else:
                have = self.accs[which][at + (slice(None), columns)]
            got = buf[tuple(frm[d] for d in DIMS)]
            self.accs[which][at + (slice(None), columns)] = (
                have.astype(jnp.float32) + got.astype(jnp.float32)
            ).astype(jnp.bfloat16)
            return carry

        lax.fori_loop(0, 2 ** len(free), step, 0)

    def start(self):
        for i in range(len(self.pieces)):
            self.exchange(i, 0).start()

    def run(self):
        n = len(self.pieces)
        for s in range(self.last + 1):
            for i in range(n):
                self.exchange(i, s).wait_recv()
                self.add(i, s)
                if s < self.last:
                    self.exchange(i, s + 1).start()
        for s in range(self.last + 1):
            for i in range(n):
                self.exchange(i, s).wait_send()

    @staticmethod
    def scratch(pieces, rows, widths):
        whole = 2 if "t" in pieces[0][3] else 1
        stages = len(pieces[0][3]) + 1
        bufs = []
        for _, _, width, order in pieces:
            for s in range(stages):
                free = tuple(2 if d in order[s:] else 1 for d in DIMS)
                bufs.append(pltpu.VMEM(free + (rows, width), jnp.bfloat16))
        accs = [pltpu.VMEM((2, 2, 2, whole, rows, w), jnp.bfloat16) for w in widths]
        sems = [pltpu.SemaphoreType.DMA((len(pieces), stages))] * 2
        return accs, bufs, sems

    @staticmethod
    def view(array, whole):
        blocks = 32 if whole else 16
        return array.reshape(
            2, 2, 2, 2, 2 if whole else 1, array.shape[0] // blocks, array.shape[1]
        )


def home_pieces(wide, thin):
    cut = wide * 3 // 4
    return (
        (0, 0, cut, ORDERS[0]),
        (2, 0, cut, ORDERS[1]),
        (0, cut, wide - cut, ORDERS[2]),
        (2, cut, wide - cut, ORDERS[2]),
        (1, 0, thin, ORDERS[2]),
    )


def home_kernel(count, pieces, *refs):
    n = len(pieces) * 5
    sums = Sum(pieces, refs[:3], refs[6:9], refs[12:15], refs[15 : 15 + n], *refs[15 + n : 17 + n])
    job = Swap(True, count, refs[3:6], refs[9:12], *refs[17 + n :])
    greet_plane(count, [partner("t")])
    sums.start()
    job.start()
    sums.run()
    job.finish()


def bring_home(back, slots, out, grads):
    count = lax.axis_size("dp")
    wide, thin = back.shape[1], slots.shape[1]
    rows = back.shape[0] // 32
    pieces = home_pieces(wide, thin)
    widths = (wide, thin, wide)
    holders, tall, width = grads[0].shape
    accs, bufs, sems = Sum.scratch(pieces, rows, widths)
    results = pl.pallas_call(
        functools.partial(home_kernel, count, pieces),
        out_shape=[jax.ShapeDtypeStruct((rows, w), jnp.float32) for w in widths]
        + [
            jax.ShapeDtypeStruct((holders * count, tall // count, width), g.dtype) for g in grads
        ],
        in_specs=[pl.BlockSpec(memory_space=pltpu.VMEM)] * 3
        + [pl.BlockSpec(memory_space=pl.ANY)] * 3,
        out_specs=[pl.BlockSpec(memory_space=pltpu.VMEM)] * 3
        + [pl.BlockSpec(memory_space=pl.ANY)] * 3,
        scratch_shapes=accs + bufs + sems + Swap.sems(count),
        compiler_params=pltpu.CompilerParams(
            collective_id=2, has_side_effects=True, vmem_limit_bytes=48 << 20
        ),
        name="bring_home",
    )(Sum.view(back, True), Sum.view(slots, True), Sum.view(out, True), *grads)
    return results[:3], results[3:]


def gather_kernel(count, x_ref, o_ref, direct_s, direct_r, side_s, side_r, core_s, core_r, own_sem):
    me, side = lax.axis_index("dp"), lax.axis_index("tensor")
    rows = x_ref.shape[0]
    n = count // 2
    pos, core = lax.div(me, 2), lax.rem(me, 2)

    def at(p, t, c):
        return o_ref.at[pl.ds(((p * 2 + c) * 2 + t) * rows, rows)]

    def peer(k):
        return lax.rem(pos + k, n) * 2 + core

    barrier = pltpu.get_barrier_semaphore()

    def hello(k, carry):
        pl.semaphore_signal(barrier, inc=1, device_id=(peer(k), side), device_id_type=MESH)
        return carry

    lax.fori_loop(1, n, hello, 0)
    for name in ("t", "core"):
        pl.semaphore_signal(barrier, inc=1, device_id=partner(name), device_id_type=MESH)
    pl.semaphore_wait(barrier, n + 1)

    def direct(k, p, src):
        return pltpu.make_async_remote_copy(
            src_ref=src,
            dst_ref=at(p, side, core),
            send_sem=direct_s.at[k],
            recv_sem=direct_r.at[k],
            device_id=(peer(k), side),
            device_id_type=MESH,
        )

    def over(p, t, src):
        return pltpu.make_async_remote_copy(
            src_ref=src,
            dst_ref=at(p, t, core),
            send_sem=side_s.at[p],
            recv_sem=side_r.at[p],
            device_id=partner("t"),
            device_id_type=MESH,
        )

    def across(p, t, c, src):
        return pltpu.make_async_remote_copy(
            src_ref=src,
            dst_ref=at(p, t, c),
            send_sem=core_s.at[p, t],
            recv_sem=core_r.at[p, t],
            device_id=partner("core"),
            device_id_type=MESH,
        )

    over(pos, side, x_ref).start()

    def start(k, carry):
        direct(k, pos, x_ref).start()
        return carry

    lax.fori_loop(1, n, start, 0)
    across(pos, side, core, x_ref).start()
    own = pltpu.make_async_copy(x_ref, at(pos, side, core), own_sem)
    own.start()

    def from_over(q):
        block = at(q, 1 - side, core)
        over(q, 1 - side, block).wait_recv()
        across(q, 1 - side, core, block).start()

    def pass_on(k, carry):
        p = lax.rem(pos - k + n, n)
        block = at(p, side, core)
        direct(k, p, block).wait_recv()
        over(p, side, block).start()
        across(p, side, core, block).start()
        from_over(lax.rem(pos - k + 1 + n, n))
        return carry

    lax.fori_loop(1, n, pass_on, 0)
    from_over(lax.rem(pos + 1, n))

    def finish(p, carry):
        over(p, side, at(p, side, core)).wait_send()
        for t in range(2):
            across(p, t, core, at(p, t, core)).wait_send()
            across(p, t, 1 - core, at(p, t, 1 - core)).wait_recv()
        return carry

    lax.fori_loop(0, n, finish, 0)

    def sent(k, carry):
        direct(k, pos, x_ref).wait_send()
        return carry

    lax.fori_loop(1, n, sent, 0)
    own.wait()


def gather_rows(x, collective_id):
    count = lax.axis_size("dp")
    n = count // 2
    return pl.pallas_call(
        functools.partial(gather_kernel, count),
        out_shape=jax.ShapeDtypeStruct((x.shape[0] * count * 2, x.shape[1]), x.dtype),
        in_specs=[pl.BlockSpec(memory_space=pltpu.VMEM)],
        out_specs=pl.BlockSpec(memory_space=pl.ANY),
        scratch_shapes=[
            pltpu.SemaphoreType.DMA((n,)),
            pltpu.SemaphoreType.DMA((n,)),
            pltpu.SemaphoreType.DMA((n,)),
            pltpu.SemaphoreType.DMA((n,)),
            pltpu.SemaphoreType.DMA((n, 2)),
            pltpu.SemaphoreType.DMA((n, 2)),
            pltpu.SemaphoreType.DMA,
        ],
        compiler_params=pltpu.CompilerParams(collective_id=collective_id, has_side_effects=True),
        name="gather_rows",
    )(x)


def last_pieces(width):
    cut = width // 2
    return ((0, 0, cut, ("x", "z0", "z1")), (0, cut, width - cut, ("z0", "x", "z1")))


def last_kernel(count, width, pieces, *refs):
    n = len(pieces) * 4
    x_ref, g_ref, o_ref, sum_ref = refs[:4]
    sums = Sum(pieces, [g_ref], [sum_ref], refs[4:5], refs[5 : 5 + n], *refs[5 + n : 7 + n])
    send_sem, recv_sem, own_sem = refs[7 + n :]
    total = count * width
    me = lax.axis_index("dp") * width + lax.axis_index("tensor")
    barrier = pltpu.get_barrier_semaphore()

    def place(k):
        peer = lax.rem(me + k, total)
        return (lax.div(peer, width), lax.rem(peer, width))

    def greet(k, carry):
        pl.semaphore_signal(barrier, inc=1, device_id=place(k), device_id_type=MESH)
        return carry

    def copy(k, slot):
        return pltpu.make_async_remote_copy(
            src_ref=x_ref,
            dst_ref=o_ref.at[slot],
            send_sem=send_sem.at[k],
            recv_sem=recv_sem.at[k],
            device_id=place(k),
            device_id_type=MESH,
        )

    def start(k, carry):
        copy(k, me).start()
        return carry

    def finish(k, carry):
        copy(k, me).wait_send()
        copy(k, lax.rem(me - k + total, total)).wait_recv()
        return carry

    lax.fori_loop(1, total, greet, 0)
    pl.semaphore_wait(barrier, total - 1)
    sums.start()
    own = pltpu.make_async_copy(x_ref, o_ref.at[me], own_sem)
    own.start()
    lax.fori_loop(1, total, start, 0)
    sums.run()
    lax.fori_loop(1, total, finish, 0)
    own.wait()


def last_sums(block, grads):
    count, width = lax.axis_size("dp"), lax.axis_size("tensor")
    total = count * width
    rows, columns = grads.shape[0] // count, grads.shape[1]
    pieces = last_pieces(columns)
    accs, bufs, sems = Sum.scratch(pieces, rows, (columns,))
    return pl.pallas_call(
        functools.partial(last_kernel, count, width, pieces),
        out_shape=[
            jax.ShapeDtypeStruct((total,) + block.shape, block.dtype),
            jax.ShapeDtypeStruct((rows, columns), jnp.float32),
        ],
        in_specs=[pl.BlockSpec(memory_space=pltpu.VMEM)] * 2,
        out_specs=[pl.BlockSpec(memory_space=pltpu.VMEM)] * 2,
        scratch_shapes=accs
        + bufs
        + sems
        + [
            pltpu.SemaphoreType.DMA((total,)),
            pltpu.SemaphoreType.DMA((total,)),
            pltpu.SemaphoreType.DMA,
        ],
        compiler_params=pltpu.CompilerParams(
            collective_id=4, has_side_effects=True, vmem_limit_bytes=40 << 20
        ),
        name="last_sums",
    )(block, Sum.view(grads, False))


def local(
    tokens,
    out_grad,
    lengths,
    routes,
    attn_gain,
    w_query,
    w_key,
    w_value,
    w_out,
    ffn_gain,
    w_router,
    w_gate,
    w_up,
    w_down,
):
    local_rows = tokens.shape[0]
    row_count = routes.shape[0]
    model_width = tokens.shape[1]
    dp_count = lax.axis_size("dp")
    replicas = max(1, dp_count // EXPERTS)
    holders = max(1, EXPERTS // dp_count)
    clusters = EXPERTS // holders
    half_ff = w_gate.shape[2]
    heads_here = w_query.shape[1] // HEAD_DIM
    kv_here = w_key.shape[1] // HEAD_DIM
    own_row = lax.axis_index("tensor") * local_rows
    groups = (
        None
        if replicas == 1
        else [[r * clusters + c for c in range(clusters)] for r in range(replicas)]
    )
    q_cols, k_cols = w_query.shape[1], w_key.shape[1]
    cuts = (q_cols, q_cols + k_cols, q_cols + 2 * k_cols)
    packed_attn = gather_weights(jnp.concatenate([w_query, w_key, w_value, w_out], axis=1))
    full_qkv = packed_attn[:, : cuts[2]]
    full_out = packed_attn[:, cuts[2] :]

    def spread_out(weight):
        grouped = weight.reshape(clusters, holders, weight.shape[1], half_ff)
        return jnp.broadcast_to(grouped[None], (replicas,) + grouped.shape).reshape(
            dp_count, holders, weight.shape[1], half_ff
        )

    def fetch(weight):
        moved = lax.all_to_all(spread_out(weight), "dp", split_axis=0, concat_axis=2, tiled=True)
        return moved.reshape(holders, model_width, half_ff)

    near = dp_count == 16 and lax.axis_size("tensor") == 2
    if near:
        local_gate, local_up, local_down = fetch_experts([w_gate, w_up, w_down])
    else:
        local_gate, local_up, local_down = fetch(w_gate), fetch(w_up), fetch(w_down)
    tokens_f32 = tokens.astype(jnp.float32)
    out_f32 = out_grad.astype(jnp.float32)
    position, allowed = seq_layout(lengths[0], row_count)
    cosine, sine_table = rope_tables(position, HEAD_DIM)
    unit_first, scale_first, normed_first = norm_forward(tokens_f32, attn_gain)
    both = spread_rows(
        jnp.concatenate(
            [normed_first, (residual_scale * out_f32).astype(jnp.bfloat16)], axis=1
        )
    )
    wide_first = both[:, :model_width]
    tagged = jnp.concatenate(
        [
            both[:, model_width:],
            jnp.pad(routes.astype(jnp.bfloat16), ((0, 0), (0, 128 - TOPK))),
        ],
        axis=1,
    )
    tagged_all = gather_dp(tagged, groups)
    moe_all = tagged_all[:, :model_width]
    routes_all = tagged_all[:, model_width : model_width + TOPK].astype(jnp.int32)
    qkv = jnp.dot(wide_first, full_qkv, preferred_element_type=jnp.float32)
    query_heads = rotate(
        qkv[:, : cuts[0]].reshape(row_count, heads_here, HEAD_DIM), cosine, sine_table
    ).astype(jnp.bfloat16)
    key_heads = rotate(
        qkv[:, cuts[0] : cuts[1]].reshape(row_count, kv_here, HEAD_DIM), cosine, sine_table
    ).astype(jnp.bfloat16)
    value_heads = qkv[:, cuts[1] :].astype(jnp.bfloat16).reshape(row_count, kv_here, HEAD_DIM)
    mixed_out, log_total = attend(query_heads, key_heads, value_heads, allowed)
    hidden = tokens_f32 + residual_scale * narrow(dot_f32(mixed_out, full_out, ((1,), (1,))))
    unit_second, scale_second, normed_second = norm_forward(hidden, ffn_gain)
    if near:
        rows_all = gather_rows(normed_second, 3)
    else:
        rows_all = gather_dp(spread_rows(normed_second), groups)

    expert_ids = jnp.arange(EXPERTS, dtype=jnp.int32)

    def gate_of(rows_bf, row_routes):
        picked = row_routes[:, :, None] == expert_ids[None, None, :]
        logits = exact_dot(rows_bf, w_router, ((1,), (0,)))
        named = jnp.any(picked, axis=1)
        masked = jnp.where(named, logits, -jnp.inf)
        raised = jnp.exp(masked - jnp.max(masked, axis=1, keepdims=True))
        return picked, named, raised / jnp.sum(raised, axis=1, keepdims=True)

    _, named_all, gates_all = gate_of(rows_all, routes_all)
    first_expert = lax.axis_index("dp") % clusters * holders
    out_part = back_part = gate_slots = 0.0
    grads = []
    for h in range(holders):
        gate = lax.dynamic_slice_in_dim(gates_all, first_expert + h, 1, 1)
        here = lax.dynamic_slice_in_dim(named_all, first_expert + h, 1, 1)
        gate_pre = dot_f32(rows_all, local_gate[h], ((1,), (0,)))
        up_pre = dot_f32(rows_all, local_up[h], ((1,), (0,)))
        sigmoid_gate = jax.nn.sigmoid(gate_pre)
        activated = gate_pre * sigmoid_gate
        inner_act = (activated * up_pre).astype(jnp.bfloat16)
        produced = dot_f32(inner_act, local_down[h], ((1,), (1,))).astype(jnp.bfloat16)
        produced = produced.astype(jnp.float32)
        out_part = out_part + jnp.where(here, gate * produced, 0.0)
        moe_f32 = moe_all.astype(jnp.float32)
        gate_part = jnp.sum(moe_f32 * produced, axis=1, keepdims=True)
        gate_slots = gate_slots + jnp.where(routes_all == first_expert + h, gate_part, 0.0)
        route_grad = jnp.where(here, gate * moe_f32, 0.0).astype(jnp.bfloat16)
        inner_grad = dot_f32(route_grad, local_down[h], ((1,), (0,)))
        gate_pre_grad = (
            inner_grad * up_pre * sigmoid_gate * (1.0 + gate_pre * (1.0 - sigmoid_gate))
        ).astype(jnp.bfloat16)
        up_pre_grad = (inner_grad * activated).astype(jnp.bfloat16)
        back = dot_f32(gate_pre_grad, local_gate[h], ((1,), (1,))) + dot_f32(
            up_pre_grad, local_up[h], ((1,), (1,))
        )
        back_part = back_part + back.astype(jnp.bfloat16).astype(jnp.float32)
        grads.append(
            (
                dot_f32(rows_all, gate_pre_grad, ((0,), (0,))).astype(jnp.bfloat16),
                dot_f32(rows_all, up_pre_grad, ((0,), (0,))).astype(jnp.bfloat16),
                dot_f32(route_grad, inner_act, ((0,), (0,))).astype(jnp.bfloat16),
            )
        )
    slot_parts = split_three(gate_slots)
    pad = jnp.zeros((rows_all.shape[0], 128 - 3 * TOPK), jnp.bfloat16)
    if near:
        stacks = [jnp.stack([grads[h][i] for h in range(holders)]) for i in range(3)]
        slot_parts = jnp.concatenate(slot_parts + [pad], axis=1)
        (own_back, slots, out_home), expert_grads = bring_home(
            back_part.astype(jnp.bfloat16), slot_parts, out_part.astype(jnp.bfloat16), stacks
        )
        expert_back = own_back
        gate_grad = slots[:, :TOPK] + slots[:, TOPK : 2 * TOPK] + slots[:, 2 * TOPK : 3 * TOPK]
        expert_grads = [g.astype(jnp.float32) for g in expert_grads]
    else:
        home = scatter_dp(
            jnp.concatenate(
                [back_part.astype(jnp.bfloat16)]
                + slot_parts
                + [pad, out_part.astype(jnp.bfloat16)],
                axis=1,
            ),
            groups,
        ).astype(jnp.float32)
        back_home = home[:, : model_width + 128]
        slots = back_home[:, model_width:]
        gate_half = slots[:, :TOPK] + slots[:, TOPK : 2 * TOPK] + slots[:, 2 * TOPK : 3 * TOPK]
        own_back = narrow(
            jnp.concatenate(
                [back_home[:, :model_width], jnp.pad(gate_half, ((0, 0), (0, 128 - TOPK)))],
                axis=1,
            )
        )
        expert_back = own_back[:, :model_width]
        gate_grad = own_back[:, model_width : model_width + TOPK]
        out_home = narrow(home[:, model_width + 128 :])
    block_rows = (hidden + residual_scale * out_home).astype(jnp.bfloat16)

    def send_home(index):
        stacked = jnp.stack([grads[h][index] for h in range(holders)])
        moved = lax.all_to_all(stacked[None], "dp", split_axis=2, concat_axis=0, tiled=True)
        return jnp.sum(
            moved.astype(jnp.float32).reshape(
                replicas, clusters * holders, moved.shape[2], half_ff
            ),
            axis=0,
        )

    own_routes = lax.dynamic_slice_in_dim(routes, own_row, local_rows, 0)
    picked_own, _, gates_dense = gate_of(normed_second, own_routes)
    gates_own = jnp.sum(jnp.where(picked_own, gates_dense[:, None, :], 0.0), axis=2)
    chosen_grad = gates_own * (gate_grad - jnp.sum(gates_own * gate_grad, axis=1, keepdims=True))
    logits_grad = jnp.sum(jnp.where(picked_own, chosen_grad[:, :, None], 0.0), axis=1)
    second_grad = expert_back + jnp.dot(logits_grad, w_router.T, precision=lax.Precision.HIGHEST)
    hidden_back, ffn_gain_grad = norm_backward(second_grad, unit_second, scale_second, ffn_gain)
    hidden_grad = out_f32 + hidden_back
    attn_grad = spread_rows((residual_scale * hidden_grad).astype(jnp.bfloat16))
    mixed_grad = jnp.dot(attn_grad, full_out, preferred_element_type=jnp.float32).astype(
        jnp.bfloat16
    )
    out_w_grad = dot_f32(attn_grad, mixed_out, ((0,), (0,)))
    dquery, key_grad, dvalues = attend_back(
        query_heads, key_heads, value_heads, allowed, log_total, mixed_grad
    )
    query_grad = (
        unrotate(dquery, cosine, sine_table)
        .astype(jnp.bfloat16)
        .reshape(row_count, heads_here * HEAD_DIM)
    )
    keys_grad = (
        unrotate(key_grad, cosine, sine_table)
        .astype(jnp.bfloat16)
        .reshape(row_count, kv_here * HEAD_DIM)
    )
    value_grad = dvalues.astype(jnp.bfloat16).reshape(row_count, kv_here * HEAD_DIM)
    qkv_grad = jnp.concatenate([query_grad, keys_grad, value_grad], axis=1)
    qkv_w_grad = dot_f32(wide_first, qkv_grad, ((0,), (0,)))
    packed_grad = jnp.concatenate([qkv_w_grad, out_w_grad], axis=1).astype(jnp.bfloat16)
    first_grad = narrow(dot_f32(qkv_grad, full_qkv, ((1,), (1,))))
    tokens_back, attn_gain_grad = norm_backward(first_grad, unit_first, scale_first, attn_gain)
    tokens_grad = hidden_grad + tokens_back
    if near:
        tall = local_rows * EXPERTS // 128
        wide = model_width // 128
        shared, packed_grad = last_sums(
            jnp.concatenate(
                [
                    logits_grad.reshape(tall, 128),
                    attn_gain_grad.reshape(wide, 128),
                    ffn_gain_grad.reshape(wide, 128),
                ],
                axis=0,
            ),
            packed_grad,
        )
        logits_grad_all = shared[:, :tall].reshape(rows_all.shape[0], EXPERTS)
        router_total = exact_dot(rows_all, logits_grad_all, ((0,), (0,)))
        gains = jnp.sum(shared[:, tall:], axis=0).reshape(2, model_width)
        attn_gain_total, ffn_gain_total = gains[0], gains[1]
    else:
        packed_grad = scatter_weights(packed_grad).astype(jnp.float32)
        expert_grads = [send_home(i) for i in range(3)]
        attn_gain_total, ffn_gain_total, router_total = lax.psum(
            (
                attn_gain_grad,
                ffn_gain_grad,
                exact_dot(normed_second, logits_grad, ((0,), (0,))),
            ),
            ("dp", "tensor"),
        )
    return (
        block_rows,
        tokens_grad,
        attn_gain_total,
        packed_grad[:, : cuts[0]],
        packed_grad[:, cuts[0] : cuts[1]],
        packed_grad[:, cuts[1] : cuts[2]],
        packed_grad[:, cuts[2] :],
        ffn_gain_total,
        router_total,
        *expert_grads,
    )


def solution(mesh):
    placed = (
        P(("dp", "tensor"), None),
        P(("dp", "tensor"), None),
        P("dp", None),
        P("dp", None),
        P(),
        P("dp", "tensor"),
        P("dp", "tensor"),
        P("dp", "tensor"),
        P("dp", "tensor"),
        P(),
        P(),
        P(None, "dp", "tensor"),
        P(None, "dp", "tensor"),
        P(None, "dp", "tensor"),
    )
    return jax.shard_map(
        local,
        mesh=mesh,
        in_specs=placed,
        out_specs=(
            P(("dp", "tensor"), None),
            P(("dp", "tensor"), None),
            P(),
            P("dp", "tensor"),
            P("dp", "tensor"),
            P("dp", "tensor"),
            P("dp", "tensor"),
            P(),
            P(),
            P(None, "dp", "tensor"),
            P(None, "dp", "tensor"),
            P(None, "dp", "tensor"),
        ),
        check_vma=False,
    )
```

```python
import functools

import jax
import jax.numpy as jnp
from jax import lax
from jax.experimental import pallas as pl
from jax.experimental.pallas import tpu as pltpu
from jax.sharding import PartitionSpec as P

EXPERTS = 32
TOPK = 8
HEAD_DIM = 64


eps_norm = 1e-06
residual_scale = 0.22
score_scale = 0.015625
rope_base = 10000.0
masked_score = -1e30


def norm_forward(row_block, gain_vec):
    rscale = lax.rsqrt(jnp.mean(row_block * row_block, axis=1, keepdims=True) + eps_norm)
    unit_rows = row_block * rscale
    return (unit_rows, rscale, (unit_rows * gain_vec).astype(jnp.bfloat16))


def norm_backward(gradient, unit_rows, rscale, gain_vec):
    unit_grad = gradient * gain_vec
    back_rows = rscale * (
        unit_grad - unit_rows * jnp.mean(unit_grad * unit_rows, axis=1, keepdims=True)
    )
    return (back_rows, jnp.sum(gradient * unit_rows, axis=0))


def seq_layout(seq_lengths, row_count):
    order = jnp.arange(seq_lengths.shape[0], dtype=jnp.int32)
    seq_ends = jnp.sum(jnp.where(order[:, None] <= order[None, :], seq_lengths[:, None], 0), axis=0)
    starts = seq_ends - seq_lengths
    places = jnp.arange(row_count, dtype=jnp.int32)
    segment = jnp.sum((places[:, None] >= seq_ends[None, :]).astype(jnp.int32), axis=1)
    member = segment[:, None] == jnp.arange(seq_lengths.shape[0], dtype=jnp.int32)[None, :]
    offset = jnp.sum(jnp.where(member, starts[None, :], 0), axis=1)
    allowed = (segment[:, None] == segment[None, :]) & (places[None, :] <= places[:, None])
    return (places - offset, allowed)


def rope_tables(position, head_width):
    frequency = rope_base ** (-(jnp.arange(head_width // 2, dtype=jnp.float32) * 2.0) / head_width)
    angles = position.astype(jnp.float32)[:, None] * frequency[None, :]
    cosine = jnp.concatenate([jnp.cos(angles), jnp.cos(angles)], axis=1)[:, None, :]
    sine_table = jnp.concatenate([jnp.sin(angles), jnp.sin(angles)], axis=1)[:, None, :]
    return (cosine, sine_table)


def rotate(vectors, cosine, sine_table):
    half_width = vectors.shape[-1] // 2
    first_half = vectors[..., :half_width]
    second_half = vectors[..., half_width:]
    return vectors * cosine + jnp.concatenate([-second_half, first_half], axis=-1) * sine_table


def unrotate(gradient, cosine, sine_table):
    half_width = gradient.shape[-1] // 2
    first_half = gradient[..., :half_width]
    second_half = gradient[..., half_width:]
    return gradient * cosine + jnp.concatenate([second_half, -first_half], axis=-1) * sine_table


def score_block(query_heads, key_heads, allowed):
    row_count, head_count, head_width = query_heads.shape
    kv_count = key_heads.shape[1]
    grouped = query_heads.reshape(row_count, kv_count, head_count // kv_count, head_width)
    scores = (
        jnp.einsum("igrd,jgd->grij", grouped, key_heads, preferred_element_type=jnp.float32)
        * score_scale
    )
    return (grouped, jnp.where(allowed[None, None], scores, masked_score))


def attend(query_heads, key_heads, value_heads, allowed):
    row_count, head_count, head_width = query_heads.shape
    grouped, scores = score_block(query_heads, key_heads, allowed)
    row_max = jnp.max(scores, axis=-1, keepdims=True)
    log_total = row_max + jnp.log(jnp.sum(jnp.exp(scores - row_max), axis=-1, keepdims=True))
    prob_bf = jnp.exp(scores - log_total).astype(jnp.bfloat16)
    mixed_out = jnp.einsum(
        "grij,jgd->igrd", prob_bf, value_heads, preferred_element_type=jnp.float32
    )
    return (mixed_out.reshape(row_count, head_count * head_width).astype(jnp.bfloat16), log_total)


def attend_back(query_heads, key_heads, value_heads, allowed, log_total, mixed_grad):
    row_count, head_count, head_width = query_heads.shape
    kv_count = key_heads.shape[1]
    grouped, scores = score_block(query_heads, key_heads, allowed)
    prob_full = jnp.exp(scores - log_total)
    grad_heads = mixed_grad.reshape(row_count, kv_count, head_count // kv_count, head_width)
    dprobs = jnp.einsum(
        "igrd,jgd->grij", grad_heads, value_heads, preferred_element_type=jnp.float32
    )
    row_delta = jnp.sum(prob_full * dprobs, axis=-1, keepdims=True)
    dscores = (prob_full * (dprobs - row_delta)).astype(jnp.bfloat16)
    dquery = (
        jnp.einsum("grij,jgd->igrd", dscores, key_heads, preferred_element_type=jnp.float32)
        * score_scale
    )
    key_grad = (
        jnp.einsum("grij,igrd->jgd", dscores, grouped, preferred_element_type=jnp.float32)
        * score_scale
    )
    dvalues = jnp.einsum(
        "grij,igrd->jgd",
        prob_full.astype(jnp.bfloat16),
        grad_heads,
        preferred_element_type=jnp.float32,
    )
    return (dquery.reshape(row_count, head_count, head_width), key_grad, dvalues)


def spread_rows(row_block):
    return lax.all_gather(row_block, "tensor", axis=0, tiled=True)


def narrow(partial_rows):
    if lax.axis_size("tensor") != 2:
        return lax.psum_scatter(partial_rows, "tensor", scatter_dimension=0, tiled=True)
    half = partial_rows.shape[0] // 2
    mine = lax.axis_index("tensor")
    away = lax.dynamic_slice_in_dim(partial_rows, (1 - mine) * half, half, 0)
    kept = lax.dynamic_slice_in_dim(partial_rows, mine * half, half, 0)
    return kept + lax.ppermute(away, "tensor", [(0, 1), (1, 0)])


def split_three(values):
    high = lax.reduce_precision(values, 8, 7)
    rest = values - high
    middle = lax.reduce_precision(rest, 8, 7)
    return [part.astype(jnp.bfloat16) for part in (high, middle, rest - middle)]


def dot_f32(left, right, dims):
    return lax.dot_general(left, right, (dims, ((), ())), preferred_element_type=jnp.float32)


def exact_dot(rows_bf, values, dims):
    width = values.shape[1]
    product = dot_f32(rows_bf, jnp.concatenate(split_three(values), axis=1), dims)
    return product[:, :width] + (product[:, width : 2 * width] + product[:, 2 * width :])


def gather_dp(rows, groups):
    return lax.all_gather(rows, "dp", axis=0, tiled=True, axis_index_groups=groups)


def scatter_dp(rows, groups):
    return lax.psum_scatter(
        rows, "dp", scatter_dimension=0, tiled=True, axis_index_groups=groups
    )


def gather_weights(packed):
    return lax.all_gather(packed, "dp", axis=0, tiled=True)


def scatter_weights(packed):
    return lax.psum_scatter(packed, "dp", scatter_dimension=0, tiled=True)


MESH = pl.DeviceIdType.MESH
WEIGHT = {"core": 1, "x": 2, "z0": 4, "z1": 8}
DIMS = ("z1", "z0", "x", "t")
ORDERS = (("x", "t", "z0", "z1"), ("t", "z0", "x", "z1"), ("z0", "x", "z1", "t"))


def bit_of(me, weight):
    return lax.rem(lax.div(me, weight), 2)


def partner(name):
    me, side = lax.axis_index("dp"), lax.axis_index("tensor")
    if name == "t":
        return (me, 1 - side)
    return (me + WEIGHT[name] * (1 - 2 * bit_of(me, WEIGHT[name])), side)


def greet_plane(count, others=()):
    me, side = lax.axis_index("dp"), lax.axis_index("tensor")
    barrier = pltpu.get_barrier_semaphore()

    def greet(k, carry):
        pl.semaphore_signal(
            barrier, inc=1, device_id=(lax.rem(me + k, count), side), device_id_type=MESH
        )
        return carry

    lax.fori_loop(1, count, greet, 0)
    for place in others:
        pl.semaphore_signal(barrier, inc=1, device_id=place, device_id_type=MESH)
    pl.semaphore_wait(barrier, count - 1 + len(others))


def far_first(i, count):
    return count // 2 + (1 - 2 * lax.rem(i, 2)) * lax.div(i + 1, 2)


class Swap:
    def __init__(self, home, count, ins, outs, send_sem, recv_sem, own_sem):
        self.home, self.count = home, count
        self.ins, self.outs = ins, outs
        self.sems = (send_sem, recv_sem, own_sem)
        if home:
            self.holders, self.rows = ins[0].shape[0], ins[0].shape[1] // count
        else:
            self.holders, self.rows = ins[0].shape[0] // count, ins[0].shape[1]

    def pick(self, ref, peer, home):
        if home:
            return ref.at[:, pl.ds(peer * self.rows, self.rows)]
        return ref.at[pl.ds(peer * self.holders, self.holders)]

    def copy(self, w, k, owner):
        me, side = lax.axis_index("dp"), lax.axis_index("tensor")
        peer = lax.rem(me + k, self.count)
        return pltpu.make_async_remote_copy(
            src_ref=self.pick(self.ins[w], peer, self.home),
            dst_ref=self.pick(self.outs[w], owner, not self.home),
            send_sem=self.sems[0].at[w, k],
            recv_sem=self.sems[1].at[w, k],
            device_id=(peer, side),
            device_id_type=MESH,
        )

    def own(self, w):
        me = lax.axis_index("dp")
        return pltpu.make_async_copy(
            self.pick(self.ins[w], me, self.home),
            self.pick(self.outs[w], me, not self.home),
            self.sems[2].at[w],
        )

    def start(self):
        def step(i, carry):
            for w in range(3):
                self.copy(w, far_first(i, self.count), lax.axis_index("dp")).start()
            return carry

        lax.fori_loop(0, self.count - 1, step, 0)
        for w in range(3):
            self.own(w).start()

    def finish(self):
        me = lax.axis_index("dp")

        def step(i, carry):
            k = far_first(i, self.count)
            for w in range(3):
                self.copy(w, k, me).wait_send()
                self.copy(w, k, lax.rem(me - k + self.count, self.count)).wait_recv()
            return carry

        lax.fori_loop(0, self.count - 1, step, 0)
        for w in range(3):
            self.own(w).wait()

    @staticmethod
    def sems(count):
        return [
            pltpu.SemaphoreType.DMA((3, count)),
            pltpu.SemaphoreType.DMA((3, count)),
            pltpu.SemaphoreType.DMA((3,)),
        ]


class Sum:
    def __init__(self, pieces, ins, outs, accs, bufs, send_sem, recv_sem):
        me, side = lax.axis_index("dp"), lax.axis_index("tensor")
        self.pieces, self.ins, self.outs, self.accs, self.bufs = pieces, ins, outs, accs, bufs
        self.send_sem, self.recv_sem = send_sem, recv_sem
        self.core = bit_of(me, 1)
        self.whole = "t" in pieces[0][3]
        self.last = len(pieces[0][3])
        self.mine = {
            "z1": bit_of(me, 8),
            "z0": bit_of(me, 4),
            "x": bit_of(me, 2),
            "t": side if self.whole else 0,
        }

    def exchange(self, i, s):
        which, first, width, order = self.pieces[i]
        columns = pl.ds(first, width)
        if s == 0:
            src = self.ins[which].at[:, :, :, 1 - self.core, :, :, columns]
            place = partner("core")
        else:
            done, now = order[: s - 1], order[s - 1]
            index = []
            for d in DIMS:
                if d in done:
                    index.append(pl.ds(self.mine[d], 1))
                elif d == now:
                    index.append(pl.ds(1 - self.mine[d], 1))
                else:
                    index.append(slice(None))
            src = self.accs[which].at[tuple(index) + (slice(None), columns)]
            place = partner(now)
        return pltpu.make_async_remote_copy(
            src_ref=src,
            dst_ref=self.bufs[i * (self.last + 1) + s],
            send_sem=self.send_sem.at[i, s],
            recv_sem=self.recv_sem.at[i, s],
            device_id=place,
            device_id_type=MESH,
        )

    def add(self, i, s):
        which, first, width, order = self.pieces[i]
        buf = self.bufs[i * (self.last + 1) + s]
        columns = pl.ds(first, width)
        if s == self.last:
            at = tuple(self.mine[d] for d in DIMS) + (slice(None), columns)
            self.outs[which][:, columns] = self.accs[which][at].astype(jnp.float32) + buf[
                0, 0, 0, 0
            ].astype(jnp.float32)
            return
        free = [d for d in DIMS if d in order[s:]]

        def step(b, carry):
            at, frm = dict(self.mine), {d: 0 for d in DIMS}
            left = b
            for d in reversed(free):
                at[d] = frm[d] = lax.rem(left, 2)
                left = lax.div(left, 2)
            at = tuple(at[d] for d in DIMS)
            if s == 0:
                have = self.ins[which][at[:3] + (self.core, at[3], slice(None), columns)]
            else:
                have = self.accs[which][at + (slice(None), columns)]
            got = buf[tuple(frm[d] for d in DIMS)]
            self.accs[which][at + (slice(None), columns)] = (
                have.astype(jnp.float32) + got.astype(jnp.float32)
            ).astype(jnp.bfloat16)
            return carry

        lax.fori_loop(0, 2 ** len(free), step, 0)

    def start(self):
        for i in range(len(self.pieces)):
            self.exchange(i, 0).start()

    def run(self):
        n = len(self.pieces)
        for s in range(self.last + 1):
            for i in range(n):
                self.exchange(i, s).wait_recv()
                self.add(i, s)
                if s < self.last:
                    self.exchange(i, s + 1).start()
        for s in range(self.last + 1):
            for i in range(n):
                self.exchange(i, s).wait_send()

    @staticmethod
    def scratch(pieces, rows, widths):
        whole = 2 if "t" in pieces[0][3] else 1
        stages = len(pieces[0][3]) + 1
        bufs = []
        for _, _, width, order in pieces:
            for s in range(stages):
                free = tuple(2 if d in order[s:] else 1 for d in DIMS)
                bufs.append(pltpu.VMEM(free + (rows, width), jnp.bfloat16))
        accs = [pltpu.VMEM((2, 2, 2, whole, rows, w), jnp.bfloat16) for w in widths]
        sems = [pltpu.SemaphoreType.DMA((len(pieces), stages))] * 2
        return accs, bufs, sems

    @staticmethod
    def view(array, whole):
        blocks = 32 if whole else 16
        return array.reshape(
            2, 2, 2, 2, 2 if whole else 1, array.shape[0] // blocks, array.shape[1]
        )


def home_pieces(wide, thin):
    cut = wide * 3 // 4
    return (
        (0, 0, cut, ORDERS[0]),
        (2, 0, cut, ORDERS[1]),
        (0, cut, wide - cut, ORDERS[2]),
        (2, cut, wide - cut, ORDERS[2]),
        (1, 0, thin, ORDERS[2]),
    )


def home_kernel(count, pieces, *refs):
    n = len(pieces) * 5
    sums = Sum(pieces, refs[:3], refs[6:9], refs[12:15], refs[15 : 15 + n], *refs[15 + n : 17 + n])
    job = Swap(True, count, refs[3:6], refs[9:12], *refs[17 + n :])
    greet_plane(count, [partner("t")])
    sums.start()
    job.start()
    sums.run()
    job.finish()


def bring_home(back, slots, out, grads):
    count = lax.axis_size("dp")
    wide, thin = back.shape[1], slots.shape[1]
    rows = back.shape[0] // 32
    pieces = home_pieces(wide, thin)
    widths = (wide, thin, wide)
    holders, tall, width = grads[0].shape
    accs, bufs, sems = Sum.scratch(pieces, rows, widths)
    results = pl.pallas_call(
        functools.partial(home_kernel, count, pieces),
        out_shape=[jax.ShapeDtypeStruct((rows, w), jnp.float32) for w in widths]
        + [
            jax.ShapeDtypeStruct((holders * count, tall // count, width), g.dtype) for g in grads
        ],
        in_specs=[pl.BlockSpec(memory_space=pltpu.VMEM)] * 3
        + [pl.BlockSpec(memory_space=pl.ANY)] * 3,
        out_specs=[pl.BlockSpec(memory_space=pltpu.VMEM)] * 3
        + [pl.BlockSpec(memory_space=pl.ANY)] * 3,
        scratch_shapes=accs + bufs + sems + Swap.sems(count),
        compiler_params=pltpu.CompilerParams(
            collective_id=2, has_side_effects=True, vmem_limit_bytes=48 << 20
        ),
        name="bring_home",
    )(Sum.view(back, True), Sum.view(slots, True), Sum.view(out, True), *grads)
    return results[:3], results[3:]


class Gather:
    def __init__(self, src, out, sides, sems):
        me, side = lax.axis_index("dp"), lax.axis_index("tensor")
        self.src, self.out, self.sides, self.sems = src, out, sides, sems
        self.rows = src.shape[0]
        self.me, self.t = me, side
        self.z, self.x, self.core = lax.div(me, 4), bit_of(me, 2), bit_of(me, 1)

    def at(self, z, x, t, core):
        place = z * 4 + x * 2 + core
        if self.sides:
            place = place * 2 + t
        return self.out.at[pl.ds(pl.multiple_of(place * self.rows, self.rows), self.rows)]

    def copy(self, pair, index, src, dst, device):
        return pltpu.make_async_remote_copy(
            src_ref=src,
            dst_ref=dst,
            send_sem=self.sems[pair].at[index],
            recv_sem=self.sems[pair + 1].at[index],
            device_id=device,
            device_id_type=MESH,
        )

    def line(self, up, z, src=None):
        block = self.at(z, self.x, self.t, self.core)
        step = 4 if up else -4
        device = (lax.rem(self.me + step + 16, 16), self.t)
        return self.copy(0, (int(up), z), block if src is None else src, block, device)

    def over_x(self, diag, z, x, t, src=None):
        block = self.at(z, x, t, self.core)
        return self.copy(
            2, (int(diag), z), block if src is None else src, block, partner("x")
        )

    def over_t(self, diag, z, x, t, src=None):
        block = self.at(z, x, t, self.core)
        return self.copy(
            4, (int(diag), z), block if src is None else src, block, partner("t")
        )

    def over_core(self, z, x, t, core, src=None):
        block = self.at(z, x, t, core)
        return self.copy(6, (t, x, z), block if src is None else src, block, partner("core"))

    def own(self):
        return pltpu.make_async_copy(
            self.src, self.at(self.z, self.x, self.t, self.core), self.sems[8]
        )

    def sideways(self, z, src=None):
        self.over_x(False, z, self.x, self.t, src).start()
        if self.sides:
            self.over_t(False, z, self.x, self.t, src).start()
        self.over_core(z, self.x, self.t, self.core, src).start()

    def start(self):
        @pl.when(self.z < 3)
        def _():
            self.line(True, self.z, self.src).start()

        @pl.when(self.z > 0)
        def _():
            self.line(False, self.z, self.src).start()

        self.sideways(self.z, self.src)
        self.own().start()

    def pass_line(self, s):
        @pl.when(self.z >= s)
        def _():
            z = self.z - s
            self.line(True, z).wait_recv()

            @pl.when(self.z < 3)
            def _():
                self.line(True, z).start()

            self.sideways(z)

        @pl.when(self.z + s <= 3)
        def _():
            z = self.z + s
            self.line(False, z).wait_recv()

            @pl.when(self.z > 0)
            def _():
                self.line(False, z).start()

            self.sideways(z)

    def second(self, z):
        x, t = self.x, self.t
        self.over_x(False, z, 1 - x, t).wait_recv()
        if self.sides:

            @pl.when(z >= 2)
            def _():
                self.over_t(True, z, 1 - x, t).start()

        self.over_core(z, 1 - x, t, self.core).start()
        if self.sides:
            self.over_t(False, z, x, 1 - t).wait_recv()

            @pl.when(z < 2)
            def _():
                self.over_x(True, z, x, 1 - t).start()

            self.over_core(z, x, 1 - t, self.core).start()

    def pass_second(self, s):
        @pl.when(self.z >= s)
        def _():
            self.second(self.z - s)

        if s:

            @pl.when(self.z + s <= 3)
            def _():
                self.second(self.z + s)

    def third(self, z):
        block = (z, 1 - self.x, 1 - self.t)
        (self.over_x if z < 2 else self.over_t)(True, *block).wait_recv()
        self.over_core(*block, self.core).start()

    def run(self):
        self.pass_line(1)
        self.pass_second(0)
        self.pass_line(2)
        self.pass_second(1)
        self.pass_line(3)
        self.pass_second(2)
        self.pass_second(3)
        if self.sides:
            for z in range(4):
                self.third(z)
        for z in range(4):
            for x in range(2):
                for t in range(2) if self.sides else [self.t]:
                    self.over_core(z, x, t, 1 - self.core).wait_recv()
        self.own().wait()

    def finish(self):
        x, t = self.x, self.t
        for z in range(4):

            @pl.when((z <= self.z) & (self.z < 3))
            def _():
                self.line(True, z).wait_send()

            @pl.when((z >= self.z) & (self.z > 0))
            def _():
                self.line(False, z).wait_send()

            self.over_x(False, z, x, t).wait_send()
            if self.sides:
                self.over_t(False, z, x, t).wait_send()
                if z < 2:
                    self.over_x(True, z, x, 1 - t).wait_send()
                else:
                    self.over_t(True, z, 1 - x, t).wait_send()
            for xb in range(2):
                for tb in range(2) if self.sides else [t]:
                    self.over_core(z, xb, tb, self.core).wait_send()

    @staticmethod
    def semaphores():
        dma = pltpu.SemaphoreType.DMA
        return [dma((2, 4))] * 6 + [dma((2, 2, 4))] * 2 + [dma]


def lanes_of(shape):
    return lax.broadcasted_iota(jnp.int32, shape, 1)


def turn(values, cosine, sine_table, back):
    width = values.shape[1]
    low = lax.rem(lanes_of(values.shape), HEAD_DIM) < HEAD_DIM // 2
    later = pltpu.roll(values, width - HEAD_DIM // 2, 1)
    earlier = pltpu.roll(values, HEAD_DIM // 2, 1)
    moved = jnp.where(low, later, -earlier) if back else jnp.where(low, -later, earlier)
    return values * cosine + moved * sine_table


def twice(pair, second):
    wide = pair.astype(jnp.float32)
    other = pltpu.roll(wide, HEAD_DIM, 1)
    low = lanes_of(wide.shape) < HEAD_DIM
    both = jnp.where(low, other, wide) if second else jnp.where(low, wide, other)
    return both.astype(jnp.bfloat16)


def stack_heads(pair):
    wide = pair.astype(jnp.float32)
    low = lanes_of(wide.shape) < HEAD_DIM
    return jnp.concatenate(
        [jnp.where(low, wide, 0.0), jnp.where(low, 0.0, wide)], axis=0
    ).astype(jnp.bfloat16)


def unstack_heads(stacked):
    rows = stacked.shape[0] // 2
    low = lanes_of((rows, stacked.shape[1])) < HEAD_DIM
    return jnp.where(low, stacked[:rows], stacked[rows:])


def probabilities(query, keys, mask):
    scores = dot_f32(query, keys, ((1,), (1,))) * score_scale
    scores = jnp.where(jnp.concatenate([mask, mask], axis=0) > 0.0, scores, masked_score)
    row_max = jnp.max(scores, axis=1, keepdims=True)
    log_total = row_max + jnp.log(jnp.sum(jnp.exp(scores - row_max), axis=1, keepdims=True))
    return jnp.exp(scores - log_total)


def chunk(ref, i, width):
    return ref[:, i * width : (i + 1) * width]


def front_kernel(count, *refs):
    attn_ref, gate_ref, up_ref, down_ref, first_ref, moe_ref, tokens_ref = refs[:7]
    cos_ref, sin_ref, mask_ref, gain_ref = refs[7:11]
    gate_o, up_o, down_o, rows_o, moe_o, attn_o, wide_o = refs[11:18]
    q_o, k_o, v_o, mixed_o, hidden_o, normed_o = refs[18:24]
    part, got, pair_sem = refs[24:27]
    swap = Swap(False, count, [gate_ref, up_ref, down_ref], [gate_o, up_o, down_o], *refs[27:30])
    attn = Gather(attn_ref, attn_o, False, refs[30:39])
    moe = Gather(moe_ref, moe_o, True, refs[39:48])
    rows_job = Gather(normed_o, rows_o, True, refs[48:57])
    side = lax.axis_index("tensor")
    rows = first_ref.shape[0]

    def half(which):
        return pl.ds(pl.multiple_of(which * rows, rows), rows)

    spread = pltpu.make_async_remote_copy(
        src_ref=first_ref,
        dst_ref=wide_o.at[half(side)],
        send_sem=pair_sem.at[0, 0],
        recv_sem=pair_sem.at[0, 1],
        device_id=partner("t"),
        device_id_type=MESH,
    )
    narrowed = pltpu.make_async_remote_copy(
        src_ref=part.at[half(1 - side)],
        dst_ref=got,
        send_sem=pair_sem.at[1, 0],
        recv_sem=pair_sem.at[1, 1],
        device_id=partner("t"),
        device_id_type=MESH,
    )
    greet_plane(count, [partner("t")])
    attn.start()
    spread.start()
    moe.start()
    swap.start()
    wide_o[half(side), :] = first_ref[...]
    attn.run()
    spread.wait()
    q_cols, k_cols = q_o.shape[1], k_o.shape[1]
    step = 256
    for i in range((q_cols + 2 * k_cols) // step):
        at = i * step
        made = dot_f32(wide_o[...], chunk(attn_o, i, step), ((1,), (0,)))
        if at < q_cols + k_cols:
            made = turn(made, cos_ref[...], sin_ref[...], False)
        made = made.astype(jnp.bfloat16)
        if at < q_cols:
            q_o[:, at : at + step] = made
        elif at < q_cols + k_cols:
            k_o[:, at - q_cols : at - q_cols + step] = made
        else:
            v_o[:, at - q_cols - k_cols : at - q_cols - k_cols + step] = made
    pair_width = 2 * HEAD_DIM
    for g in range(q_cols // pair_width):
        query = stack_heads(chunk(q_o, g, pair_width))
        keys = twice(chunk(k_o, g // 2, pair_width), g % 2)
        values = twice(chunk(v_o, g // 2, pair_width), g % 2)
        probs = probabilities(query, keys, mask_ref[...]).astype(jnp.bfloat16)
        mixed = unstack_heads(dot_f32(probs, values, ((1,), (0,))))
        mixed_o[:, g * pair_width : (g + 1) * pair_width] = mixed.astype(jnp.bfloat16)
    base = q_cols + 2 * k_cols
    for i in range(attn_o.shape[0] // step):
        part[:, i * step : (i + 1) * step] = dot_f32(
            mixed_o[...], attn_o[i * step : (i + 1) * step, base:], ((1,), (1,))
        )
    narrowed.start()
    narrowed.wait()
    hidden = tokens_ref[...].astype(jnp.float32) + residual_scale * (
        part[half(side), :] + got[...]
    )
    hidden_o[...] = hidden
    rscale = lax.rsqrt(jnp.mean(hidden * hidden, axis=1, keepdims=True) + eps_norm)
    normed_o[...] = (hidden * rscale * gain_ref[...]).astype(jnp.bfloat16)
    rows_job.start()
    moe.run()
    rows_job.run()
    attn.finish()
    moe.finish()
    rows_job.finish()
    swap.finish()


def front(packed, experts, first, moe, tokens, cosine, sine_table, mask, gain, q_cols, k_cols):
    count = lax.axis_size("dp")
    rows, width = tokens.shape
    total = rows * count * 2
    wide_rows = 2 * rows
    experts_all, expert_rows, half_ff = experts[0].shape
    bf16, f32 = jnp.bfloat16, jnp.float32
    shape = jax.ShapeDtypeStruct
    vmem, anywhere = pl.BlockSpec(memory_space=pltpu.VMEM), pl.BlockSpec(memory_space=pl.ANY)
    return pl.pallas_call(
        functools.partial(front_kernel, count),
        out_shape=[
            shape((experts_all // count, expert_rows * count, half_ff), bf16) for _ in range(3)
        ]
        + [
            shape((total, width), bf16),
            shape((total, moe.shape[1]), bf16),
            shape((packed.shape[0] * count, packed.shape[1]), bf16),
            shape((wide_rows, width), bf16),
            shape((wide_rows, q_cols), bf16),
            shape((wide_rows, k_cols), bf16),
            shape((wide_rows, k_cols), bf16),
            shape((wide_rows, q_cols), bf16),
            shape((rows, width), f32),
            shape((rows, width), bf16),
        ],
        in_specs=[vmem] + [anywhere] * 3 + [vmem] * 7,
        out_specs=[anywhere] * 5 + [vmem] * 8,
        scratch_shapes=[
            pltpu.VMEM((wide_rows, width), f32),
            pltpu.VMEM((rows, width), f32),
            pltpu.SemaphoreType.DMA((2, 2)),
        ]
        + Swap.sems(count)
        + Gather.semaphores() * 3,
        compiler_params=pltpu.CompilerParams(
            collective_id=1, has_side_effects=True, vmem_limit_bytes=40 << 20
        ),
        name="front",
    )(packed, *experts, first, moe, tokens, cosine, sine_table, mask, gain)


def last_pieces(width):
    cut = width // 2
    return ((0, 0, cut, ("x", "z0", "z1")), (0, cut, width - cut, ("z0", "x", "z1")))


def last_kernel(count, width, pieces, *refs):
    n = len(pieces) * 4
    x_ref, g_ref, o_ref, sum_ref = refs[:4]
    sums = Sum(pieces, [g_ref], [sum_ref], refs[4:5], refs[5 : 5 + n], *refs[5 + n : 7 + n])
    send_sem, recv_sem, own_sem = refs[7 + n :]
    total = count * width
    me = lax.axis_index("dp") * width + lax.axis_index("tensor")
    barrier = pltpu.get_barrier_semaphore()

    def place(k):
        peer = lax.rem(me + k, total)
        return (lax.div(peer, width), lax.rem(peer, width))

    def greet(k, carry):
        pl.semaphore_signal(barrier, inc=1, device_id=place(k), device_id_type=MESH)
        return carry

    def copy(k, slot):
        return pltpu.make_async_remote_copy(
            src_ref=x_ref,
            dst_ref=o_ref.at[slot],
            send_sem=send_sem.at[k],
            recv_sem=recv_sem.at[k],
            device_id=place(k),
            device_id_type=MESH,
        )

    def start(k, carry):
        copy(k, me).start()
        return carry

    def finish(k, carry):
        copy(k, me).wait_send()
        copy(k, lax.rem(me - k + total, total)).wait_recv()
        return carry

    lax.fori_loop(1, total, greet, 0)
    pl.semaphore_wait(barrier, total - 1)
    sums.start()
    own = pltpu.make_async_copy(x_ref, o_ref.at[me], own_sem)
    own.start()
    lax.fori_loop(1, total, start, 0)
    sums.run()
    lax.fori_loop(1, total, finish, 0)
    own.wait()


def last_sums(block, grads):
    count, width = lax.axis_size("dp"), lax.axis_size("tensor")
    total = count * width
    rows, columns = grads.shape[0] // count, grads.shape[1]
    pieces = last_pieces(columns)
    accs, bufs, sems = Sum.scratch(pieces, rows, (columns,))
    return pl.pallas_call(
        functools.partial(last_kernel, count, width, pieces),
        out_shape=[
            jax.ShapeDtypeStruct((total,) + block.shape, block.dtype),
            jax.ShapeDtypeStruct((rows, columns), jnp.float32),
        ],
        in_specs=[pl.BlockSpec(memory_space=pltpu.VMEM)] * 2,
        out_specs=[pl.BlockSpec(memory_space=pltpu.VMEM)] * 2,
        scratch_shapes=accs
        + bufs
        + sems
        + [
            pltpu.SemaphoreType.DMA((total,)),
            pltpu.SemaphoreType.DMA((total,)),
            pltpu.SemaphoreType.DMA,
        ],
        compiler_params=pltpu.CompilerParams(
            collective_id=4, has_side_effects=True, vmem_limit_bytes=40 << 20
        ),
        name="last_sums",
    )(block, Sum.view(grads, False))


def local_near(
    tokens,
    out_grad,
    lengths,
    routes,
    attn_gain,
    w_query,
    w_key,
    w_value,
    w_out,
    ffn_gain,
    w_router,
    w_gate,
    w_up,
    w_down,
):
    local_rows = tokens.shape[0]
    row_count = routes.shape[0]
    model_width = tokens.shape[1]
    holders = EXPERTS // lax.axis_size("dp")
    heads_here = w_query.shape[1] // HEAD_DIM
    kv_here = w_key.shape[1] // HEAD_DIM
    own_row = lax.axis_index("tensor") * local_rows
    q_cols, k_cols = w_query.shape[1], w_key.shape[1]
    cuts = (q_cols, q_cols + k_cols, q_cols + 2 * k_cols)
    tokens_f32 = tokens.astype(jnp.float32)
    out_f32 = out_grad.astype(jnp.float32)
    own_routes = lax.dynamic_slice_in_dim(routes, own_row, local_rows, 0)
    position, allowed = seq_layout(lengths[0], row_count)
    cosine, sine_table = rope_tables(position, HEAD_DIM)
    unit_first, scale_first, normed_first = norm_forward(tokens_f32, attn_gain)
    tagged = jnp.concatenate(
        [
            (residual_scale * out_f32).astype(jnp.bfloat16),
            jnp.pad(own_routes.astype(jnp.bfloat16), ((0, 0), (0, 128 - TOPK))),
        ],
        axis=1,
    )
    (
        local_gate,
        local_up,
        local_down,
        rows_all,
        tagged_all,
        full_attn,
        wide_first,
        query_flat,
        key_flat,
        value_flat,
        mixed_out,
        hidden,
        normed_second,
    ) = front(
        jnp.concatenate([w_query, w_key, w_value, w_out], axis=1),
        [w_gate, w_up, w_down],
        normed_first,
        tagged,
        tokens,
        jnp.tile(cosine[:, 0], (1, 4)),
        jnp.tile(sine_table[:, 0], (1, 4)),
        allowed.astype(jnp.float32),
        ffn_gain[None, :],
        q_cols,
        k_cols,
    )
    full_qkv = full_attn[:, : cuts[2]]
    full_out = full_attn[:, cuts[2] :]
    moe_all = tagged_all[:, :model_width]
    routes_all = tagged_all[:, model_width : model_width + TOPK].astype(jnp.int32)
    unit_second, scale_second, _ = norm_forward(hidden, ffn_gain)
    expert_ids = jnp.arange(EXPERTS, dtype=jnp.int32)

    def gate_of(rows_bf, row_routes):
        named = jnp.any(row_routes[:, :, None] == expert_ids[None, None, :], axis=1)
        logits = exact_dot(rows_bf, w_router, ((1,), (0,)))
        masked = jnp.where(named, logits, -jnp.inf)
        raised = jnp.exp(masked - jnp.max(masked, axis=1, keepdims=True))
        return named, raised / jnp.sum(raised, axis=1, keepdims=True)

    named_all, gates_all = gate_of(rows_all, routes_all)
    first_expert = lax.axis_index("dp") * holders
    out_part = back_part = gate_slots = 0.0
    grads = []
    for h in range(holders):
        gate = lax.dynamic_slice_in_dim(gates_all, first_expert + h, 1, 1)
        here = lax.dynamic_slice_in_dim(named_all, first_expert + h, 1, 1)
        gate_pre = dot_f32(rows_all, local_gate[h], ((1,), (0,)))
        up_pre = dot_f32(rows_all, local_up[h], ((1,), (0,)))
        sigmoid_gate = jax.nn.sigmoid(gate_pre)
        activated = gate_pre * sigmoid_gate
        inner_act = (activated * up_pre).astype(jnp.bfloat16)
        produced = dot_f32(inner_act, local_down[h], ((1,), (1,))).astype(jnp.bfloat16)
        produced = produced.astype(jnp.float32)
        out_part = out_part + jnp.where(here, gate * produced, 0.0)
        moe_f32 = moe_all.astype(jnp.float32)
        gate_part = jnp.sum(moe_f32 * produced, axis=1, keepdims=True)
        gate_slots = gate_slots + jnp.where(
            here & (expert_ids[None, :] == first_expert + h), gate_part, 0.0
        )
        route_grad = jnp.where(here, gate * moe_f32, 0.0).astype(jnp.bfloat16)
        inner_grad = dot_f32(route_grad, local_down[h], ((1,), (0,)))
        gate_pre_grad = (
            inner_grad * up_pre * sigmoid_gate * (1.0 + gate_pre * (1.0 - sigmoid_gate))
        ).astype(jnp.bfloat16)
        up_pre_grad = (inner_grad * activated).astype(jnp.bfloat16)
        back = dot_f32(gate_pre_grad, local_gate[h], ((1,), (1,))) + dot_f32(
            up_pre_grad, local_up[h], ((1,), (1,))
        )
        back_part = back_part + back.astype(jnp.bfloat16).astype(jnp.float32)
        grads.append(
            (
                dot_f32(rows_all, gate_pre_grad, ((0,), (0,))).astype(jnp.bfloat16),
                dot_f32(rows_all, up_pre_grad, ((0,), (0,))).astype(jnp.bfloat16),
                dot_f32(route_grad, inner_act, ((0,), (0,))).astype(jnp.bfloat16),
            )
        )
    slot_parts = jnp.concatenate(
        split_three(gate_slots)
        + [jnp.zeros((rows_all.shape[0], 128 - 3 * EXPERTS), jnp.bfloat16)],
        axis=1,
    )
    stacks = [jnp.stack([grads[h][i] for h in range(holders)]) for i in range(3)]
    (expert_back, slots, out_home), expert_grads = bring_home(
        back_part.astype(jnp.bfloat16), slot_parts, out_part.astype(jnp.bfloat16), stacks
    )
    gate_grad = (
        slots[:, :EXPERTS]
        + slots[:, EXPERTS : 2 * EXPERTS]
        + slots[:, 2 * EXPERTS : 3 * EXPERTS]
    )
    block_rows = (hidden + residual_scale * out_home).astype(jnp.bfloat16)
    _, gates_own = gate_of(normed_second, own_routes)
    logits_grad = gates_own * (gate_grad - jnp.sum(gates_own * gate_grad, axis=1, keepdims=True))
    second_grad = expert_back + jnp.dot(logits_grad, w_router.T, precision=lax.Precision.HIGHEST)
    hidden_back, ffn_gain_grad = norm_backward(second_grad, unit_second, scale_second, ffn_gain)
    hidden_grad = out_f32 + hidden_back
    attn_grad = spread_rows((residual_scale * hidden_grad).astype(jnp.bfloat16))
    mixed_grad = jnp.dot(attn_grad, full_out, preferred_element_type=jnp.float32).astype(
        jnp.bfloat16
    )
    out_w_grad = dot_f32(attn_grad, mixed_out, ((0,), (0,)))
    query_heads = query_flat.reshape(row_count, heads_here, HEAD_DIM)
    key_heads = key_flat.reshape(row_count, kv_here, HEAD_DIM)
    value_heads = value_flat.reshape(row_count, kv_here, HEAD_DIM)
    _, scores = score_block(query_heads, key_heads, allowed)
    row_max = jnp.max(scores, axis=-1, keepdims=True)
    log_total = row_max + jnp.log(jnp.sum(jnp.exp(scores - row_max), axis=-1, keepdims=True))
    dquery, key_grad, dvalues = attend_back(
        query_heads, key_heads, value_heads, allowed, log_total, mixed_grad
    )
    query_grad = (
        unrotate(dquery, cosine, sine_table)
        .astype(jnp.bfloat16)
        .reshape(row_count, heads_here * HEAD_DIM)
    )
    keys_grad = (
        unrotate(key_grad, cosine, sine_table)
        .astype(jnp.bfloat16)
        .reshape(row_count, kv_here * HEAD_DIM)
    )
    value_grad = dvalues.astype(jnp.bfloat16).reshape(row_count, kv_here * HEAD_DIM)
    qkv_grad = jnp.concatenate([query_grad, keys_grad, value_grad], axis=1)
    qkv_w_grad = dot_f32(wide_first, qkv_grad, ((0,), (0,)))
    packed_grad = jnp.concatenate([qkv_w_grad, out_w_grad], axis=1).astype(jnp.bfloat16)
    first_grad = narrow(dot_f32(qkv_grad, full_qkv, ((1,), (1,))))
    tokens_back, attn_gain_grad = norm_backward(first_grad, unit_first, scale_first, attn_gain)
    tokens_grad = hidden_grad + tokens_back
    tall = local_rows * EXPERTS // 128
    wide = model_width // 128
    shared, packed_grad = last_sums(
        jnp.concatenate(
            [
                logits_grad.reshape(tall, 128),
                attn_gain_grad.reshape(wide, 128),
                ffn_gain_grad.reshape(wide, 128),
            ],
            axis=0,
        ),
        packed_grad,
    )
    logits_grad_all = shared[:, :tall].reshape(rows_all.shape[0], EXPERTS)
    router_total = exact_dot(rows_all, logits_grad_all, ((0,), (0,)))
    gains = jnp.sum(shared[:, tall:], axis=0).reshape(2, model_width)
    return (
        block_rows,
        tokens_grad,
        gains[0],
        packed_grad[:, : cuts[0]],
        packed_grad[:, cuts[0] : cuts[1]],
        packed_grad[:, cuts[1] : cuts[2]],
        packed_grad[:, cuts[2] :],
        gains[1],
        router_total,
        *[g.astype(jnp.float32) for g in expert_grads],
    )


def local_far(
    tokens,
    out_grad,
    lengths,
    routes,
    attn_gain,
    w_query,
    w_key,
    w_value,
    w_out,
    ffn_gain,
    w_router,
    w_gate,
    w_up,
    w_down,
):
    local_rows = tokens.shape[0]
    row_count = routes.shape[0]
    model_width = tokens.shape[1]
    dp_count = lax.axis_size("dp")
    replicas = max(1, dp_count // EXPERTS)
    holders = max(1, EXPERTS // dp_count)
    clusters = EXPERTS // holders
    half_ff = w_gate.shape[2]
    heads_here = w_query.shape[1] // HEAD_DIM
    kv_here = w_key.shape[1] // HEAD_DIM
    own_row = lax.axis_index("tensor") * local_rows
    groups = (
        None
        if replicas == 1
        else [[r * clusters + c for c in range(clusters)] for r in range(replicas)]
    )
    q_cols, k_cols = w_query.shape[1], w_key.shape[1]
    cuts = (q_cols, q_cols + k_cols, q_cols + 2 * k_cols)
    packed_attn = gather_weights(jnp.concatenate([w_query, w_key, w_value, w_out], axis=1))
    full_qkv = packed_attn[:, : cuts[2]]
    full_out = packed_attn[:, cuts[2] :]

    def spread_out(weight):
        grouped = weight.reshape(clusters, holders, weight.shape[1], half_ff)
        return jnp.broadcast_to(grouped[None], (replicas,) + grouped.shape).reshape(
            dp_count, holders, weight.shape[1], half_ff
        )

    def fetch(weight):
        moved = lax.all_to_all(spread_out(weight), "dp", split_axis=0, concat_axis=2, tiled=True)
        return moved.reshape(holders, model_width, half_ff)

    local_gate, local_up, local_down = fetch(w_gate), fetch(w_up), fetch(w_down)
    tokens_f32 = tokens.astype(jnp.float32)
    out_f32 = out_grad.astype(jnp.float32)
    position, allowed = seq_layout(lengths[0], row_count)
    cosine, sine_table = rope_tables(position, HEAD_DIM)
    unit_first, scale_first, normed_first = norm_forward(tokens_f32, attn_gain)
    both = spread_rows(
        jnp.concatenate(
            [normed_first, (residual_scale * out_f32).astype(jnp.bfloat16)], axis=1
        )
    )
    wide_first = both[:, :model_width]
    tagged = jnp.concatenate(
        [
            both[:, model_width:],
            jnp.pad(routes.astype(jnp.bfloat16), ((0, 0), (0, 128 - TOPK))),
        ],
        axis=1,
    )
    tagged_all = gather_dp(tagged, groups)
    moe_all = tagged_all[:, :model_width]
    routes_all = tagged_all[:, model_width : model_width + TOPK].astype(jnp.int32)
    qkv = jnp.dot(wide_first, full_qkv, preferred_element_type=jnp.float32)
    query_heads = rotate(
        qkv[:, : cuts[0]].reshape(row_count, heads_here, HEAD_DIM), cosine, sine_table
    ).astype(jnp.bfloat16)
    key_heads = rotate(
        qkv[:, cuts[0] : cuts[1]].reshape(row_count, kv_here, HEAD_DIM), cosine, sine_table
    ).astype(jnp.bfloat16)
    value_heads = qkv[:, cuts[1] :].astype(jnp.bfloat16).reshape(row_count, kv_here, HEAD_DIM)
    mixed_out, log_total = attend(query_heads, key_heads, value_heads, allowed)
    hidden = tokens_f32 + residual_scale * narrow(dot_f32(mixed_out, full_out, ((1,), (1,))))
    unit_second, scale_second, normed_second = norm_forward(hidden, ffn_gain)
    rows_all = gather_dp(spread_rows(normed_second), groups)

    expert_ids = jnp.arange(EXPERTS, dtype=jnp.int32)

    def gate_of(rows_bf, row_routes):
        picked = row_routes[:, :, None] == expert_ids[None, None, :]
        logits = exact_dot(rows_bf, w_router, ((1,), (0,)))
        named = jnp.any(picked, axis=1)
        masked = jnp.where(named, logits, -jnp.inf)
        raised = jnp.exp(masked - jnp.max(masked, axis=1, keepdims=True))
        return picked, named, raised / jnp.sum(raised, axis=1, keepdims=True)

    _, named_all, gates_all = gate_of(rows_all, routes_all)
    first_expert = lax.axis_index("dp") % clusters * holders
    out_part = back_part = gate_slots = 0.0
    grads = []
    for h in range(holders):
        gate = lax.dynamic_slice_in_dim(gates_all, first_expert + h, 1, 1)
        here = lax.dynamic_slice_in_dim(named_all, first_expert + h, 1, 1)
        gate_pre = dot_f32(rows_all, local_gate[h], ((1,), (0,)))
        up_pre = dot_f32(rows_all, local_up[h], ((1,), (0,)))
        sigmoid_gate = jax.nn.sigmoid(gate_pre)
        activated = gate_pre * sigmoid_gate
        inner_act = (activated * up_pre).astype(jnp.bfloat16)
        produced = dot_f32(inner_act, local_down[h], ((1,), (1,))).astype(jnp.bfloat16)
        produced = produced.astype(jnp.float32)
        out_part = out_part + jnp.where(here, gate * produced, 0.0)
        moe_f32 = moe_all.astype(jnp.float32)
        gate_part = jnp.sum(moe_f32 * produced, axis=1, keepdims=True)
        gate_slots = gate_slots + jnp.where(routes_all == first_expert + h, gate_part, 0.0)
        route_grad = jnp.where(here, gate * moe_f32, 0.0).astype(jnp.bfloat16)
        inner_grad = dot_f32(route_grad, local_down[h], ((1,), (0,)))
        gate_pre_grad = (
            inner_grad * up_pre * sigmoid_gate * (1.0 + gate_pre * (1.0 - sigmoid_gate))
        ).astype(jnp.bfloat16)
        up_pre_grad = (inner_grad * activated).astype(jnp.bfloat16)
        back = dot_f32(gate_pre_grad, local_gate[h], ((1,), (1,))) + dot_f32(
            up_pre_grad, local_up[h], ((1,), (1,))
        )
        back_part = back_part + back.astype(jnp.bfloat16).astype(jnp.float32)
        grads.append(
            (
                dot_f32(rows_all, gate_pre_grad, ((0,), (0,))).astype(jnp.bfloat16),
                dot_f32(rows_all, up_pre_grad, ((0,), (0,))).astype(jnp.bfloat16),
                dot_f32(route_grad, inner_act, ((0,), (0,))).astype(jnp.bfloat16),
            )
        )
    slot_parts = split_three(gate_slots)
    pad = jnp.zeros((rows_all.shape[0], 128 - 3 * TOPK), jnp.bfloat16)
    home = scatter_dp(
        jnp.concatenate(
            [back_part.astype(jnp.bfloat16)] + slot_parts + [pad, out_part.astype(jnp.bfloat16)],
            axis=1,
        ),
        groups,
    ).astype(jnp.float32)
    back_home = home[:, : model_width + 128]
    out_home = home[:, model_width + 128 :]
    slots = back_home[:, model_width:]
    gate_half = slots[:, :TOPK] + slots[:, TOPK : 2 * TOPK] + slots[:, 2 * TOPK : 3 * TOPK]
    own_back = narrow(
        jnp.concatenate(
            [back_home[:, :model_width], jnp.pad(gate_half, ((0, 0), (0, 128 - TOPK)))], axis=1
        )
    )
    expert_back = own_back[:, :model_width]
    gate_grad = own_back[:, model_width : model_width + TOPK]
    block_rows = (hidden + residual_scale * narrow(out_home)).astype(jnp.bfloat16)

    def send_home(index):
        stacked = jnp.stack([grads[h][index] for h in range(holders)])
        moved = lax.all_to_all(stacked[None], "dp", split_axis=2, concat_axis=0, tiled=True)
        return jnp.sum(
            moved.astype(jnp.float32).reshape(
                replicas, clusters * holders, moved.shape[2], half_ff
            ),
            axis=0,
        )

    own_routes = lax.dynamic_slice_in_dim(routes, own_row, local_rows, 0)
    picked_own, _, gates_dense = gate_of(normed_second, own_routes)
    gates_own = jnp.sum(jnp.where(picked_own, gates_dense[:, None, :], 0.0), axis=2)
    chosen_grad = gates_own * (gate_grad - jnp.sum(gates_own * gate_grad, axis=1, keepdims=True))
    logits_grad = jnp.sum(jnp.where(picked_own, chosen_grad[:, :, None], 0.0), axis=1)
    second_grad = expert_back + jnp.dot(logits_grad, w_router.T, precision=lax.Precision.HIGHEST)
    hidden_back, ffn_gain_grad = norm_backward(second_grad, unit_second, scale_second, ffn_gain)
    hidden_grad = out_f32 + hidden_back
    attn_grad = spread_rows((residual_scale * hidden_grad).astype(jnp.bfloat16))
    mixed_grad = jnp.dot(attn_grad, full_out, preferred_element_type=jnp.float32).astype(
        jnp.bfloat16
    )
    out_w_grad = dot_f32(attn_grad, mixed_out, ((0,), (0,)))
    dquery, key_grad, dvalues = attend_back(
        query_heads, key_heads, value_heads, allowed, log_total, mixed_grad
    )
    query_grad = (
        unrotate(dquery, cosine, sine_table)
        .astype(jnp.bfloat16)
        .reshape(row_count, heads_here * HEAD_DIM)
    )
    keys_grad = (
        unrotate(key_grad, cosine, sine_table)
        .astype(jnp.bfloat16)
        .reshape(row_count, kv_here * HEAD_DIM)
    )
    value_grad = dvalues.astype(jnp.bfloat16).reshape(row_count, kv_here * HEAD_DIM)
    qkv_grad = jnp.concatenate([query_grad, keys_grad, value_grad], axis=1)
    qkv_w_grad = dot_f32(wide_first, qkv_grad, ((0,), (0,)))
    packed_grad = scatter_weights(
        jnp.concatenate([qkv_w_grad, out_w_grad], axis=1).astype(jnp.bfloat16)
    ).astype(jnp.float32)
    first_grad = narrow(dot_f32(qkv_grad, full_qkv, ((1,), (1,))))
    tokens_back, attn_gain_grad = norm_backward(first_grad, unit_first, scale_first, attn_gain)
    tokens_grad = hidden_grad + tokens_back
    attn_gain_total, ffn_gain_total, router_total = lax.psum(
        (
            attn_gain_grad,
            ffn_gain_grad,
            exact_dot(normed_second, logits_grad, ((0,), (0,))),
        ),
        ("dp", "tensor"),
    )
    return (
        block_rows,
        tokens_grad,
        attn_gain_total,
        packed_grad[:, : cuts[0]],
        packed_grad[:, cuts[0] : cuts[1]],
        packed_grad[:, cuts[1] : cuts[2]],
        packed_grad[:, cuts[2] :],
        ffn_gain_total,
        router_total,
        send_home(0),
        send_home(1),
        send_home(2),
    )


def solution(mesh):
    placed = (
        P(("dp", "tensor"), None),
        P(("dp", "tensor"), None),
        P("dp", None),
        P("dp", None),
        P(),
        P("dp", "tensor"),
        P("dp", "tensor"),
        P("dp", "tensor"),
        P("dp", "tensor"),
        P(),
        P(),
        P(None, "dp", "tensor"),
        P(None, "dp", "tensor"),
        P(None, "dp", "tensor"),
    )
    near = mesh.shape["dp"] == 16 and mesh.shape["tensor"] == 2
    return jax.shard_map(
        local_near if near else local_far,
        mesh=mesh,
        in_specs=placed,
        out_specs=(
            P(("dp", "tensor"), None),
            P(("dp", "tensor"), None),
            P(),
            P("dp", "tensor"),
            P("dp", "tensor"),
            P("dp", "tensor"),
            P("dp", "tensor"),
            P(),
            P(),
            P(None, "dp", "tensor"),
            P(None, "dp", "tensor"),
            P(None, "dp", "tensor"),
        ),
        check_vma=False,
    )
```

```python
import functools

import jax
import jax.numpy as jnp
from jax import lax
from jax.experimental import pallas as pl
from jax.experimental.pallas import tpu as pltpu
from jax.sharding import PartitionSpec as P

EXPERTS = 32
TOPK = 8
HEAD_DIM = 64


eps_norm = 1e-06
residual_scale = 0.22
score_scale = 0.015625
rope_base = 10000.0
masked_score = -1e30


def norm_forward(row_block, gain_vec):
    rscale = lax.rsqrt(jnp.mean(row_block * row_block, axis=1, keepdims=True) + eps_norm)
    unit_rows = row_block * rscale
    return (unit_rows, rscale, (unit_rows * gain_vec).astype(jnp.bfloat16))


def norm_backward(gradient, unit_rows, rscale, gain_vec):
    unit_grad = gradient * gain_vec
    back_rows = rscale * (
        unit_grad - unit_rows * jnp.mean(unit_grad * unit_rows, axis=1, keepdims=True)
    )
    return (back_rows, jnp.sum(gradient * unit_rows, axis=0))


def seq_layout(seq_lengths, row_count):
    order = jnp.arange(seq_lengths.shape[0], dtype=jnp.int32)
    seq_ends = jnp.sum(jnp.where(order[:, None] <= order[None, :], seq_lengths[:, None], 0), axis=0)
    starts = seq_ends - seq_lengths
    places = jnp.arange(row_count, dtype=jnp.int32)
    segment = jnp.sum((places[:, None] >= seq_ends[None, :]).astype(jnp.int32), axis=1)
    member = segment[:, None] == jnp.arange(seq_lengths.shape[0], dtype=jnp.int32)[None, :]
    offset = jnp.sum(jnp.where(member, starts[None, :], 0), axis=1)
    allowed = (segment[:, None] == segment[None, :]) & (places[None, :] <= places[:, None])
    return (places - offset, allowed)


def rope_tables(position, head_width):
    frequency = rope_base ** (-(jnp.arange(head_width // 2, dtype=jnp.float32) * 2.0) / head_width)
    angles = position.astype(jnp.float32)[:, None] * frequency[None, :]
    cosine = jnp.concatenate([jnp.cos(angles), jnp.cos(angles)], axis=1)[:, None, :]
    sine_table = jnp.concatenate([jnp.sin(angles), jnp.sin(angles)], axis=1)[:, None, :]
    return (cosine, sine_table)


def rotate(vectors, cosine, sine_table):
    half_width = vectors.shape[-1] // 2
    first_half = vectors[..., :half_width]
    second_half = vectors[..., half_width:]
    return vectors * cosine + jnp.concatenate([-second_half, first_half], axis=-1) * sine_table


def unrotate(gradient, cosine, sine_table):
    half_width = gradient.shape[-1] // 2
    first_half = gradient[..., :half_width]
    second_half = gradient[..., half_width:]
    return gradient * cosine + jnp.concatenate([second_half, -first_half], axis=-1) * sine_table


def score_block(query_heads, key_heads, allowed):
    row_count, head_count, head_width = query_heads.shape
    kv_count = key_heads.shape[1]
    grouped = query_heads.reshape(row_count, kv_count, head_count // kv_count, head_width)
    scores = (
        jnp.einsum("igrd,jgd->grij", grouped, key_heads, preferred_element_type=jnp.float32)
        * score_scale
    )
    return (grouped, jnp.where(allowed[None, None], scores, masked_score))


def attend(query_heads, key_heads, value_heads, allowed):
    row_count, head_count, head_width = query_heads.shape
    grouped, scores = score_block(query_heads, key_heads, allowed)
    row_max = jnp.max(scores, axis=-1, keepdims=True)
    log_total = row_max + jnp.log(jnp.sum(jnp.exp(scores - row_max), axis=-1, keepdims=True))
    prob_bf = jnp.exp(scores - log_total).astype(jnp.bfloat16)
    mixed_out = jnp.einsum(
        "grij,jgd->igrd", prob_bf, value_heads, preferred_element_type=jnp.float32
    )
    return (mixed_out.reshape(row_count, head_count * head_width).astype(jnp.bfloat16), log_total)


def attend_back(query_heads, key_heads, value_heads, allowed, log_total, mixed_grad):
    row_count, head_count, head_width = query_heads.shape
    kv_count = key_heads.shape[1]
    grouped, scores = score_block(query_heads, key_heads, allowed)
    prob_full = jnp.exp(scores - log_total)
    grad_heads = mixed_grad.reshape(row_count, kv_count, head_count // kv_count, head_width)
    dprobs = jnp.einsum(
        "igrd,jgd->grij", grad_heads, value_heads, preferred_element_type=jnp.float32
    )
    row_delta = jnp.sum(prob_full * dprobs, axis=-1, keepdims=True)
    dscores = (prob_full * (dprobs - row_delta)).astype(jnp.bfloat16)
    dquery = (
        jnp.einsum("grij,jgd->igrd", dscores, key_heads, preferred_element_type=jnp.float32)
        * score_scale
    )
    key_grad = (
        jnp.einsum("grij,igrd->jgd", dscores, grouped, preferred_element_type=jnp.float32)
        * score_scale
    )
    dvalues = jnp.einsum(
        "grij,igrd->jgd",
        prob_full.astype(jnp.bfloat16),
        grad_heads,
        preferred_element_type=jnp.float32,
    )
    return (dquery.reshape(row_count, head_count, head_width), key_grad, dvalues)


def spread_rows(row_block):
    return lax.all_gather(row_block, "tensor", axis=0, tiled=True)


def narrow(partial_rows):
    if lax.axis_size("tensor") != 2:
        return lax.psum_scatter(partial_rows, "tensor", scatter_dimension=0, tiled=True)
    half = partial_rows.shape[0] // 2
    mine = lax.axis_index("tensor")
    away = lax.dynamic_slice_in_dim(partial_rows, (1 - mine) * half, half, 0)
    kept = lax.dynamic_slice_in_dim(partial_rows, mine * half, half, 0)
    return kept + lax.ppermute(away, "tensor", [(0, 1), (1, 0)])


def split_three(values):
    high = lax.reduce_precision(values, 8, 7)
    rest = values - high
    middle = lax.reduce_precision(rest, 8, 7)
    return [part.astype(jnp.bfloat16) for part in (high, middle, rest - middle)]


def dot_f32(left, right, dims):
    return lax.dot_general(left, right, (dims, ((), ())), preferred_element_type=jnp.float32)


def exact_dot(rows_bf, values, dims):
    width = values.shape[1]
    product = dot_f32(rows_bf, jnp.concatenate(split_three(values), axis=1), dims)
    return product[:, :width] + (product[:, width : 2 * width] + product[:, 2 * width :])


def gather_dp(rows, groups):
    return lax.all_gather(rows, "dp", axis=0, tiled=True, axis_index_groups=groups)


def scatter_dp(rows, groups):
    return lax.psum_scatter(
        rows, "dp", scatter_dimension=0, tiled=True, axis_index_groups=groups
    )


def gather_weights(packed):
    return lax.all_gather(packed, "dp", axis=0, tiled=True)


def scatter_weights(packed):
    return lax.psum_scatter(packed, "dp", scatter_dimension=0, tiled=True)


MESH = pl.DeviceIdType.MESH
WEIGHT = {"core": 1, "x": 2, "z0": 4, "z1": 8}
DIMS = ("z1", "z0", "x", "t")
ORDERS = (("x", "t", "z0", "z1"), ("t", "z0", "x", "z1"), ("z0", "x", "z1", "t"))


def bit_of(me, weight):
    return lax.rem(lax.div(me, weight), 2)


def partner(name):
    me, side = lax.axis_index("dp"), lax.axis_index("tensor")
    if name == "t":
        return (me, 1 - side)
    return (me + WEIGHT[name] * (1 - 2 * bit_of(me, WEIGHT[name])), side)


def greet_plane(count, others=()):
    me, side = lax.axis_index("dp"), lax.axis_index("tensor")
    barrier = pltpu.get_barrier_semaphore()

    def greet(k, carry):
        pl.semaphore_signal(
            barrier, inc=1, device_id=(lax.rem(me + k, count), side), device_id_type=MESH
        )
        return carry

    lax.fori_loop(1, count, greet, 0)
    for place in others:
        pl.semaphore_signal(barrier, inc=1, device_id=place, device_id_type=MESH)
    pl.semaphore_wait(barrier, count - 1 + len(others))


def far_first(i, count):
    return count // 2 + (1 - 2 * lax.rem(i, 2)) * lax.div(i + 1, 2)


class Swap:
    def __init__(self, home, count, ins, outs, send_sem, recv_sem, own_sem):
        self.home, self.count = home, count
        self.issued = 0
        self.ins, self.outs = ins, outs
        self.sems = (send_sem, recv_sem, own_sem)
        if home:
            self.holders, self.rows = ins[0].shape[0], ins[0].shape[1] // count
        else:
            self.holders, self.rows = ins[0].shape[0] // count, ins[0].shape[1]

    def pick(self, ref, peer, home):
        if home:
            return ref.at[:, pl.ds(peer * self.rows, self.rows)]
        return ref.at[pl.ds(peer * self.holders, self.holders)]

    def copy(self, w, k, owner):
        me, side = lax.axis_index("dp"), lax.axis_index("tensor")
        peer = lax.rem(me + k, self.count)
        return pltpu.make_async_remote_copy(
            src_ref=self.pick(self.ins[w], peer, self.home),
            dst_ref=self.pick(self.outs[w], owner, not self.home),
            send_sem=self.sems[0].at[w, k],
            recv_sem=self.sems[1].at[w, k],
            device_id=(peer, side),
            device_id_type=MESH,
        )

    def own(self, w):
        me = lax.axis_index("dp")
        return pltpu.make_async_copy(
            self.pick(self.ins[w], me, self.home),
            self.pick(self.outs[w], me, not self.home),
            self.sems[2].at[w],
        )

    def start(self):
        def step(i, carry):
            for w in range(3):
                self.copy(w, far_first(i, self.count), lax.axis_index("dp")).start()
            return carry

        lax.fori_loop(0, self.count - 1, step, 0)
        for w in range(3):
            self.own(w).start()

    def some(self, amount):
        for _ in range(amount):
            if self.issued < 3 * (self.count - 1):
                i, w = divmod(self.issued, 3)
                k = self.count // 2 + (1 - 2 * (i % 2)) * ((i + 1) // 2)
                self.copy(w, k, lax.axis_index("dp")).start()
                self.issued += 1

    def rest(self):
        self.some(3 * self.count)
        for w in range(3):
            self.own(w).start()

    def finish(self):
        me = lax.axis_index("dp")

        def step(i, carry):
            k = far_first(i, self.count)
            for w in range(3):
                self.copy(w, k, me).wait_send()
                self.copy(w, k, lax.rem(me - k + self.count, self.count)).wait_recv()
            return carry

        lax.fori_loop(0, self.count - 1, step, 0)
        for w in range(3):
            self.own(w).wait()

    @staticmethod
    def sems(count):
        return [
            pltpu.SemaphoreType.DMA((3, count)),
            pltpu.SemaphoreType.DMA((3, count)),
            pltpu.SemaphoreType.DMA((3,)),
        ]


class Sum:
    def __init__(self, pieces, ins, outs, accs, bufs, send_sem, recv_sem):
        me, side = lax.axis_index("dp"), lax.axis_index("tensor")
        self.pieces, self.ins, self.outs, self.accs, self.bufs = pieces, ins, outs, accs, bufs
        self.send_sem, self.recv_sem = send_sem, recv_sem
        self.core = bit_of(me, 1)
        self.whole = "t" in pieces[0][3]
        self.last = len(pieces[0][3])
        self.mine = {
            "z1": bit_of(me, 8),
            "z0": bit_of(me, 4),
            "x": bit_of(me, 2),
            "t": side if self.whole else 0,
        }

    def exchange(self, i, s):
        which, first, width, order = self.pieces[i]
        columns = pl.ds(first, width)
        if s == 0:
            src = self.ins[which].at[:, :, :, 1 - self.core, :, :, columns]
            place = partner("core")
        else:
            done, now = order[: s - 1], order[s - 1]
            index = []
            for d in DIMS:
                if d in done:
                    index.append(pl.ds(self.mine[d], 1))
                elif d == now:
                    index.append(pl.ds(1 - self.mine[d], 1))
                else:
                    index.append(slice(None))
            src = self.accs[which].at[tuple(index) + (slice(None), columns)]
            place = partner(now)
        return pltpu.make_async_remote_copy(
            src_ref=src,
            dst_ref=self.bufs[i * (self.last + 1) + s],
            send_sem=self.send_sem.at[i, s],
            recv_sem=self.recv_sem.at[i, s],
            device_id=place,
            device_id_type=MESH,
        )

    def add(self, i, s):
        which, first, width, order = self.pieces[i]
        buf = self.bufs[i * (self.last + 1) + s]
        columns = pl.ds(first, width)
        if s == self.last:
            at = tuple(self.mine[d] for d in DIMS) + (slice(None), columns)
            self.outs[which][:, columns] = self.accs[which][at].astype(jnp.float32) + buf[
                0, 0, 0, 0
            ].astype(jnp.float32)
            return
        free = [d for d in DIMS if d in order[s:]]

        def step(b, carry):
            at, frm = dict(self.mine), {d: 0 for d in DIMS}
            left = b
            for d in reversed(free):
                at[d] = frm[d] = lax.rem(left, 2)
                left = lax.div(left, 2)
            at = tuple(at[d] for d in DIMS)
            if s == 0:
                have = self.ins[which][at[:3] + (self.core, at[3], slice(None), columns)]
            else:
                have = self.accs[which][at + (slice(None), columns)]
            got = buf[tuple(frm[d] for d in DIMS)]
            self.accs[which][at + (slice(None), columns)] = (
                have.astype(jnp.float32) + got.astype(jnp.float32)
            ).astype(jnp.bfloat16)
            return carry

        lax.fori_loop(0, 2 ** len(free), step, 0)

    def start(self):
        for i in range(len(self.pieces)):
            self.exchange(i, 0).start()

    def run(self):
        n = len(self.pieces)
        for s in range(self.last + 1):
            for i in range(n):
                self.exchange(i, s).wait_recv()
                self.add(i, s)
                if s < self.last:
                    self.exchange(i, s + 1).start()
        for s in range(self.last + 1):
            for i in range(n):
                self.exchange(i, s).wait_send()

    @staticmethod
    def scratch(pieces, rows, widths):
        whole = 2 if "t" in pieces[0][3] else 1
        stages = len(pieces[0][3]) + 1
        bufs = []
        for _, _, width, order in pieces:
            for s in range(stages):
                free = tuple(2 if d in order[s:] else 1 for d in DIMS)
                bufs.append(pltpu.VMEM(free + (rows, width), jnp.bfloat16))
        accs = [pltpu.VMEM((2, 2, 2, whole, rows, w), jnp.bfloat16) for w in widths]
        sems = [pltpu.SemaphoreType.DMA((len(pieces), stages))] * 2
        return accs, bufs, sems

    @staticmethod
    def view(array, whole):
        blocks = 32 if whole else 16
        return array.reshape(
            2, 2, 2, 2, 2 if whole else 1, array.shape[0] // blocks, array.shape[1]
        )


def home_pieces(wide, thin):
    cut = wide * 3 // 4
    return (
        (0, 0, cut, ORDERS[0]),
        (2, 0, cut, ORDERS[1]),
        (0, cut, wide - cut, ORDERS[2]),
        (2, cut, wide - cut, ORDERS[2]),
        (1, 0, thin, ORDERS[2]),
    )


def home_kernel(count, pieces, *refs):
    n = len(pieces) * 5
    sums = Sum(pieces, refs[:3], refs[6:9], refs[12:15], refs[15 : 15 + n], *refs[15 + n : 17 + n])
    job = Swap(True, count, refs[3:6], refs[9:12], *refs[17 + n :])
    greet_plane(count, [partner("t")])
    sums.start()
    job.start()
    sums.run()
    job.finish()


def bring_home(back, slots, out, grads):
    count = lax.axis_size("dp")
    wide, thin = back.shape[1], slots.shape[1]
    rows = back.shape[0] // 32
    pieces = home_pieces(wide, thin)
    widths = (wide, thin, wide)
    holders, tall, width = grads[0].shape
    accs, bufs, sems = Sum.scratch(pieces, rows, widths)
    results = pl.pallas_call(
        functools.partial(home_kernel, count, pieces),
        out_shape=[jax.ShapeDtypeStruct((rows, w), jnp.float32) for w in widths]
        + [
            jax.ShapeDtypeStruct((holders * count, tall // count, width), g.dtype) for g in grads
        ],
        in_specs=[pl.BlockSpec(memory_space=pltpu.VMEM)] * 3
        + [pl.BlockSpec(memory_space=pl.ANY)] * 3,
        out_specs=[pl.BlockSpec(memory_space=pltpu.VMEM)] * 3
        + [pl.BlockSpec(memory_space=pl.ANY)] * 3,
        scratch_shapes=accs + bufs + sems + Swap.sems(count),
        compiler_params=pltpu.CompilerParams(
            collective_id=2, has_side_effects=True, vmem_limit_bytes=48 << 20
        ),
        name="bring_home",
    )(Sum.view(back, True), Sum.view(slots, True), Sum.view(out, True), *grads)
    return results[:3], results[3:]


class Gather:
    def __init__(self, src, out, sides, sems):
        me, side = lax.axis_index("dp"), lax.axis_index("tensor")
        self.src, self.out, self.sides, self.sems = src, out, sides, sems
        self.rows = src.shape[0]
        self.me, self.t = me, side
        self.z, self.x, self.core = lax.div(me, 4), bit_of(me, 2), bit_of(me, 1)

    def at(self, z, x, t, core):
        place = z * 4 + x * 2 + core
        if self.sides:
            place = place * 2 + t
        return self.out.at[pl.ds(pl.multiple_of(place * self.rows, self.rows), self.rows)]

    def copy(self, pair, index, src, dst, device):
        return pltpu.make_async_remote_copy(
            src_ref=src,
            dst_ref=dst,
            send_sem=self.sems[pair].at[index],
            recv_sem=self.sems[pair + 1].at[index],
            device_id=device,
            device_id_type=MESH,
        )

    def line(self, up, z, src=None):
        block = self.at(z, self.x, self.t, self.core)
        step = 4 if up else -4
        device = (lax.rem(self.me + step + 16, 16), self.t)
        return self.copy(0, (int(up), z), block if src is None else src, block, device)

    def over_x(self, diag, z, x, t, src=None):
        block = self.at(z, x, t, self.core)
        return self.copy(
            2, (int(diag), z), block if src is None else src, block, partner("x")
        )

    def over_t(self, diag, z, x, t, src=None):
        block = self.at(z, x, t, self.core)
        return self.copy(
            4, (int(diag), z), block if src is None else src, block, partner("t")
        )

    def over_core(self, z, x, t, core, src=None):
        block = self.at(z, x, t, core)
        return self.copy(6, (t, x, z), block if src is None else src, block, partner("core"))

    def own(self):
        return pltpu.make_async_copy(
            self.src, self.at(self.z, self.x, self.t, self.core), self.sems[8]
        )

    def sideways(self, z, src=None):
        self.over_x(False, z, self.x, self.t, src).start()
        if self.sides:
            self.over_t(False, z, self.x, self.t, src).start()
        self.over_core(z, self.x, self.t, self.core, src).start()

    def start(self):
        @pl.when(self.z < 3)
        def _():
            self.line(True, self.z, self.src).start()

        @pl.when(self.z > 0)
        def _():
            self.line(False, self.z, self.src).start()

        self.sideways(self.z, self.src)
        self.own().start()

    def pass_line(self, s):
        @pl.when(self.z >= s)
        def _():
            z = self.z - s
            self.line(True, z).wait_recv()

            @pl.when(self.z < 3)
            def _():
                self.line(True, z).start()

            self.sideways(z)

        @pl.when(self.z + s <= 3)
        def _():
            z = self.z + s
            self.line(False, z).wait_recv()

            @pl.when(self.z > 0)
            def _():
                self.line(False, z).start()

            self.sideways(z)

    def second(self, z):
        x, t = self.x, self.t
        self.over_x(False, z, 1 - x, t).wait_recv()
        if self.sides:

            @pl.when(z >= 2)
            def _():
                self.over_t(True, z, 1 - x, t).start()

        self.over_core(z, 1 - x, t, self.core).start()
        if self.sides:
            self.over_t(False, z, x, 1 - t).wait_recv()

            @pl.when(z < 2)
            def _():
                self.over_x(True, z, x, 1 - t).start()

            self.over_core(z, x, 1 - t, self.core).start()

    def pass_second(self, s):
        @pl.when(self.z >= s)
        def _():
            self.second(self.z - s)

        if s:

            @pl.when(self.z + s <= 3)
            def _():
                self.second(self.z + s)

    def third(self, z):
        block = (z, 1 - self.x, 1 - self.t)
        (self.over_x if z < 2 else self.over_t)(True, *block).wait_recv()
        self.over_core(*block, self.core).start()

    def steps(self):
        line, second = self.pass_line, self.pass_second
        order = (line, 1), (second, 0), (line, 2), (second, 1), (line, 3), (second, 2), (second, 3)
        steps = [functools.partial(*each) for each in order]
        if self.sides:
            steps += [functools.partial(self.third, z) for z in range(4)]
        return steps + [self.arrived]

    def arrived(self):
        for z in range(4):
            for x in range(2):
                for t in range(2) if self.sides else [self.t]:
                    self.over_core(z, x, t, 1 - self.core).wait_recv()
        self.own().wait()

    def finish(self):
        x, t = self.x, self.t
        for z in range(4):

            @pl.when((z <= self.z) & (self.z < 3))
            def _():
                self.line(True, z).wait_send()

            @pl.when((z >= self.z) & (self.z > 0))
            def _():
                self.line(False, z).wait_send()

            self.over_x(False, z, x, t).wait_send()
            if self.sides:
                self.over_t(False, z, x, t).wait_send()
                if z < 2:
                    self.over_x(True, z, x, 1 - t).wait_send()
                else:
                    self.over_t(True, z, 1 - x, t).wait_send()
            for xb in range(2):
                for tb in range(2) if self.sides else [t]:
                    self.over_core(z, xb, tb, self.core).wait_send()

    @staticmethod
    def semaphores():
        dma = pltpu.SemaphoreType.DMA
        return [dma((2, 4))] * 6 + [dma((2, 2, 4))] * 2 + [dma]


def lanes_of(shape):
    return lax.broadcasted_iota(jnp.int32, shape, 1)


def turn(values, cosine, sine_table, back):
    width = values.shape[1]
    low = lax.rem(lanes_of(values.shape), HEAD_DIM) < HEAD_DIM // 2
    later = pltpu.roll(values, width - HEAD_DIM // 2, 1)
    earlier = pltpu.roll(values, HEAD_DIM // 2, 1)
    moved = jnp.where(low, later, -earlier) if back else jnp.where(low, -later, earlier)
    return values * cosine + moved * sine_table


def twice(pair, second):
    wide = pair.astype(jnp.float32)
    other = pltpu.roll(wide, HEAD_DIM, 1)
    low = lanes_of(wide.shape) < HEAD_DIM
    both = jnp.where(low, other, wide) if second else jnp.where(low, wide, other)
    return both.astype(jnp.bfloat16)


def stack_heads(pair):
    wide = pair.astype(jnp.float32)
    low = lanes_of(wide.shape) < HEAD_DIM
    return jnp.concatenate(
        [jnp.where(low, wide, 0.0), jnp.where(low, 0.0, wide)], axis=0
    ).astype(jnp.bfloat16)


def unstack_heads(stacked):
    rows = stacked.shape[0] // 2
    low = lanes_of((rows, stacked.shape[1])) < HEAD_DIM
    return jnp.where(low, stacked[:rows], stacked[rows:])


def probabilities(query, keys, mask):
    scores = dot_f32(query, keys, ((1,), (1,))) * score_scale
    scores = jnp.where(jnp.concatenate([mask, mask], axis=0) > 0.0, scores, masked_score)
    row_max = jnp.max(scores, axis=1, keepdims=True)
    log_total = row_max + jnp.log(jnp.sum(jnp.exp(scores - row_max), axis=1, keepdims=True))
    return jnp.exp(scores - log_total)


def chunk(ref, i, width):
    return ref[:, i * width : (i + 1) * width]


PLAN = (2, 2, 2, 2, 2)


def experts_kernel(
    rows_ref, tag_ref, gate_ref, up_ref, down_ref, router_ref, *refs
):
    back_o, slots_o, out_o, grad_o, acc = refs[0], refs[1], refs[2], refs[3:6], refs[6]
    i, steps = pl.program_id(0), pl.num_programs(0)
    holders = gate_ref.shape[0]
    rows_bf = rows_ref[...]
    width = rows_bf.shape[1]
    moe = tag_ref[:, :width].astype(jnp.float32)
    routes = tag_ref[:, width:].astype(jnp.float32)
    lane = lanes_of(routes.shape).astype(jnp.float32)
    split = dot_f32(rows_bf, router_ref[...], ((1,), (0,)))
    logits = split + (pltpu.roll(split, 128 - EXPERTS, 1) + pltpu.roll(split, 128 - 2 * EXPERTS, 1))
    named = jnp.zeros(routes.shape, jnp.float32)
    for k in range(TOPK):
        named = jnp.where(routes[:, k : k + 1] == lane, 1.0, named)
    masked = jnp.where(named > 0.0, logits, -jnp.inf)
    raised = jnp.exp(masked - jnp.max(masked, axis=1, keepdims=True))
    gates = raised / jnp.sum(raised, axis=1, keepdims=True)
    first = lax.axis_index("dp") * holders
    out_part = back_part = gate_slots = 0.0
    for h in range(holders):
        at = (lane == (first + h).astype(jnp.float32)) & (named > 0.0)
        gate = jnp.sum(jnp.where(at, gates, 0.0), axis=1, keepdims=True)
        here = jnp.sum(jnp.where(at, 1.0, 0.0), axis=1, keepdims=True) > 0.0
        gate_pre = dot_f32(rows_bf, gate_ref[h], ((1,), (0,)))
        up_pre = dot_f32(rows_bf, up_ref[h], ((1,), (0,)))
        route_grad = (gate * moe).astype(jnp.bfloat16)
        inner_grad = dot_f32(route_grad, down_ref[h], ((1,), (0,)))
        sigmoid_gate = jax.nn.sigmoid(gate_pre)
        activated = gate_pre * sigmoid_gate
        inner_act = (activated * up_pre).astype(jnp.bfloat16)
        gate_pre_grad = (
            inner_grad * up_pre * sigmoid_gate * (1.0 + gate_pre * (1.0 - sigmoid_gate))
        ).astype(jnp.bfloat16)
        up_pre_grad = (inner_grad * activated).astype(jnp.bfloat16)
        produced = dot_f32(inner_act, down_ref[h], ((1,), (1,))).astype(jnp.bfloat16)
        produced = produced.astype(jnp.float32)
        out_part = out_part + gate * produced
        gate_part = jnp.sum(moe * produced, axis=1, keepdims=True)
        gate_slots = gate_slots + jnp.where(at & here, gate_part, 0.0)
        back = dot_f32(gate_pre_grad, gate_ref[h], ((1,), (1,))) + dot_f32(
            up_pre_grad, up_ref[h], ((1,), (1,))
        )
        back_part = back_part + back.astype(jnp.bfloat16).astype(jnp.float32)
        for w, (left, right) in enumerate(
            ((rows_bf, gate_pre_grad), (rows_bf, up_pre_grad), (route_grad, inner_act))
        ):
            made = dot_f32(left, right, ((0,), (0,)))

            @pl.when(i == 0)
            def _():
                acc[w, h] = made

            @pl.when(i > 0)
            def _():
                acc[w, h] += made

    back_o[...] = back_part.astype(jnp.bfloat16)
    out_o[...] = out_part.astype(jnp.bfloat16)
    high = gate_slots.astype(jnp.bfloat16).astype(jnp.float32)
    rest = gate_slots - high
    middle = rest.astype(jnp.bfloat16).astype(jnp.float32)
    low = (rest - middle).astype(jnp.bfloat16).astype(jnp.float32)
    slots_o[...] = (
        high + (pltpu.roll(middle, EXPERTS, 1) + pltpu.roll(low, 2 * EXPERTS, 1))
    ).astype(jnp.bfloat16)

    @pl.when(i == steps - 1)
    def _():
        for w in range(3):
            grad_o[w][...] = acc[w].astype(jnp.bfloat16)


def run_experts(rows_all, tagged_all, weights, router, tile=512):
    total, width = rows_all.shape
    bf16 = jnp.bfloat16
    shape = jax.ShapeDtypeStruct
    still = lambda a: pl.BlockSpec(a.shape, lambda i: (0,) * a.ndim)
    moving = lambda w: pl.BlockSpec((tile, w), lambda i: (i, 0))
    results = pl.pallas_call(
        experts_kernel,
        grid=(total // tile,),
        out_shape=[shape((total, width), bf16), shape((total, 128), bf16), shape((total, width), bf16)]
        + [shape(w.shape, bf16) for w in weights],
        in_specs=[moving(width), moving(tagged_all.shape[1])]
        + [still(w) for w in weights]
        + [still(router)],
        out_specs=[moving(width), moving(128), moving(width)] + [still(w) for w in weights],
        scratch_shapes=[pltpu.VMEM((3,) + weights[0].shape, jnp.float32)],
        compiler_params=pltpu.CompilerParams(vmem_limit_bytes=48 << 20),
        name="experts",
    )(rows_all, tagged_all, *weights, router)
    return results[:3], results[3:]


def front_kernel(count, *refs):
    attn_ref, gate_ref, up_ref, down_ref, first_ref, tokens_ref = refs[:6]
    cos_ref, sin_ref, mask_ref, gain_ref = refs[6:10]
    gate_o, up_o, down_o, rows_o, attn_o, wide_o = refs[10:16]
    q_o, k_o, v_o, mixed_o, hidden_o, normed_o = refs[16:22]
    part, got, pair_sem = refs[22:25]
    swap = Swap(False, count, [gate_ref, up_ref, down_ref], [gate_o, up_o, down_o], *refs[25:28])
    attn = Gather(attn_ref, attn_o, False, refs[28:37])
    rows_job = Gather(normed_o, rows_o, True, refs[37:46])
    side = lax.axis_index("tensor")
    rows = first_ref.shape[0]

    def half(which):
        return pl.ds(pl.multiple_of(which * rows, rows), rows)

    spread = pltpu.make_async_remote_copy(
        src_ref=first_ref,
        dst_ref=wide_o.at[half(side)],
        send_sem=pair_sem.at[0, 0],
        recv_sem=pair_sem.at[0, 1],
        device_id=partner("t"),
        device_id_type=MESH,
    )
    narrowed = pltpu.make_async_remote_copy(
        src_ref=part.at[half(1 - side)],
        dst_ref=got,
        send_sem=pair_sem.at[1, 0],
        recv_sem=pair_sem.at[1, 1],
        device_id=partner("t"),
        device_id_type=MESH,
    )
    greet_plane(count, [partner("t")])
    attn.start()
    spread.start()
    wide_o[half(side), :] = first_ref[...]
    swap.some(PLAN[0])
    for each in attn.steps():
        each()
        swap.some(PLAN[1])
    spread.wait()
    swap.some(PLAN[2])
    q_cols, k_cols = q_o.shape[1], k_o.shape[1]
    step = 256
    for i in range((q_cols + 2 * k_cols) // step):
        at = i * step
        made = dot_f32(wide_o[...], chunk(attn_o, i, step), ((1,), (0,)))
        if at < q_cols + k_cols:
            made = turn(made, cos_ref[...], sin_ref[...], False)
        made = made.astype(jnp.bfloat16)
        if at < q_cols:
            q_o[:, at : at + step] = made
        elif at < q_cols + k_cols:
            k_o[:, at - q_cols : at - q_cols + step] = made
        else:
            v_o[:, at - q_cols - k_cols : at - q_cols - k_cols + step] = made
        swap.some(PLAN[2])
    pair_width = 2 * HEAD_DIM
    for g in range(q_cols // pair_width):
        query = stack_heads(chunk(q_o, g, pair_width))
        keys = twice(chunk(k_o, g // 2, pair_width), g % 2)
        values = twice(chunk(v_o, g // 2, pair_width), g % 2)
        probs = probabilities(query, keys, mask_ref[...]).astype(jnp.bfloat16)
        mixed = unstack_heads(dot_f32(probs, values, ((1,), (0,))))
        mixed_o[:, g * pair_width : (g + 1) * pair_width] = mixed.astype(jnp.bfloat16)
        swap.some(PLAN[2])
    base = q_cols + 2 * k_cols
    for i in range(attn_o.shape[0] // step):
        part[:, i * step : (i + 1) * step] = dot_f32(
            mixed_o[...], attn_o[i * step : (i + 1) * step, base:], ((1,), (1,))
        )
    narrowed.start()
    swap.some(PLAN[3])
    narrowed.wait()
    hidden = tokens_ref[...].astype(jnp.float32) + residual_scale * (
        part[half(side), :] + got[...]
    )
    hidden_o[...] = hidden
    rscale = lax.rsqrt(jnp.mean(hidden * hidden, axis=1, keepdims=True) + eps_norm)
    normed_o[...] = (hidden * rscale * gain_ref[...]).astype(jnp.bfloat16)
    rows_job.start()
    for each in rows_job.steps():
        swap.some(PLAN[4])
        each()
    swap.rest()
    attn.finish()
    rows_job.finish()
    swap.finish()


def front(packed, experts, first, tokens, cosine, sine_table, mask, gain, q_cols, k_cols):
    count = lax.axis_size("dp")
    rows, width = tokens.shape
    total = rows * count * 2
    wide_rows = 2 * rows
    experts_all, expert_rows, half_ff = experts[0].shape
    bf16, f32 = jnp.bfloat16, jnp.float32
    shape = jax.ShapeDtypeStruct
    vmem, anywhere = pl.BlockSpec(memory_space=pltpu.VMEM), pl.BlockSpec(memory_space=pl.ANY)
    return pl.pallas_call(
        functools.partial(front_kernel, count),
        out_shape=[
            shape((experts_all // count, expert_rows * count, half_ff), bf16) for _ in range(3)
        ]
        + [
            shape((total, width), bf16),
            shape((packed.shape[0] * count, packed.shape[1]), bf16),
            shape((wide_rows, width), bf16),
            shape((wide_rows, q_cols), bf16),
            shape((wide_rows, k_cols), bf16),
            shape((wide_rows, k_cols), bf16),
            shape((wide_rows, q_cols), bf16),
            shape((rows, width), f32),
            shape((rows, width), bf16),
        ],
        in_specs=[vmem] + [anywhere] * 3 + [vmem] * 6,
        out_specs=[anywhere] * 4 + [vmem] * 8,
        scratch_shapes=[
            pltpu.VMEM((wide_rows, width), f32),
            pltpu.VMEM((rows, width), f32),
            pltpu.SemaphoreType.DMA((2, 2)),
        ]
        + Swap.sems(count)
        + Gather.semaphores() * 2,
        compiler_params=pltpu.CompilerParams(
            collective_id=1, has_side_effects=True, vmem_limit_bytes=40 << 20
        ),
        name="front",
    )(packed, *experts, first, tokens, cosine, sine_table, mask, gain)


def last_pieces(width):
    cut = width // 2
    return ((0, 0, cut, ("x", "z0", "z1")), (0, cut, width - cut, ("z0", "x", "z1")))


def last_kernel(count, width, pieces, *refs):
    n = len(pieces) * 4
    x_ref, g_ref, o_ref, sum_ref = refs[:4]
    sums = Sum(pieces, [g_ref], [sum_ref], refs[4:5], refs[5 : 5 + n], *refs[5 + n : 7 + n])
    send_sem, recv_sem, own_sem = refs[7 + n :]
    total = count * width
    me = lax.axis_index("dp") * width + lax.axis_index("tensor")
    barrier = pltpu.get_barrier_semaphore()

    def place(k):
        peer = lax.rem(me + k, total)
        return (lax.div(peer, width), lax.rem(peer, width))

    def greet(k, carry):
        pl.semaphore_signal(barrier, inc=1, device_id=place(k), device_id_type=MESH)
        return carry

    def copy(k, slot):
        return pltpu.make_async_remote_copy(
            src_ref=x_ref,
            dst_ref=o_ref.at[slot],
            send_sem=send_sem.at[k],
            recv_sem=recv_sem.at[k],
            device_id=place(k),
            device_id_type=MESH,
        )

    def start(k, carry):
        copy(k, me).start()
        return carry

    def finish(k, carry):
        copy(k, me).wait_send()
        copy(k, lax.rem(me - k + total, total)).wait_recv()
        return carry

    lax.fori_loop(1, total, greet, 0)
    pl.semaphore_wait(barrier, total - 1)
    sums.start()
    own = pltpu.make_async_copy(x_ref, o_ref.at[me], own_sem)
    own.start()
    lax.fori_loop(1, total, start, 0)
    sums.run()
    lax.fori_loop(1, total, finish, 0)
    own.wait()


def last_sums(block, grads):
    count, width = lax.axis_size("dp"), lax.axis_size("tensor")
    total = count * width
    rows, columns = grads.shape[0] // count, grads.shape[1]
    pieces = last_pieces(columns)
    accs, bufs, sems = Sum.scratch(pieces, rows, (columns,))
    return pl.pallas_call(
        functools.partial(last_kernel, count, width, pieces),
        out_shape=[
            jax.ShapeDtypeStruct((total,) + block.shape, block.dtype),
            jax.ShapeDtypeStruct((rows, columns), jnp.float32),
        ],
        in_specs=[pl.BlockSpec(memory_space=pltpu.VMEM)] * 2,
        out_specs=[pl.BlockSpec(memory_space=pltpu.VMEM)] * 2,
        scratch_shapes=accs
        + bufs
        + sems
        + [
            pltpu.SemaphoreType.DMA((total,)),
            pltpu.SemaphoreType.DMA((total,)),
            pltpu.SemaphoreType.DMA,
        ],
        compiler_params=pltpu.CompilerParams(
            collective_id=4, has_side_effects=True, vmem_limit_bytes=40 << 20
        ),
        name="last_sums",
    )(block, Sum.view(grads, False))


def local_near(
    tokens,
    out_grad,
    lengths,
    routes,
    attn_gain,
    w_query,
    w_key,
    w_value,
    w_out,
    ffn_gain,
    w_router,
    w_gate,
    w_up,
    w_down,
):
    local_rows = tokens.shape[0]
    row_count = routes.shape[0]
    model_width = tokens.shape[1]
    holders = EXPERTS // lax.axis_size("dp")
    heads_here = w_query.shape[1] // HEAD_DIM
    kv_here = w_key.shape[1] // HEAD_DIM
    own_row = lax.axis_index("tensor") * local_rows
    q_cols, k_cols = w_query.shape[1], w_key.shape[1]
    cuts = (q_cols, q_cols + k_cols, q_cols + 2 * k_cols)
    tokens_f32 = tokens.astype(jnp.float32)
    out_f32 = out_grad.astype(jnp.float32)
    own_routes = lax.dynamic_slice_in_dim(routes, own_row, local_rows, 0)
    position, allowed = seq_layout(lengths[0], row_count)
    cosine, sine_table = rope_tables(position, HEAD_DIM)
    unit_first, scale_first, normed_first = norm_forward(tokens_f32, attn_gain)
    tagged = jnp.concatenate(
        [
            (residual_scale * out_f32).astype(jnp.bfloat16),
            jnp.pad(own_routes.astype(jnp.bfloat16), ((0, 0), (0, 128 - TOPK))),
        ],
        axis=1,
    )
    tagged_all = lax.all_gather(tagged, ("dp", "tensor"), axis=0, tiled=True)
    (
        local_gate,
        local_up,
        local_down,
        rows_all,
        full_attn,
        wide_first,
        query_flat,
        key_flat,
        value_flat,
        mixed_out,
        hidden,
        normed_second,
    ) = front(
        jnp.concatenate([w_query, w_key, w_value, w_out], axis=1),
        [w_gate, w_up, w_down],
        normed_first,
        tokens,
        jnp.tile(cosine[:, 0], (1, 4)),
        jnp.tile(sine_table[:, 0], (1, 4)),
        allowed.astype(jnp.float32),
        ffn_gain[None, :],
        q_cols,
        k_cols,
    )
    full_qkv = full_attn[:, : cuts[2]]
    full_out = full_attn[:, cuts[2] :]
    unit_second, scale_second, _ = norm_forward(hidden, ffn_gain)
    expert_ids = jnp.arange(EXPERTS, dtype=jnp.int32)

    def gate_of(rows_bf, row_routes):
        named = jnp.any(row_routes[:, :, None] == expert_ids[None, None, :], axis=1)
        logits = exact_dot(rows_bf, w_router, ((1,), (0,)))
        masked = jnp.where(named, logits, -jnp.inf)
        raised = jnp.exp(masked - jnp.max(masked, axis=1, keepdims=True))
        return named, raised / jnp.sum(raised, axis=1, keepdims=True)

    router_parts = jnp.pad(
        jnp.concatenate(split_three(w_router), axis=1), ((0, 0), (0, 128 - 3 * EXPERTS))
    )
    (back_part, slot_parts, out_part), stacks = run_experts(
        rows_all, tagged_all, [local_gate, local_up, local_down], router_parts
    )
    (expert_back, slots, out_home), expert_grads = bring_home(
        back_part, slot_parts, out_part, stacks
    )
    gate_grad = (
        slots[:, :EXPERTS]
        + slots[:, EXPERTS : 2 * EXPERTS]
        + slots[:, 2 * EXPERTS : 3 * EXPERTS]
    )
    block_rows = (hidden + residual_scale * out_home).astype(jnp.bfloat16)
    _, gates_own = gate_of(normed_second, own_routes)
    logits_grad = gates_own * (gate_grad - jnp.sum(gates_own * gate_grad, axis=1, keepdims=True))
    second_grad = expert_back + jnp.dot(logits_grad, w_router.T, precision=lax.Precision.HIGHEST)
    hidden_back, ffn_gain_grad = norm_backward(second_grad, unit_second, scale_second, ffn_gain)
    hidden_grad = out_f32 + hidden_back
    attn_grad = spread_rows((residual_scale * hidden_grad).astype(jnp.bfloat16))
    mixed_grad = jnp.dot(attn_grad, full_out, preferred_element_type=jnp.float32).astype(
        jnp.bfloat16
    )
    out_w_grad = dot_f32(attn_grad, mixed_out, ((0,), (0,)))
    query_heads = query_flat.reshape(row_count, heads_here, HEAD_DIM)
    key_heads = key_flat.reshape(row_count, kv_here, HEAD_DIM)
    value_heads = value_flat.reshape(row_count, kv_here, HEAD_DIM)
    _, scores = score_block(query_heads, key_heads, allowed)
    row_max = jnp.max(scores, axis=-1, keepdims=True)
    log_total = row_max + jnp.log(jnp.sum(jnp.exp(scores - row_max), axis=-1, keepdims=True))
    dquery, key_grad, dvalues = attend_back(
        query_heads, key_heads, value_heads, allowed, log_total, mixed_grad
    )
    query_grad = (
        unrotate(dquery, cosine, sine_table)
        .astype(jnp.bfloat16)
        .reshape(row_count, heads_here * HEAD_DIM)
    )
    keys_grad = (
        unrotate(key_grad, cosine, sine_table)
        .astype(jnp.bfloat16)
        .reshape(row_count, kv_here * HEAD_DIM)
    )
    value_grad = dvalues.astype(jnp.bfloat16).reshape(row_count, kv_here * HEAD_DIM)
    qkv_grad = jnp.concatenate([query_grad, keys_grad, value_grad], axis=1)
    qkv_w_grad = dot_f32(wide_first, qkv_grad, ((0,), (0,)))
    packed_grad = jnp.concatenate([qkv_w_grad, out_w_grad], axis=1).astype(jnp.bfloat16)
    first_grad = narrow(dot_f32(qkv_grad, full_qkv, ((1,), (1,))))
    tokens_back, attn_gain_grad = norm_backward(first_grad, unit_first, scale_first, attn_gain)
    tokens_grad = hidden_grad + tokens_back
    tall = local_rows * EXPERTS // 128
    wide = model_width // 128
    shared, packed_grad = last_sums(
        jnp.concatenate(
            [
                logits_grad.reshape(tall, 128),
                attn_gain_grad.reshape(wide, 128),
                ffn_gain_grad.reshape(wide, 128),
            ],
            axis=0,
        ),
        packed_grad,
    )
    logits_grad_all = shared[:, :tall].reshape(rows_all.shape[0], EXPERTS)
    router_total = exact_dot(rows_all, logits_grad_all, ((0,), (0,)))
    gains = jnp.sum(shared[:, tall:], axis=0).reshape(2, model_width)
    return (
        block_rows,
        tokens_grad,
        gains[0],
        packed_grad[:, : cuts[0]],
        packed_grad[:, cuts[0] : cuts[1]],
        packed_grad[:, cuts[1] : cuts[2]],
        packed_grad[:, cuts[2] :],
        gains[1],
        router_total,
        *[g.astype(jnp.float32) for g in expert_grads],
    )


def local_far(
    tokens,
    out_grad,
    lengths,
    routes,
    attn_gain,
    w_query,
    w_key,
    w_value,
    w_out,
    ffn_gain,
    w_router,
    w_gate,
    w_up,
    w_down,
):
    local_rows = tokens.shape[0]
    row_count = routes.shape[0]
    model_width = tokens.shape[1]
    dp_count = lax.axis_size("dp")
    replicas = max(1, dp_count // EXPERTS)
    holders = max(1, EXPERTS // dp_count)
    clusters = EXPERTS // holders
    half_ff = w_gate.shape[2]
    heads_here = w_query.shape[1] // HEAD_DIM
    kv_here = w_key.shape[1] // HEAD_DIM
    own_row = lax.axis_index("tensor") * local_rows
    groups = (
        None
        if replicas == 1
        else [[r * clusters + c for c in range(clusters)] for r in range(replicas)]
    )
    q_cols, k_cols = w_query.shape[1], w_key.shape[1]
    cuts = (q_cols, q_cols + k_cols, q_cols + 2 * k_cols)
    packed_attn = gather_weights(jnp.concatenate([w_query, w_key, w_value, w_out], axis=1))
    full_qkv = packed_attn[:, : cuts[2]]
    full_out = packed_attn[:, cuts[2] :]

    def spread_out(weight):
        grouped = weight.reshape(clusters, holders, weight.shape[1], half_ff)
        return jnp.broadcast_to(grouped[None], (replicas,) + grouped.shape).reshape(
            dp_count, holders, weight.shape[1], half_ff
        )

    def fetch(weight):
        moved = lax.all_to_all(spread_out(weight), "dp", split_axis=0, concat_axis=2, tiled=True)
        return moved.reshape(holders, model_width, half_ff)

    local_gate, local_up, local_down = fetch(w_gate), fetch(w_up), fetch(w_down)
    tokens_f32 = tokens.astype(jnp.float32)
    out_f32 = out_grad.astype(jnp.float32)
    position, allowed = seq_layout(lengths[0], row_count)
    cosine, sine_table = rope_tables(position, HEAD_DIM)
    unit_first, scale_first, normed_first = norm_forward(tokens_f32, attn_gain)
    both = spread_rows(
        jnp.concatenate(
            [normed_first, (residual_scale * out_f32).astype(jnp.bfloat16)], axis=1
        )
    )
    wide_first = both[:, :model_width]
    tagged = jnp.concatenate(
        [
            both[:, model_width:],
            jnp.pad(routes.astype(jnp.bfloat16), ((0, 0), (0, 128 - TOPK))),
        ],
        axis=1,
    )
    tagged_all = gather_dp(tagged, groups)
    moe_all = tagged_all[:, :model_width]
    routes_all = tagged_all[:, model_width : model_width + TOPK].astype(jnp.int32)
    qkv = jnp.dot(wide_first, full_qkv, preferred_element_type=jnp.float32)
    query_heads = rotate(
        qkv[:, : cuts[0]].reshape(row_count, heads_here, HEAD_DIM), cosine, sine_table
    ).astype(jnp.bfloat16)
    key_heads = rotate(
        qkv[:, cuts[0] : cuts[1]].reshape(row_count, kv_here, HEAD_DIM), cosine, sine_table
    ).astype(jnp.bfloat16)
    value_heads = qkv[:, cuts[1] :].astype(jnp.bfloat16).reshape(row_count, kv_here, HEAD_DIM)
    mixed_out, log_total = attend(query_heads, key_heads, value_heads, allowed)
    hidden = tokens_f32 + residual_scale * narrow(dot_f32(mixed_out, full_out, ((1,), (1,))))
    unit_second, scale_second, normed_second = norm_forward(hidden, ffn_gain)
    rows_all = gather_dp(spread_rows(normed_second), groups)

    expert_ids = jnp.arange(EXPERTS, dtype=jnp.int32)

    def gate_of(rows_bf, row_routes):
        picked = row_routes[:, :, None] == expert_ids[None, None, :]
        logits = exact_dot(rows_bf, w_router, ((1,), (0,)))
        named = jnp.any(picked, axis=1)
        masked = jnp.where(named, logits, -jnp.inf)
        raised = jnp.exp(masked - jnp.max(masked, axis=1, keepdims=True))
        return picked, named, raised / jnp.sum(raised, axis=1, keepdims=True)

    _, named_all, gates_all = gate_of(rows_all, routes_all)
    first_expert = lax.axis_index("dp") % clusters * holders
    out_part = back_part = gate_slots = 0.0
    grads = []
    for h in range(holders):
        gate = lax.dynamic_slice_in_dim(gates_all, first_expert + h, 1, 1)
        here = lax.dynamic_slice_in_dim(named_all, first_expert + h, 1, 1)
        gate_pre = dot_f32(rows_all, local_gate[h], ((1,), (0,)))
        up_pre = dot_f32(rows_all, local_up[h], ((1,), (0,)))
        sigmoid_gate = jax.nn.sigmoid(gate_pre)
        activated = gate_pre * sigmoid_gate
        inner_act = (activated * up_pre).astype(jnp.bfloat16)
        produced = dot_f32(inner_act, local_down[h], ((1,), (1,))).astype(jnp.bfloat16)
        produced = produced.astype(jnp.float32)
        out_part = out_part + jnp.where(here, gate * produced, 0.0)
        moe_f32 = moe_all.astype(jnp.float32)
        gate_part = jnp.sum(moe_f32 * produced, axis=1, keepdims=True)
        gate_slots = gate_slots + jnp.where(routes_all == first_expert + h, gate_part, 0.0)
        route_grad = jnp.where(here, gate * moe_f32, 0.0).astype(jnp.bfloat16)
        inner_grad = dot_f32(route_grad, local_down[h], ((1,), (0,)))
        gate_pre_grad = (
            inner_grad * up_pre * sigmoid_gate * (1.0 + gate_pre * (1.0 - sigmoid_gate))
        ).astype(jnp.bfloat16)
        up_pre_grad = (inner_grad * activated).astype(jnp.bfloat16)
        back = dot_f32(gate_pre_grad, local_gate[h], ((1,), (1,))) + dot_f32(
            up_pre_grad, local_up[h], ((1,), (1,))
        )
        back_part = back_part + back.astype(jnp.bfloat16).astype(jnp.float32)
        grads.append(
            (
                dot_f32(rows_all, gate_pre_grad, ((0,), (0,))).astype(jnp.bfloat16),
                dot_f32(rows_all, up_pre_grad, ((0,), (0,))).astype(jnp.bfloat16),
                dot_f32(route_grad, inner_act, ((0,), (0,))).astype(jnp.bfloat16),
            )
        )
    slot_parts = split_three(gate_slots)
    pad = jnp.zeros((rows_all.shape[0], 128 - 3 * TOPK), jnp.bfloat16)
    home = scatter_dp(
        jnp.concatenate(
            [back_part.astype(jnp.bfloat16)] + slot_parts + [pad, out_part.astype(jnp.bfloat16)],
            axis=1,
        ),
        groups,
    ).astype(jnp.float32)
    back_home = home[:, : model_width + 128]
    out_home = home[:, model_width + 128 :]
    slots = back_home[:, model_width:]
    gate_half = slots[:, :TOPK] + slots[:, TOPK : 2 * TOPK] + slots[:, 2 * TOPK : 3 * TOPK]
    own_back = narrow(
        jnp.concatenate(
            [back_home[:, :model_width], jnp.pad(gate_half, ((0, 0), (0, 128 - TOPK)))], axis=1
        )
    )
    expert_back = own_back[:, :model_width]
    gate_grad = own_back[:, model_width : model_width + TOPK]
    block_rows = (hidden + residual_scale * narrow(out_home)).astype(jnp.bfloat16)

    def send_home(index):
        stacked = jnp.stack([grads[h][index] for h in range(holders)])
        moved = lax.all_to_all(stacked[None], "dp", split_axis=2, concat_axis=0, tiled=True)
        return jnp.sum(
            moved.astype(jnp.float32).reshape(
                replicas, clusters * holders, moved.shape[2], half_ff
            ),
            axis=0,
        )

    own_routes = lax.dynamic_slice_in_dim(routes, own_row, local_rows, 0)
    picked_own, _, gates_dense = gate_of(normed_second, own_routes)
    gates_own = jnp.sum(jnp.where(picked_own, gates_dense[:, None, :], 0.0), axis=2)
    chosen_grad = gates_own * (gate_grad - jnp.sum(gates_own * gate_grad, axis=1, keepdims=True))
    logits_grad = jnp.sum(jnp.where(picked_own, chosen_grad[:, :, None], 0.0), axis=1)
    second_grad = expert_back + jnp.dot(logits_grad, w_router.T, precision=lax.Precision.HIGHEST)
    hidden_back, ffn_gain_grad = norm_backward(second_grad, unit_second, scale_second, ffn_gain)
    hidden_grad = out_f32 + hidden_back
    attn_grad = spread_rows((residual_scale * hidden_grad).astype(jnp.bfloat16))
    mixed_grad = jnp.dot(attn_grad, full_out, preferred_element_type=jnp.float32).astype(
        jnp.bfloat16
    )
    out_w_grad = dot_f32(attn_grad, mixed_out, ((0,), (0,)))
    dquery, key_grad, dvalues = attend_back(
        query_heads, key_heads, value_heads, allowed, log_total, mixed_grad
    )
    query_grad = (
        unrotate(dquery, cosine, sine_table)
        .astype(jnp.bfloat16)
        .reshape(row_count, heads_here * HEAD_DIM)
    )
    keys_grad = (
        unrotate(key_grad, cosine, sine_table)
        .astype(jnp.bfloat16)
        .reshape(row_count, kv_here * HEAD_DIM)
    )
    value_grad = dvalues.astype(jnp.bfloat16).reshape(row_count, kv_here * HEAD_DIM)
    qkv_grad = jnp.concatenate([query_grad, keys_grad, value_grad], axis=1)
    qkv_w_grad = dot_f32(wide_first, qkv_grad, ((0,), (0,)))
    packed_grad = scatter_weights(
        jnp.concatenate([qkv_w_grad, out_w_grad], axis=1).astype(jnp.bfloat16)
    ).astype(jnp.float32)
    first_grad = narrow(dot_f32(qkv_grad, full_qkv, ((1,), (1,))))
    tokens_back, attn_gain_grad = norm_backward(first_grad, unit_first, scale_first, attn_gain)
    tokens_grad = hidden_grad + tokens_back
    attn_gain_total, ffn_gain_total, router_total = lax.psum(
        (
            attn_gain_grad,
            ffn_gain_grad,
            exact_dot(normed_second, logits_grad, ((0,), (0,))),
        ),
        ("dp", "tensor"),
    )
    return (
        block_rows,
        tokens_grad,
        attn_gain_total,
        packed_grad[:, : cuts[0]],
        packed_grad[:, cuts[0] : cuts[1]],
        packed_grad[:, cuts[1] : cuts[2]],
        packed_grad[:, cuts[2] :],
        ffn_gain_total,
        router_total,
        send_home(0),
        send_home(1),
        send_home(2),
    )


def solution(mesh):
    placed = (
        P(("dp", "tensor"), None),
        P(("dp", "tensor"), None),
        P("dp", None),
        P("dp", None),
        P(),
        P("dp", "tensor"),
        P("dp", "tensor"),
        P("dp", "tensor"),
        P("dp", "tensor"),
        P(),
        P(),
        P(None, "dp", "tensor"),
        P(None, "dp", "tensor"),
        P(None, "dp", "tensor"),
    )
    near = mesh.shape["dp"] == 16 and mesh.shape["tensor"] == 2
    return jax.shard_map(
        local_near if near else local_far,
        mesh=mesh,
        in_specs=placed,
        out_specs=(
            P(("dp", "tensor"), None),
            P(("dp", "tensor"), None),
            P(),
            P("dp", "tensor"),
            P("dp", "tensor"),
            P("dp", "tensor"),
            P("dp", "tensor"),
            P(),
            P(),
            P(None, "dp", "tensor"),
            P(None, "dp", "tensor"),
            P(None, "dp", "tensor"),
        ),
        check_vma=False,
    )
```

```python
import functools

import jax
import jax.numpy as jnp
from jax import lax
from jax.experimental import pallas as pl
from jax.experimental.pallas import tpu as pltpu
from jax.sharding import PartitionSpec as P

EXPERTS = 32
TOPK = 8
HEAD_DIM = 64


eps_norm = 1e-06
residual_scale = 0.22
score_scale = 0.015625
rope_base = 10000.0
masked_score = -1e30


def norm_forward(row_block, gain_vec):
    rscale = lax.rsqrt(jnp.mean(row_block * row_block, axis=1, keepdims=True) + eps_norm)
    unit_rows = row_block * rscale
    return (unit_rows, rscale, (unit_rows * gain_vec).astype(jnp.bfloat16))


def norm_backward(gradient, unit_rows, rscale, gain_vec):
    unit_grad = gradient * gain_vec
    back_rows = rscale * (
        unit_grad - unit_rows * jnp.mean(unit_grad * unit_rows, axis=1, keepdims=True)
    )
    return (back_rows, jnp.sum(gradient * unit_rows, axis=0))


def seq_layout(seq_lengths, row_count):
    order = jnp.arange(seq_lengths.shape[0], dtype=jnp.int32)
    seq_ends = jnp.sum(jnp.where(order[:, None] <= order[None, :], seq_lengths[:, None], 0), axis=0)
    starts = seq_ends - seq_lengths
    places = jnp.arange(row_count, dtype=jnp.int32)
    segment = jnp.sum((places[:, None] >= seq_ends[None, :]).astype(jnp.int32), axis=1)
    member = segment[:, None] == jnp.arange(seq_lengths.shape[0], dtype=jnp.int32)[None, :]
    offset = jnp.sum(jnp.where(member, starts[None, :], 0), axis=1)
    allowed = (segment[:, None] == segment[None, :]) & (places[None, :] <= places[:, None])
    return (places - offset, allowed)


def rope_tables(position, head_width):
    frequency = rope_base ** (-(jnp.arange(head_width // 2, dtype=jnp.float32) * 2.0) / head_width)
    angles = position.astype(jnp.float32)[:, None] * frequency[None, :]
    cosine = jnp.concatenate([jnp.cos(angles), jnp.cos(angles)], axis=1)[:, None, :]
    sine_table = jnp.concatenate([jnp.sin(angles), jnp.sin(angles)], axis=1)[:, None, :]
    return (cosine, sine_table)


def rotate(vectors, cosine, sine_table):
    half_width = vectors.shape[-1] // 2
    first_half = vectors[..., :half_width]
    second_half = vectors[..., half_width:]
    return vectors * cosine + jnp.concatenate([-second_half, first_half], axis=-1) * sine_table


def unrotate(gradient, cosine, sine_table):
    half_width = gradient.shape[-1] // 2
    first_half = gradient[..., :half_width]
    second_half = gradient[..., half_width:]
    return gradient * cosine + jnp.concatenate([second_half, -first_half], axis=-1) * sine_table


def score_block(query_heads, key_heads, allowed):
    row_count, head_count, head_width = query_heads.shape
    kv_count = key_heads.shape[1]
    grouped = query_heads.reshape(row_count, kv_count, head_count // kv_count, head_width)
    scores = (
        jnp.einsum("igrd,jgd->grij", grouped, key_heads, preferred_element_type=jnp.float32)
        * score_scale
    )
    return (grouped, jnp.where(allowed[None, None], scores, masked_score))


def attend(query_heads, key_heads, value_heads, allowed):
    row_count, head_count, head_width = query_heads.shape
    grouped, scores = score_block(query_heads, key_heads, allowed)
    row_max = jnp.max(scores, axis=-1, keepdims=True)
    log_total = row_max + jnp.log(jnp.sum(jnp.exp(scores - row_max), axis=-1, keepdims=True))
    prob_bf = jnp.exp(scores - log_total).astype(jnp.bfloat16)
    mixed_out = jnp.einsum(
        "grij,jgd->igrd", prob_bf, value_heads, preferred_element_type=jnp.float32
    )
    return (mixed_out.reshape(row_count, head_count * head_width).astype(jnp.bfloat16), log_total)


def attend_back(query_heads, key_heads, value_heads, allowed, log_total, mixed_grad):
    row_count, head_count, head_width = query_heads.shape
    kv_count = key_heads.shape[1]
    grouped, scores = score_block(query_heads, key_heads, allowed)
    prob_full = jnp.exp(scores - log_total)
    grad_heads = mixed_grad.reshape(row_count, kv_count, head_count // kv_count, head_width)
    dprobs = jnp.einsum(
        "igrd,jgd->grij", grad_heads, value_heads, preferred_element_type=jnp.float32
    )
    row_delta = jnp.sum(prob_full * dprobs, axis=-1, keepdims=True)
    dscores = (prob_full * (dprobs - row_delta)).astype(jnp.bfloat16)
    dquery = (
        jnp.einsum("grij,jgd->igrd", dscores, key_heads, preferred_element_type=jnp.float32)
        * score_scale
    )
    key_grad = (
        jnp.einsum("grij,igrd->jgd", dscores, grouped, preferred_element_type=jnp.float32)
        * score_scale
    )
    dvalues = jnp.einsum(
        "grij,igrd->jgd",
        prob_full.astype(jnp.bfloat16),
        grad_heads,
        preferred_element_type=jnp.float32,
    )
    return (dquery.reshape(row_count, head_count, head_width), key_grad, dvalues)


def spread_rows(row_block):
    return lax.all_gather(row_block, "tensor", axis=0, tiled=True)


def narrow(partial_rows):
    if lax.axis_size("tensor") != 2:
        return lax.psum_scatter(partial_rows, "tensor", scatter_dimension=0, tiled=True)
    half = partial_rows.shape[0] // 2
    mine = lax.axis_index("tensor")
    away = lax.dynamic_slice_in_dim(partial_rows, (1 - mine) * half, half, 0)
    kept = lax.dynamic_slice_in_dim(partial_rows, mine * half, half, 0)
    return kept + lax.ppermute(away, "tensor", [(0, 1), (1, 0)])


def split_three(values):
    high = lax.reduce_precision(values, 8, 7)
    rest = values - high
    middle = lax.reduce_precision(rest, 8, 7)
    return [part.astype(jnp.bfloat16) for part in (high, middle, rest - middle)]


def dot_f32(left, right, dims):
    return lax.dot_general(left, right, (dims, ((), ())), preferred_element_type=jnp.float32)


def exact_dot(rows_bf, values, dims):
    width = values.shape[1]
    product = dot_f32(rows_bf, jnp.concatenate(split_three(values), axis=1), dims)
    return product[:, :width] + (product[:, width : 2 * width] + product[:, 2 * width :])


def gather_dp(rows, groups):
    return lax.all_gather(rows, "dp", axis=0, tiled=True, axis_index_groups=groups)


def scatter_dp(rows, groups):
    return lax.psum_scatter(
        rows, "dp", scatter_dimension=0, tiled=True, axis_index_groups=groups
    )


def gather_weights(packed):
    return lax.all_gather(packed, "dp", axis=0, tiled=True)


def scatter_weights(packed):
    return lax.psum_scatter(packed, "dp", scatter_dimension=0, tiled=True)


MESH = pl.DeviceIdType.MESH
WEIGHT = {"core": 1, "x": 2, "z0": 4, "z1": 8}
DIMS = ("z1", "z0", "x", "t")
ORDERS = (("x", "t", "z0", "z1"), ("t", "z0", "x", "z1"), ("z0", "x", "z1", "t"))


def bit_of(me, weight):
    return lax.rem(lax.div(me, weight), 2)


def partner(name):
    me, side = lax.axis_index("dp"), lax.axis_index("tensor")
    if name == "t":
        return (me, 1 - side)
    return (me + WEIGHT[name] * (1 - 2 * bit_of(me, WEIGHT[name])), side)


def greet_plane(count, others=()):
    me, side = lax.axis_index("dp"), lax.axis_index("tensor")
    barrier = pltpu.get_barrier_semaphore()

    def greet(k, carry):
        pl.semaphore_signal(
            barrier, inc=1, device_id=(lax.rem(me + k, count), side), device_id_type=MESH
        )
        return carry

    lax.fori_loop(1, count, greet, 0)
    for place in others:
        pl.semaphore_signal(barrier, inc=1, device_id=place, device_id_type=MESH)
    pl.semaphore_wait(barrier, count - 1 + len(others))


def far_first(i, count):
    return count // 2 + (1 - 2 * lax.rem(i, 2)) * lax.div(i + 1, 2)


class Swap:
    def __init__(self, home, count, ins, outs, send_sem, recv_sem, own_sem):
        self.home, self.count = home, count
        self.issued = 0
        self.ins, self.outs = ins, outs
        self.sems = (send_sem, recv_sem, own_sem)
        if home:
            self.holders, self.rows = ins[0].shape[0], ins[0].shape[1] // count
        else:
            self.holders, self.rows = ins[0].shape[0] // count, ins[0].shape[1]

    def pick(self, ref, peer, home):
        if home:
            return ref.at[:, pl.ds(peer * self.rows, self.rows)]
        return ref.at[pl.ds(peer * self.holders, self.holders)]

    def copy(self, w, k, owner):
        me, side = lax.axis_index("dp"), lax.axis_index("tensor")
        peer = lax.rem(me + k, self.count)
        return pltpu.make_async_remote_copy(
            src_ref=self.pick(self.ins[w], peer, self.home),
            dst_ref=self.pick(self.outs[w], owner, not self.home),
            send_sem=self.sems[0].at[w, k],
            recv_sem=self.sems[1].at[w, k],
            device_id=(peer, side),
            device_id_type=MESH,
        )

    def own(self, w):
        me = lax.axis_index("dp")
        return pltpu.make_async_copy(
            self.pick(self.ins[w], me, self.home),
            self.pick(self.outs[w], me, not self.home),
            self.sems[2].at[w],
        )

    def start(self):
        def step(i, carry):
            for w in range(3):
                self.copy(w, far_first(i, self.count), lax.axis_index("dp")).start()
            return carry

        lax.fori_loop(0, self.count - 1, step, 0)
        for w in range(3):
            self.own(w).start()

    def some(self, amount):
        for _ in range(amount):
            if self.issued < 3 * (self.count - 1):
                i, w = divmod(self.issued, 3)
                k = self.count // 2 + (1 - 2 * (i % 2)) * ((i + 1) // 2)
                self.copy(w, k, lax.axis_index("dp")).start()
                self.issued += 1

    def rest(self):
        self.some(3 * self.count)
        for w in range(3):
            self.own(w).start()

    def finish(self):
        me = lax.axis_index("dp")

        def step(i, carry):
            k = far_first(i, self.count)
            for w in range(3):
                self.copy(w, k, me).wait_send()
                self.copy(w, k, lax.rem(me - k + self.count, self.count)).wait_recv()
            return carry

        lax.fori_loop(0, self.count - 1, step, 0)
        for w in range(3):
            self.own(w).wait()

    @staticmethod
    def sems(count):
        return [
            pltpu.SemaphoreType.DMA((3, count)),
            pltpu.SemaphoreType.DMA((3, count)),
            pltpu.SemaphoreType.DMA((3,)),
        ]


class Sum:
    def __init__(
        self,
        pieces,
        ins,
        outs,
        accs,
        bufs,
        send_sem,
        recv_sem,
        firsts=None,
        first_s=None,
        first_r=None,
    ):
        me, side = lax.axis_index("dp"), lax.axis_index("tensor")
        self.pieces, self.ins, self.outs, self.accs, self.bufs = pieces, ins, outs, accs, bufs
        self.send_sem, self.recv_sem = send_sem, recv_sem
        self.firsts, self.first_s, self.first_r = firsts, first_s, first_r
        self.core = bit_of(me, 1)
        self.whole = "t" in pieces[0][3]
        self.last = len(pieces[0][3])
        self.mine = {
            "z1": bit_of(me, 8),
            "z0": bit_of(me, 4),
            "x": bit_of(me, 2),
            "t": side if self.whole else 0,
        }

    def buf(self, i, s):
        if self.firsts is not None:
            return self.bufs[i * self.last + s - 1] if s else None
        return self.bufs[i * (self.last + 1) + s]

    def first_copy(self, which, z):
        z1, z0 = (z // 2, z % 2) if isinstance(z, int) else (lax.div(z, 2), lax.rem(z, 2))
        return pltpu.make_async_remote_copy(
            src_ref=self.ins[which].at[z1, z0, :, 1 - self.core],
            dst_ref=self.firsts[which].at[z1, z0],
            send_sem=self.first_s.at[which, z],
            recv_sem=self.first_r.at[which, z],
            device_id=partner("core"),
            device_id_type=MESH,
        )

    def send_first(self, which, z):
        self.first_copy(which, z).start()

    def exchange(self, i, s):
        which, first, width, order = self.pieces[i]
        columns = pl.ds(first, width)
        if s == 0:
            src = self.ins[which].at[:, :, :, 1 - self.core, :, :, columns]
            place = partner("core")
        else:
            done, now = order[: s - 1], order[s - 1]
            index = []
            for d in DIMS:
                if d in done:
                    index.append(pl.ds(self.mine[d], 1))
                elif d == now:
                    index.append(pl.ds(1 - self.mine[d], 1))
                else:
                    index.append(slice(None))
            src = self.accs[which].at[tuple(index) + (slice(None), columns)]
            place = partner(now)
        return pltpu.make_async_remote_copy(
            src_ref=src,
            dst_ref=self.buf(i, s),
            send_sem=self.send_sem.at[i, s],
            recv_sem=self.recv_sem.at[i, s],
            device_id=place,
            device_id_type=MESH,
        )

    def add(self, i, s):
        which, first, width, order = self.pieces[i]
        buf = self.buf(i, s)
        columns = pl.ds(first, width)
        if s == self.last:
            at = tuple(self.mine[d] for d in DIMS) + (slice(None), columns)
            self.outs[which][:, columns] = self.accs[which][at].astype(jnp.float32) + buf[
                0, 0, 0, 0
            ].astype(jnp.float32)
            return
        free = [d for d in DIMS if d in order[s:]]

        def step(b, carry):
            at, frm = dict(self.mine), {d: 0 for d in DIMS}
            left = b
            for d in reversed(free):
                at[d] = frm[d] = lax.rem(left, 2)
                left = lax.div(left, 2)
            at = tuple(at[d] for d in DIMS)
            if s == 0:
                have = self.ins[which][at[:3] + (self.core, at[3], slice(None), columns)]
            else:
                have = self.accs[which][at + (slice(None), columns)]
            frm = tuple(frm[d] for d in DIMS)
            if s == 0 and self.firsts is not None:
                got = self.firsts[which][frm + (slice(None), columns)]
            else:
                got = buf[frm]
            self.accs[which][at + (slice(None), columns)] = (
                have.astype(jnp.float32) + got.astype(jnp.float32)
            ).astype(jnp.bfloat16)
            return carry

        lax.fori_loop(0, 2 ** len(free), step, 0)

    def start(self):
        for i in range(len(self.pieces)):
            self.exchange(i, 0).start()

    def run(self, between=lambda: None):
        n = len(self.pieces)
        early = self.firsts is not None
        if early:
            for which in range(len(self.ins)):
                for z in range(4):
                    self.first_copy(which, z).wait_recv()
        for s in range(self.last + 1):
            for i in range(n):
                if s or not early:
                    self.exchange(i, s).wait_recv()
                self.add(i, s)
                if s < self.last:
                    self.exchange(i, s + 1).start()
                between()
        if early:
            for which in range(len(self.ins)):
                for z in range(4):
                    self.first_copy(which, z).wait_send()
        for s in range(int(early), self.last + 1):
            for i in range(n):
                self.exchange(i, s).wait_send()

    @staticmethod
    def scratch(pieces, rows, widths, begin=0):
        whole = 2 if "t" in pieces[0][3] else 1
        stages = len(pieces[0][3]) + 1
        bufs = []
        for _, _, width, order in pieces:
            for s in range(begin, stages):
                free = tuple(2 if d in order[s:] else 1 for d in DIMS)
                bufs.append(pltpu.VMEM(free + (rows, width), jnp.bfloat16))
        accs = [pltpu.VMEM((2, 2, 2, whole, rows, w), jnp.bfloat16) for w in widths]
        sems = [pltpu.SemaphoreType.DMA((len(pieces), stages))] * 2
        return accs, bufs, sems

    @staticmethod
    def view(array, whole):
        blocks = 32 if whole else 16
        return array.reshape(
            2, 2, 2, 2, 2 if whole else 1, array.shape[0] // blocks, array.shape[1]
        )


def home_pieces(wide, thin):
    cut = wide * 3 // 4
    return (
        (0, 0, cut, ORDERS[0]),
        (2, 0, cut, ORDERS[1]),
        (0, cut, wide - cut, ORDERS[2]),
        (2, cut, wide - cut, ORDERS[2]),
        (1, 0, thin, ORDERS[2]),
    )


def last_pieces(width):
    cut = width // 2
    return ((0, 0, cut, ("x", "z0", "z1")), (0, cut, width - cut, ("z0", "x", "z1")))


class Gather:
    def __init__(self, src, out, sides, sems):
        me, side = lax.axis_index("dp"), lax.axis_index("tensor")
        self.src, self.out, self.sides, self.sems = src, out, sides, sems
        self.rows = src.shape[0]
        self.me, self.t = me, side
        self.z, self.x, self.core = lax.div(me, 4), bit_of(me, 2), bit_of(me, 1)

    def at(self, z, x, t, core):
        place = z * 4 + x * 2 + core
        if self.sides:
            place = place * 2 + t
        return self.out.at[pl.ds(pl.multiple_of(place * self.rows, self.rows), self.rows)]

    def copy(self, pair, index, src, dst, device):
        return pltpu.make_async_remote_copy(
            src_ref=src,
            dst_ref=dst,
            send_sem=self.sems[pair].at[index],
            recv_sem=self.sems[pair + 1].at[index],
            device_id=device,
            device_id_type=MESH,
        )

    def line(self, up, z, src=None):
        block = self.at(z, self.x, self.t, self.core)
        step = 4 if up else -4
        device = (lax.rem(self.me + step + 16, 16), self.t)
        return self.copy(0, (int(up), z), block if src is None else src, block, device)

    def over_x(self, diag, z, x, t, src=None):
        block = self.at(z, x, t, self.core)
        return self.copy(
            2, (int(diag), z), block if src is None else src, block, partner("x")
        )

    def over_t(self, diag, z, x, t, src=None):
        block = self.at(z, x, t, self.core)
        return self.copy(
            4, (int(diag), z), block if src is None else src, block, partner("t")
        )

    def over_core(self, z, x, t, core, src=None):
        block = self.at(z, x, t, core)
        return self.copy(6, (t, x, z), block if src is None else src, block, partner("core"))

    def own(self):
        return pltpu.make_async_copy(
            self.src, self.at(self.z, self.x, self.t, self.core), self.sems[8]
        )

    def sideways(self, z, src=None):
        self.over_x(False, z, self.x, self.t, src).start()
        if self.sides:
            self.over_t(False, z, self.x, self.t, src).start()
        self.over_core(z, self.x, self.t, self.core, src).start()

    def start(self):
        @pl.when(self.z < 3)
        def _():
            self.line(True, self.z, self.src).start()

        @pl.when(self.z > 0)
        def _():
            self.line(False, self.z, self.src).start()

        self.sideways(self.z, self.src)
        self.own().start()

    def pass_line(self, s):
        @pl.when(self.z >= s)
        def _():
            z = self.z - s
            self.line(True, z).wait_recv()

            @pl.when(self.z < 3)
            def _():
                self.line(True, z).start()

            self.sideways(z)

        @pl.when(self.z + s <= 3)
        def _():
            z = self.z + s
            self.line(False, z).wait_recv()

            @pl.when(self.z > 0)
            def _():
                self.line(False, z).start()

            self.sideways(z)

    def second(self, z):
        x, t = self.x, self.t
        self.over_x(False, z, 1 - x, t).wait_recv()
        if self.sides:

            @pl.when(z >= 2)
            def _():
                self.over_t(True, z, 1 - x, t).start()

        self.over_core(z, 1 - x, t, self.core).start()
        if self.sides:
            self.over_t(False, z, x, 1 - t).wait_recv()

            @pl.when(z < 2)
            def _():
                self.over_x(True, z, x, 1 - t).start()

            self.over_core(z, x, 1 - t, self.core).start()

    def pass_second(self, s):
        @pl.when(self.z >= s)
        def _():
            self.second(self.z - s)

        if s:

            @pl.when(self.z + s <= 3)
            def _():
                self.second(self.z + s)

    def third(self, z):
        block = (z, 1 - self.x, 1 - self.t)
        (self.over_x if z < 2 else self.over_t)(True, *block).wait_recv()
        self.over_core(*block, self.core).start()

    def steps(self):
        line, second = self.pass_line, self.pass_second
        order = (line, 1), (second, 0), (line, 2), (second, 1), (line, 3), (second, 2), (second, 3)
        steps = [functools.partial(*each) for each in order]
        if self.sides:
            steps += [functools.partial(self.third, z) for z in range(4)]
        return steps + [self.arrived]

    def arrived(self):
        for z in range(4):
            for x in range(2):
                for t in range(2) if self.sides else [self.t]:
                    self.over_core(z, x, t, 1 - self.core).wait_recv()
        self.own().wait()

    def finish(self):
        x, t = self.x, self.t
        for z in range(4):

            @pl.when((z <= self.z) & (self.z < 3))
            def _():
                self.line(True, z).wait_send()

            @pl.when((z >= self.z) & (self.z > 0))
            def _():
                self.line(False, z).wait_send()

            self.over_x(False, z, x, t).wait_send()
            if self.sides:
                self.over_t(False, z, x, t).wait_send()
                if z < 2:
                    self.over_x(True, z, x, 1 - t).wait_send()
                else:
                    self.over_t(True, z, 1 - x, t).wait_send()
            for xb in range(2):
                for tb in range(2) if self.sides else [t]:
                    self.over_core(z, xb, tb, self.core).wait_send()

    @staticmethod
    def semaphores():
        dma = pltpu.SemaphoreType.DMA
        return [dma((2, 4))] * 6 + [dma((2, 2, 4))] * 2 + [dma]


def lanes_of(shape):
    return lax.broadcasted_iota(jnp.int32, shape, 1)


def turn(values, cosine, sine_table, back):
    width = values.shape[1]
    low = lax.rem(lanes_of(values.shape), HEAD_DIM) < HEAD_DIM // 2
    later = pltpu.roll(values, width - HEAD_DIM // 2, 1)
    earlier = pltpu.roll(values, HEAD_DIM // 2, 1)
    moved = jnp.where(low, later, -earlier) if back else jnp.where(low, -later, earlier)
    return values * cosine + moved * sine_table


def twice(pair, second):
    wide = pair.astype(jnp.float32)
    other = pltpu.roll(wide, HEAD_DIM, 1)
    low = lanes_of(wide.shape) < HEAD_DIM
    both = jnp.where(low, other, wide) if second else jnp.where(low, wide, other)
    return both.astype(jnp.bfloat16)


def stack_heads(pair):
    wide = pair.astype(jnp.float32)
    low = lanes_of(wide.shape) < HEAD_DIM
    return jnp.concatenate(
        [jnp.where(low, wide, 0.0), jnp.where(low, 0.0, wide)], axis=0
    ).astype(jnp.bfloat16)


def unstack_heads(stacked):
    rows = stacked.shape[0] // 2
    low = lanes_of((rows, stacked.shape[1])) < HEAD_DIM
    return jnp.where(low, stacked[:rows], stacked[rows:])


def probabilities(query, keys, mask):
    scores = dot_f32(query, keys, ((1,), (1,))) * score_scale
    scores = jnp.where(jnp.concatenate([mask, mask], axis=0) > 0.0, scores, masked_score)
    row_max = jnp.max(scores, axis=1, keepdims=True)
    log_total = row_max + jnp.log(jnp.sum(jnp.exp(scores - row_max), axis=1, keepdims=True))
    return jnp.exp(scores - log_total)


def chunk(ref, i, width):
    return ref[:, i * width : (i + 1) * width]


PLAN = (2, 2, 2, 2, 2)


def front_kernel(count, *refs):
    attn_ref, gate_ref, up_ref, down_ref, first_ref, tokens_ref = refs[:6]
    cos_ref, sin_ref, mask_ref, gain_ref = refs[6:10]
    gate_o, up_o, down_o, rows_o, attn_o, wide_o = refs[10:16]
    q_o, k_o, v_o, mixed_o, hidden_o, normed_o = refs[16:22]
    part, got, pair_sem = refs[22:25]
    swap = Swap(False, count, [gate_ref, up_ref, down_ref], [gate_o, up_o, down_o], *refs[25:28])
    attn = Gather(attn_ref, attn_o, False, refs[28:37])
    rows_job = Gather(normed_o, rows_o, True, refs[37:46])
    side = lax.axis_index("tensor")
    rows = first_ref.shape[0]

    def half(which):
        return pl.ds(pl.multiple_of(which * rows, rows), rows)

    spread = pltpu.make_async_remote_copy(
        src_ref=first_ref,
        dst_ref=wide_o.at[half(side)],
        send_sem=pair_sem.at[0, 0],
        recv_sem=pair_sem.at[0, 1],
        device_id=partner("t"),
        device_id_type=MESH,
    )
    narrowed = pltpu.make_async_remote_copy(
        src_ref=part.at[half(1 - side)],
        dst_ref=got,
        send_sem=pair_sem.at[1, 0],
        recv_sem=pair_sem.at[1, 1],
        device_id=partner("t"),
        device_id_type=MESH,
    )
    greet_plane(count, [partner("t")])
    attn.start()
    spread.start()
    wide_o[half(side), :] = first_ref[...]
    swap.some(PLAN[0])
    for each in attn.steps():
        each()
        swap.some(PLAN[1])
    spread.wait()
    swap.some(PLAN[2])
    q_cols, k_cols = q_o.shape[1], k_o.shape[1]
    step = 256
    for i in range((q_cols + 2 * k_cols) // step):
        at = i * step
        made = dot_f32(wide_o[...], chunk(attn_o, i, step), ((1,), (0,)))
        if at < q_cols + k_cols:
            made = turn(made, cos_ref[...], sin_ref[...], False)
        made = made.astype(jnp.bfloat16)
        if at < q_cols:
            q_o[:, at : at + step] = made
        elif at < q_cols + k_cols:
            k_o[:, at - q_cols : at - q_cols + step] = made
        else:
            v_o[:, at - q_cols - k_cols : at - q_cols - k_cols + step] = made
        swap.some(PLAN[2])
    pair_width = 2 * HEAD_DIM
    for g in range(q_cols // pair_width):
        query = stack_heads(chunk(q_o, g, pair_width))
        keys = twice(chunk(k_o, g // 2, pair_width), g % 2)
        values = twice(chunk(v_o, g // 2, pair_width), g % 2)
        probs = probabilities(query, keys, mask_ref[...]).astype(jnp.bfloat16)
        mixed = unstack_heads(dot_f32(probs, values, ((1,), (0,))))
        mixed_o[:, g * pair_width : (g + 1) * pair_width] = mixed.astype(jnp.bfloat16)
        swap.some(PLAN[2])
    base = q_cols + 2 * k_cols
    for i in range(attn_o.shape[0] // step):
        part[:, i * step : (i + 1) * step] = dot_f32(
            mixed_o[...], attn_o[i * step : (i + 1) * step, base:], ((1,), (1,))
        )
    narrowed.start()
    swap.some(PLAN[3])
    narrowed.wait()
    hidden = tokens_ref[...].astype(jnp.float32) + residual_scale * (
        part[half(side), :] + got[...]
    )
    hidden_o[...] = hidden
    rscale = lax.rsqrt(jnp.mean(hidden * hidden, axis=1, keepdims=True) + eps_norm)
    normed_o[...] = (hidden * rscale * gain_ref[...]).astype(jnp.bfloat16)
    rows_job.start()
    for each in rows_job.steps():
        swap.some(PLAN[4])
        each()
    swap.rest()
    attn.finish()
    rows_job.finish()
    swap.finish()


def front(packed, experts, first, tokens, cosine, sine_table, mask, gain, q_cols, k_cols):
    count = lax.axis_size("dp")
    rows, width = tokens.shape
    total = rows * count * 2
    wide_rows = 2 * rows
    experts_all, expert_rows, half_ff = experts[0].shape
    bf16, f32 = jnp.bfloat16, jnp.float32
    shape = jax.ShapeDtypeStruct
    vmem, anywhere = pl.BlockSpec(memory_space=pltpu.VMEM), pl.BlockSpec(memory_space=pl.ANY)
    return pl.pallas_call(
        functools.partial(front_kernel, count),
        out_shape=[
            shape((experts_all // count, expert_rows * count, half_ff), bf16) for _ in range(3)
        ]
        + [
            shape((total, width), bf16),
            shape((packed.shape[0] * count, packed.shape[1]), bf16),
            shape((wide_rows, width), bf16),
            shape((wide_rows, q_cols), bf16),
            shape((wide_rows, k_cols), bf16),
            shape((wide_rows, k_cols), bf16),
            shape((wide_rows, q_cols), bf16),
            shape((rows, width), f32),
            shape((rows, width), bf16),
        ],
        in_specs=[vmem] + [anywhere] * 3 + [vmem] * 6,
        out_specs=[anywhere] * 4 + [vmem] * 8,
        scratch_shapes=[
            pltpu.VMEM((wide_rows, width), f32),
            pltpu.VMEM((rows, width), f32),
            pltpu.SemaphoreType.DMA((2, 2)),
        ]
        + Swap.sems(count)
        + Gather.semaphores() * 2,
        compiler_params=pltpu.CompilerParams(
            collective_id=1, has_side_effects=True, vmem_limit_bytes=40 << 20
        ),
        name="front",
    )(packed, *experts, first, tokens, cosine, sine_table, mask, gain)


def gates_of(rows_bf, routes, router):
    lane = lanes_of(routes.shape).astype(jnp.float32)
    split = dot_f32(rows_bf, router, ((1,), (0,)))
    logits = split + (pltpu.roll(split, 128 - EXPERTS, 1) + pltpu.roll(split, 128 - 2 * EXPERTS, 1))
    named = jnp.zeros(routes.shape, jnp.float32)
    for k in range(TOPK):
        named = jnp.where(routes[:, k : k + 1] == lane, 1.0, named)
    masked = jnp.where(named > 0.0, logits, -jnp.inf)
    raised = jnp.exp(masked - jnp.max(masked, axis=1, keepdims=True))
    return lane, named, raised / jnp.sum(raised, axis=1, keepdims=True)


class GradMoves:
    def __init__(self, count, grads, outs, send_sem, recv_sem, own_sem):
        self.count, self.grads, self.outs = count, grads, outs
        self.send_sem, self.recv_sem, self.own_sem = send_sem, recv_sem, own_sem
        self.holders = grads.shape[1]
        self.rows = grads.shape[2] // count
        self.issued = 0

    def copy(self, h, w, k, owner):
        me, side = lax.axis_index("dp"), lax.axis_index("tensor")
        peer = lax.rem(me + k, self.count)
        return pltpu.make_async_remote_copy(
            src_ref=self.grads.at[w, h, pl.ds(pl.multiple_of(peer * self.rows, self.rows), self.rows)],
            dst_ref=self.outs[w].at[owner * self.holders + h],
            send_sem=self.send_sem.at[h, w, k],
            recv_sem=self.recv_sem.at[h, w, k],
            device_id=(peer, side),
            device_id_type=MESH,
        )

    def own(self, h, w):
        me = lax.axis_index("dp")
        return pltpu.make_async_copy(
            self.grads.at[w, h, pl.ds(pl.multiple_of(me * self.rows, self.rows), self.rows)],
            self.outs[w].at[me * self.holders + h],
            self.own_sem.at[h, w],
        )

    def send(self, h):
        def step(i, carry):
            for w in range(3):
                self.copy(h, w, far_first(i, self.count), lax.axis_index("dp")).start()
            return carry

        lax.fori_loop(0, self.count - 1, step, 0)

    def some(self, h, amount):
        for _ in range(amount):
            if self.issued < self.count - 1:
                i = self.issued
                k = self.count // 2 + (1 - 2 * (i % 2)) * ((i + 1) // 2)
                for w in range(3):
                    self.copy(h, w, k, lax.axis_index("dp")).start()
                self.issued += 1

    def finish(self):
        me = lax.axis_index("dp")
        for h in range(self.holders):

            def step(k, carry):
                for w in range(3):
                    self.copy(h, w, k, me).wait_send()
                    self.copy(h, w, k, lax.rem(me - k + self.count, self.count)).wait_recv()
                return carry

            lax.fori_loop(1, self.count, step, 0)
            for w in range(3):
                self.own(h, w).wait()


def rms(values):
    return lax.rsqrt(jnp.mean(values * values, axis=1, keepdims=True) + eps_norm)


def back_norm(gradient, unit, scale, gain):
    inner = gradient * gain
    rows = scale * (inner - unit * jnp.mean(inner * unit, axis=1, keepdims=True))
    return rows, jnp.sum(gradient * unit, axis=0, keepdims=True)


SPREAD = (1, 1)


def back_kernel(count, sides, home, late, *refs):
    refs = list(refs)

    def take(n):
        taken = refs[:n]
        del refs[:n]
        return taken

    rows_hbm, tag_hbm, gate_ref, up_ref, down_ref, router_ref, router_t = take(7)
    attn_ref, wide_first, q_ref, k_ref, v_ref, mixed_ref, hidden_ref, normed_ref, own_tag = take(9)
    grad_ref, tokens_ref, gain1_ref, gain2_ref, cos_ref, sin_ref, mask_ref = take(7)
    block_o, tokens_o, weights_o, logits_o, gains_o = take(5)
    moved_o = take(3)
    row_buf, tag_buf, load_sem, acc, grads = take(5)
    parts, firsts, home_out = take(3), take(3), take(3)
    sum_bufs = take(len(home) * 4)
    first_s, first_r, sum_s, sum_r = take(4)
    late_in, late_acc = take(2)
    late_bufs = take(len(late) * 4)
    late_s, late_r = take(2)
    moves = GradMoves(count, grads, moved_o, *take(3))
    lg_ref, gain_blk, wide_attn, mixed_grad, qkv_grad, part, got, pair_sem = take(8)
    spread_logits = Gather(lg_ref, logits_o, True, take(9))
    share_s, share_r, share_own = take(3)
    sums = Sum(home, parts, home_out, firsts, sum_bufs, sum_s, sum_r, firsts, first_s, first_r)
    last = Sum(late, [late_in], [weights_o], [late_acc], late_bufs, late_s, late_r)
    dp, side = lax.axis_index("dp"), lax.axis_index("tensor")
    rows = hidden_ref.shape[0]
    width = hidden_ref.shape[1]
    holders = gate_ref.shape[0]
    tile = row_buf.shape[1]
    tiles = rows_hbm.shape[0] // tile
    total = count * sides
    me = dp * sides + side

    def place(k):
        peer = lax.rem(me + k, total)
        return (lax.div(peer, sides), lax.rem(peer, sides))

    def load(step):
        at = pl.ds(pl.multiple_of(lax.rem(step, tiles) * tile, tile), tile)
        slot = lax.rem(step, 2)
        return [
            pltpu.make_async_copy(rows_hbm.at[at], row_buf.at[slot], load_sem.at[0, slot]),
            pltpu.make_async_copy(tag_hbm.at[at], tag_buf.at[slot], load_sem.at[1, slot]),
        ]

    for each in load(0):
        each.start()
    barrier = pltpu.get_barrier_semaphore()

    def greet(k, carry):
        pl.semaphore_signal(barrier, inc=1, device_id=place(k), device_id_type=MESH)
        return carry

    lax.fori_loop(1, total, greet, 0)
    pl.semaphore_wait(barrier, total - 1)

    def expert_step(step, carry):
        h, z = lax.div(step, tiles), lax.rem(step, tiles)
        slot = lax.rem(step, 2)

        @pl.when(step + 1 < holders * tiles)
        def _():
            for each in load(step + 1):
                each.start()

        for each in load(step):
            each.wait()
        rows_bf = row_buf[slot]
        moe = tag_buf[slot, :, :width].astype(jnp.float32)
        routes = tag_buf[slot, :, width:].astype(jnp.float32)
        lane, named, gates = gates_of(rows_bf, routes, router_ref[...])
        at = (lane == (dp * holders + h).astype(jnp.float32)) & (named > 0.0)
        gate = jnp.sum(jnp.where(at, gates, 0.0), axis=1, keepdims=True)
        gate_w, up_w, down_w = gate_ref[h], up_ref[h], down_ref[h]
        gate_pre = dot_f32(rows_bf, gate_w, ((1,), (0,)))
        up_pre = dot_f32(rows_bf, up_w, ((1,), (0,)))
        route_grad = (gate * moe).astype(jnp.bfloat16)
        inner_grad = dot_f32(route_grad, down_w, ((1,), (0,)))
        sigmoid_gate = jax.nn.sigmoid(gate_pre)
        activated = gate_pre * sigmoid_gate
        inner_act = (activated * up_pre).astype(jnp.bfloat16)
        gate_pre_grad = (
            inner_grad * up_pre * sigmoid_gate * (1.0 + gate_pre * (1.0 - sigmoid_gate))
        ).astype(jnp.bfloat16)
        up_pre_grad = (inner_grad * activated).astype(jnp.bfloat16)
        produced = dot_f32(inner_act, down_w, ((1,), (1,))).astype(jnp.bfloat16)
        produced = produced.astype(jnp.float32)
        gate_part = jnp.sum(moe * produced, axis=1, keepdims=True)
        slots = jnp.where(at, gate_part, 0.0)
        high = slots.astype(jnp.bfloat16).astype(jnp.float32)
        rest = slots - high
        middle = rest.astype(jnp.bfloat16).astype(jnp.float32)
        low = (rest - middle).astype(jnp.bfloat16).astype(jnp.float32)
        slots = high + (pltpu.roll(middle, EXPERTS, 1) + pltpu.roll(low, 2 * EXPERTS, 1))
        back = dot_f32(gate_pre_grad, gate_w, ((1,), (1,))) + dot_f32(
            up_pre_grad, up_w, ((1,), (1,))
        )
        made = (
            back.astype(jnp.bfloat16),
            slots.astype(jnp.bfloat16),
            (gate * produced).astype(jnp.bfloat16),
        )
        z1, z0 = lax.div(z, 2), lax.rem(z, 2)
        for which in range(3):
            ref = parts[which].at[z1, z0]
            block = made[which].reshape(2, 2, 2, rows, made[which].shape[1])

            @pl.when(h == 0)
            def _():
                ref[...] = block

            @pl.when(h > 0)
            def _():
                ref[...] = (ref[...].astype(jnp.float32) + block.astype(jnp.float32)).astype(
                    jnp.bfloat16
                )

        for w, (left, right) in enumerate(
            ((rows_bf, gate_pre_grad), (rows_bf, up_pre_grad), (route_grad, inner_act))
        ):
            product = dot_f32(left, right, ((0,), (0,)))

            @pl.when(z == 0)
            def _():
                acc[w] = product

            @pl.when(z > 0)
            def _():
                acc[w] += product

        @pl.when(h == holders - 1)
        def _():
            for which in range(3):
                sums.send_first(which, z)

        @pl.when(z == tiles - 1)
        def _():
            for w in range(3):
                grads[w, h] = acc[w].astype(jnp.bfloat16)
                moves.own(h, w).start()

            @pl.when(h < holders - 1)
            def _():
                moves.send(h)

        return carry

    lax.fori_loop(0, holders * tiles, expert_step, 0)
    final = holders - 1
    sums.run(lambda: moves.some(final, SPREAD[0]))

    def half(which):
        return pl.ds(pl.multiple_of(which * rows, rows), rows)

    routes = own_tag[:, width:].astype(jnp.float32)
    _, _, gates = gates_of(normed_ref[...], routes, router_ref[...])
    slots = home_out[1][...]
    gate_grad = slots + (pltpu.roll(slots, 128 - EXPERTS, 1) + pltpu.roll(slots, 128 - 2 * EXPERTS, 1))
    logits_grad = gates * (gate_grad - jnp.sum(gates * gate_grad, axis=1, keepdims=True))
    lg_ref[...] = logits_grad
    second_grad = home_out[0][...] + jnp.dot(
        logits_grad,
        router_t[...],
        precision=lax.Precision.HIGHEST,
        preferred_element_type=jnp.float32,
    )
    hidden = hidden_ref[...]
    scale_second = rms(hidden)
    hidden_back, ffn_gain_grad = back_norm(
        second_grad, hidden * scale_second, scale_second, gain2_ref[...]
    )
    hidden_grad = grad_ref[...].astype(jnp.float32) + hidden_back
    tokens_o[...] = hidden_grad
    wide_attn[half(side), :] = (residual_scale * hidden_grad).astype(jnp.bfloat16)
    spread = pltpu.make_async_remote_copy(
        src_ref=wide_attn.at[half(side)],
        dst_ref=wide_attn.at[half(side)],
        send_sem=pair_sem.at[0, 0],
        recv_sem=pair_sem.at[0, 1],
        device_id=partner("t"),
        device_id_type=MESH,
    )
    spread.start()
    spread_logits.start()
    block_o[...] = (hidden + residual_scale * home_out[2][...]).astype(jnp.bfloat16)
    for j in range(width // 128):
        gain_blk[width // 128 + j : width // 128 + j + 1, :] = chunk(ffn_gain_grad, j, 128)
    moves.some(final, SPREAD[1])
    spread.wait()
    q_cols, k_cols = q_ref.shape[1], k_ref.shape[1]
    base = q_cols + 2 * k_cols
    pair_width = 2 * HEAD_DIM
    mixed_grad[...] = dot_f32(wide_attn[...], attn_ref[:, base:], ((1,), (0,))).astype(jnp.bfloat16)
    step = 256

    def keep(at, value):
        late_in[:, :, :, :, :, :, at : at + value.shape[1]] = value.astype(jnp.bfloat16).reshape(
            late_in.shape[:-1] + (value.shape[1],)
        )

    for i in range(q_cols // step):
        keep(
            base + i * step,
            dot_f32(wide_attn[...], chunk(mixed_ref, i, step), ((0,), (0,))),
        )
    moves.some(final, SPREAD[1])
    cosine, sine = cos_ref[:, :pair_width], sin_ref[:, :pair_width]
    low = lanes_of((2 * rows, pair_width)) < HEAD_DIM
    held = None
    for g in range(q_cols // pair_width):
        query = stack_heads(chunk(q_ref, g, pair_width))
        keys = twice(chunk(k_ref, g // 2, pair_width), g % 2)
        values = twice(chunk(v_ref, g // 2, pair_width), g % 2)
        grad_heads = stack_heads(chunk(mixed_grad, g, pair_width))
        probs = probabilities(query, keys, mask_ref[...])
        dprobs = dot_f32(grad_heads, values, ((1,), (1,)))
        delta = jnp.sum(probs * dprobs, axis=1, keepdims=True)
        dscores = (probs * (dprobs - delta)).astype(jnp.bfloat16)
        dquery = unstack_heads(dot_f32(dscores, keys, ((1,), (0,)))) * score_scale
        qkv_grad[:, g * pair_width : (g + 1) * pair_width] = turn(
            dquery, cosine, sine, True
        ).astype(jnp.bfloat16)
        dkeys = dot_f32(dscores, query, ((0,), (0,)))
        dvalues = dot_f32(probs.astype(jnp.bfloat16), grad_heads, ((0,), (0,)))
        dkeys = dkeys + pltpu.roll(dkeys, HEAD_DIM, 1)
        dvalues = dvalues + pltpu.roll(dvalues, HEAD_DIM, 1)
        if g % 2 == 0:
            held = (dkeys, dvalues)
        else:
            j = g // 2 * pair_width
            dkeys = jnp.where(low, held[0], dkeys) * score_scale
            dvalues = jnp.where(low, held[1], dvalues)
            qkv_grad[:, q_cols + j : q_cols + j + pair_width] = turn(
                dkeys, cosine, sine, True
            ).astype(jnp.bfloat16)
            qkv_grad[:, q_cols + k_cols + j : q_cols + k_cols + j + pair_width] = dvalues.astype(
                jnp.bfloat16
            )
        moves.some(final, SPREAD[1])
    for i in range(attn_ref.shape[0] // step):
        part[:, i * step : (i + 1) * step] = dot_f32(
            qkv_grad[...], attn_ref[i * step : (i + 1) * step, :base], ((1,), (1,))
        )
    narrowed = pltpu.make_async_remote_copy(
        src_ref=part.at[half(1 - side)],
        dst_ref=got,
        send_sem=pair_sem.at[1, 0],
        recv_sem=pair_sem.at[1, 1],
        device_id=partner("t"),
        device_id_type=MESH,
    )
    narrowed.start()
    for i in range(base // step):
        keep(i * step, dot_f32(wide_first[...], chunk(qkv_grad, i, step), ((0,), (0,))))
    last.start()
    moves.some(final, count)
    narrowed.wait()
    first_grad = part[half(side), :] + got[...]
    tokens = tokens_ref[...].astype(jnp.float32)
    scale_first = rms(tokens)
    tokens_back, attn_gain_grad = back_norm(
        first_grad, tokens * scale_first, scale_first, gain1_ref[...]
    )
    tokens_o[...] = tokens_o[...] + tokens_back
    for j in range(width // 128):
        gain_blk[j : j + 1, :] = chunk(attn_gain_grad, j, 128)

    def share(k, slot):
        return pltpu.make_async_remote_copy(
            src_ref=gain_blk,
            dst_ref=gains_o.at[slot],
            send_sem=share_s.at[k],
            recv_sem=share_r.at[k],
            device_id=place(k),
            device_id_type=MESH,
        )

    def share_start(k, carry):
        share(k, me).start()
        return carry

    def share_finish(k, carry):
        share(k, me).wait_send()
        share(k, lax.rem(me - k + total, total)).wait_recv()
        return carry

    lax.fori_loop(1, total, share_start, 0)
    own_gain = pltpu.make_async_copy(gain_blk, gains_o.at[me], share_own)
    own_gain.start()
    for each in spread_logits.steps():
        each()
    last.run()
    spread_logits.finish()
    lax.fori_loop(1, total, share_finish, 0)
    own_gain.wait()
    moves.finish()


def back(rows_all, tagged_all, weights, router, router_t, attention, own_tag, own, tables):
    count, sides = lax.axis_size("dp"), lax.axis_size("tensor")
    attn_all, wide_first, query, key, value, mixed, hidden, normed = attention
    rows, width = hidden.shape
    total = rows_all.shape[0]
    columns = attn_all.shape[1]
    late_rows = attn_all.shape[0] // count
    holders, tall, half_ff = weights[0].shape
    tile = total // 4
    bf16, f32 = jnp.bfloat16, jnp.float32
    shape = jax.ShapeDtypeStruct
    vmem, anywhere = pl.BlockSpec(memory_space=pltpu.VMEM), pl.BlockSpec(memory_space=pl.ANY)
    dma = pltpu.SemaphoreType.DMA
    home, late = home_pieces(width, 128), last_pieces(columns)
    widths = (width, 128, width)
    _, home_bufs, home_sems = Sum.scratch(home, rows, widths, 1)
    late_accs, late_bufs, late_sems = Sum.scratch(late, late_rows, (columns,))
    gain_rows = 2 * width // 128
    scratch = [
        pltpu.VMEM((2, tile, width), bf16),
        pltpu.VMEM((2, tile, tagged_all.shape[1]), bf16),
        dma((2, 2)),
        pltpu.VMEM((3, tall, half_ff), f32),
        pltpu.VMEM((3, holders, tall, half_ff), bf16),
    ]
    scratch += [pltpu.VMEM((2, 2, 2, 2, 2, rows, w), bf16) for w in widths]
    scratch += [pltpu.VMEM((2, 2, 2, 2, rows, w), bf16) for w in widths]
    scratch += [pltpu.VMEM((rows, w), f32) for w in widths] + home_bufs
    scratch += [dma((3, 4)), dma((3, 4))] + home_sems
    scratch += [pltpu.VMEM((2, 2, 2, 2, 1, late_rows, columns), bf16)] + late_accs + late_bufs
    scratch += late_sems
    scratch += [dma((holders, 3, count)), dma((holders, 3, count)), dma((holders, 3))]
    scratch += [
        pltpu.VMEM((rows, 128), f32),
        pltpu.VMEM((gain_rows, 128), f32),
        pltpu.VMEM((2 * rows, width), bf16),
        pltpu.VMEM((2 * rows, query.shape[1]), bf16),
        pltpu.VMEM((2 * rows, columns - query.shape[1]), bf16),
        pltpu.VMEM((2 * rows, width), f32),
        pltpu.VMEM((rows, width), f32),
        dma((2, 2)),
    ]
    scratch += Gather.semaphores()
    scratch += [dma((count * sides,)), dma((count * sides,)), dma]
    return pl.pallas_call(
        functools.partial(back_kernel, count, sides, home, late),
        out_shape=[
            shape((rows, width), bf16),
            shape((rows, width), f32),
            shape((late_rows, columns), f32),
            shape((total, 128), f32),
            shape((count * sides, gain_rows, 128), f32),
        ]
        + [shape((holders * count, tall // count, half_ff), bf16) for _ in range(3)],
        in_specs=[anywhere] * 2 + [vmem] * 21,
        out_specs=[vmem] * 5 + [anywhere] * 3,
        scratch_shapes=scratch,
        compiler_params=pltpu.CompilerParams(
            collective_id=2, has_side_effects=True, vmem_limit_bytes=60 << 20
        ),
        name="back",
    )(
        rows_all,
        tagged_all,
        *weights,
        router,
        router_t,
        *attention,
        own_tag,
        *own,
        *tables,
    )


def local_near(
    tokens,
    out_grad,
    lengths,
    routes,
    attn_gain,
    w_query,
    w_key,
    w_value,
    w_out,
    ffn_gain,
    w_router,
    w_gate,
    w_up,
    w_down,
):
    local_rows = tokens.shape[0]
    row_count = routes.shape[0]
    model_width = tokens.shape[1]
    own_row = lax.axis_index("tensor") * local_rows
    q_cols, k_cols = w_query.shape[1], w_key.shape[1]
    cuts = (q_cols, q_cols + k_cols, q_cols + 2 * k_cols)
    tokens_f32 = tokens.astype(jnp.float32)
    out_f32 = out_grad.astype(jnp.float32)
    own_routes = lax.dynamic_slice_in_dim(routes, own_row, local_rows, 0)
    position, allowed = seq_layout(lengths[0], row_count)
    places = jnp.arange(256, dtype=jnp.int32) % (HEAD_DIM // 2)
    frequency = rope_base ** (-(places.astype(jnp.float32) * 2.0) / HEAD_DIM)
    angles = position.astype(jnp.float32)[:, None] * frequency[None, :]
    tables = [jnp.cos(angles), jnp.sin(angles), allowed.astype(jnp.float32)]
    _, _, normed_first = norm_forward(tokens_f32, attn_gain)
    tagged = jnp.concatenate(
        [
            (residual_scale * out_f32).astype(jnp.bfloat16),
            jnp.pad(own_routes.astype(jnp.bfloat16), ((0, 0), (0, 128 - TOPK))),
        ],
        axis=1,
    )
    tagged_all = lax.all_gather(tagged, ("dp", "tensor"), axis=0, tiled=True)
    (
        local_gate,
        local_up,
        local_down,
        rows_all,
        full_attn,
        wide_first,
        query_flat,
        key_flat,
        value_flat,
        mixed_out,
        hidden,
        normed_second,
    ) = front(
        jnp.concatenate([w_query, w_key, w_value, w_out], axis=1),
        [w_gate, w_up, w_down],
        normed_first,
        tokens,
        *tables,
        ffn_gain[None, :],
        q_cols,
        k_cols,
    )
    router_parts = jnp.pad(
        jnp.concatenate(split_three(w_router), axis=1), ((0, 0), (0, 128 - 3 * EXPERTS))
    )
    block_rows, tokens_grad, packed_grad, logits_all, shared, *expert_grads = back(
        rows_all,
        tagged_all,
        [local_gate, local_up, local_down],
        router_parts,
        jnp.pad(w_router.T, ((0, 128 - EXPERTS), (0, 0))),
        [
            full_attn,
            wide_first,
            query_flat,
            key_flat,
            value_flat,
            mixed_out,
            hidden,
            normed_second,
        ],
        tagged,
        [out_grad, tokens, attn_gain[None, :], ffn_gain[None, :]],
        tables,
    )
    router_total = exact_dot(rows_all, logits_all[:, :EXPERTS], ((0,), (0,)))
    gains = jnp.sum(shared, axis=0).reshape(2, model_width)
    return (
        block_rows,
        tokens_grad,
        gains[0],
        packed_grad[:, : cuts[0]],
        packed_grad[:, cuts[0] : cuts[1]],
        packed_grad[:, cuts[1] : cuts[2]],
        packed_grad[:, cuts[2] :],
        gains[1],
        router_total,
        *[g.astype(jnp.float32) for g in expert_grads],
    )


def local_far(
    tokens,
    out_grad,
    lengths,
    routes,
    attn_gain,
    w_query,
    w_key,
    w_value,
    w_out,
    ffn_gain,
    w_router,
    w_gate,
    w_up,
    w_down,
):
    local_rows = tokens.shape[0]
    row_count = routes.shape[0]
    model_width = tokens.shape[1]
    dp_count = lax.axis_size("dp")
    replicas = max(1, dp_count // EXPERTS)
    holders = max(1, EXPERTS // dp_count)
    clusters = EXPERTS // holders
    half_ff = w_gate.shape[2]
    heads_here = w_query.shape[1] // HEAD_DIM
    kv_here = w_key.shape[1] // HEAD_DIM
    own_row = lax.axis_index("tensor") * local_rows
    groups = (
        None
        if replicas == 1
        else [[r * clusters + c for c in range(clusters)] for r in range(replicas)]
    )
    q_cols, k_cols = w_query.shape[1], w_key.shape[1]
    cuts = (q_cols, q_cols + k_cols, q_cols + 2 * k_cols)
    packed_attn = gather_weights(jnp.concatenate([w_query, w_key, w_value, w_out], axis=1))
    full_qkv = packed_attn[:, : cuts[2]]
    full_out = packed_attn[:, cuts[2] :]

    def spread_out(weight):
        grouped = weight.reshape(clusters, holders, weight.shape[1], half_ff)
        return jnp.broadcast_to(grouped[None], (replicas,) + grouped.shape).reshape(
            dp_count, holders, weight.shape[1], half_ff
        )

    def fetch(weight):
        moved = lax.all_to_all(spread_out(weight), "dp", split_axis=0, concat_axis=2, tiled=True)
        return moved.reshape(holders, model_width, half_ff)

    local_gate, local_up, local_down = fetch(w_gate), fetch(w_up), fetch(w_down)
    tokens_f32 = tokens.astype(jnp.float32)
    out_f32 = out_grad.astype(jnp.float32)
    position, allowed = seq_layout(lengths[0], row_count)
    cosine, sine_table = rope_tables(position, HEAD_DIM)
    unit_first, scale_first, normed_first = norm_forward(tokens_f32, attn_gain)
    both = spread_rows(
        jnp.concatenate(
            [normed_first, (residual_scale * out_f32).astype(jnp.bfloat16)], axis=1
        )
    )
    wide_first = both[:, :model_width]
    tagged = jnp.concatenate(
        [
            both[:, model_width:],
            jnp.pad(routes.astype(jnp.bfloat16), ((0, 0), (0, 128 - TOPK))),
        ],
        axis=1,
    )
    tagged_all = gather_dp(tagged, groups)
    moe_all = tagged_all[:, :model_width]
    routes_all = tagged_all[:, model_width : model_width + TOPK].astype(jnp.int32)
    qkv = jnp.dot(wide_first, full_qkv, preferred_element_type=jnp.float32)
    query_heads = rotate(
        qkv[:, : cuts[0]].reshape(row_count, heads_here, HEAD_DIM), cosine, sine_table
    ).astype(jnp.bfloat16)
    key_heads = rotate(
        qkv[:, cuts[0] : cuts[1]].reshape(row_count, kv_here, HEAD_DIM), cosine, sine_table
    ).astype(jnp.bfloat16)
    value_heads = qkv[:, cuts[1] :].astype(jnp.bfloat16).reshape(row_count, kv_here, HEAD_DIM)
    mixed_out, log_total = attend(query_heads, key_heads, value_heads, allowed)
    hidden = tokens_f32 + residual_scale * narrow(dot_f32(mixed_out, full_out, ((1,), (1,))))
    unit_second, scale_second, normed_second = norm_forward(hidden, ffn_gain)
    rows_all = gather_dp(spread_rows(normed_second), groups)

    expert_ids = jnp.arange(EXPERTS, dtype=jnp.int32)

    def gate_of(rows_bf, row_routes):
        picked = row_routes[:, :, None] == expert_ids[None, None, :]
        logits = exact_dot(rows_bf, w_router, ((1,), (0,)))
        named = jnp.any(picked, axis=1)
        masked = jnp.where(named, logits, -jnp.inf)
        raised = jnp.exp(masked - jnp.max(masked, axis=1, keepdims=True))
        return picked, named, raised / jnp.sum(raised, axis=1, keepdims=True)

    _, named_all, gates_all = gate_of(rows_all, routes_all)
    first_expert = lax.axis_index("dp") % clusters * holders
    out_part = back_part = gate_slots = 0.0
    grads = []
    for h in range(holders):
        gate = lax.dynamic_slice_in_dim(gates_all, first_expert + h, 1, 1)
        here = lax.dynamic_slice_in_dim(named_all, first_expert + h, 1, 1)
        gate_pre = dot_f32(rows_all, local_gate[h], ((1,), (0,)))
        up_pre = dot_f32(rows_all, local_up[h], ((1,), (0,)))
        sigmoid_gate = jax.nn.sigmoid(gate_pre)
        activated = gate_pre * sigmoid_gate
        inner_act = (activated * up_pre).astype(jnp.bfloat16)
        produced = dot_f32(inner_act, local_down[h], ((1,), (1,))).astype(jnp.bfloat16)
        produced = produced.astype(jnp.float32)
        out_part = out_part + jnp.where(here, gate * produced, 0.0)
        moe_f32 = moe_all.astype(jnp.float32)
        gate_part = jnp.sum(moe_f32 * produced, axis=1, keepdims=True)
        gate_slots = gate_slots + jnp.where(routes_all == first_expert + h, gate_part, 0.0)
        route_grad = jnp.where(here, gate * moe_f32, 0.0).astype(jnp.bfloat16)
        inner_grad = dot_f32(route_grad, local_down[h], ((1,), (0,)))
        gate_pre_grad = (
            inner_grad * up_pre * sigmoid_gate * (1.0 + gate_pre * (1.0 - sigmoid_gate))
        ).astype(jnp.bfloat16)
        up_pre_grad = (inner_grad * activated).astype(jnp.bfloat16)
        back = dot_f32(gate_pre_grad, local_gate[h], ((1,), (1,))) + dot_f32(
            up_pre_grad, local_up[h], ((1,), (1,))
        )
        back_part = back_part + back.astype(jnp.bfloat16).astype(jnp.float32)
        grads.append(
            (
                dot_f32(rows_all, gate_pre_grad, ((0,), (0,))).astype(jnp.bfloat16),
                dot_f32(rows_all, up_pre_grad, ((0,), (0,))).astype(jnp.bfloat16),
                dot_f32(route_grad, inner_act, ((0,), (0,))).astype(jnp.bfloat16),
            )
        )
    slot_parts = split_three(gate_slots)
    pad = jnp.zeros((rows_all.shape[0], 128 - 3 * TOPK), jnp.bfloat16)
    home = scatter_dp(
        jnp.concatenate(
            [back_part.astype(jnp.bfloat16)] + slot_parts + [pad, out_part.astype(jnp.bfloat16)],
            axis=1,
        ),
        groups,
    ).astype(jnp.float32)
    back_home = home[:, : model_width + 128]
    out_home = home[:, model_width + 128 :]
    slots = back_home[:, model_width:]
    gate_half = slots[:, :TOPK] + slots[:, TOPK : 2 * TOPK] + slots[:, 2 * TOPK : 3 * TOPK]
    own_back = narrow(
        jnp.concatenate(
            [back_home[:, :model_width], jnp.pad(gate_half, ((0, 0), (0, 128 - TOPK)))], axis=1
        )
    )
    expert_back = own_back[:, :model_width]
    gate_grad = own_back[:, model_width : model_width + TOPK]
    block_rows = (hidden + residual_scale * narrow(out_home)).astype(jnp.bfloat16)

    def send_home(index):
        stacked = jnp.stack([grads[h][index] for h in range(holders)])
        moved = lax.all_to_all(stacked[None], "dp", split_axis=2, concat_axis=0, tiled=True)
        return jnp.sum(
            moved.astype(jnp.float32).reshape(
                replicas, clusters * holders, moved.shape[2], half_ff
            ),
            axis=0,
        )

    own_routes = lax.dynamic_slice_in_dim(routes, own_row, local_rows, 0)
    picked_own, _, gates_dense = gate_of(normed_second, own_routes)
    gates_own = jnp.sum(jnp.where(picked_own, gates_dense[:, None, :], 0.0), axis=2)
    chosen_grad = gates_own * (gate_grad - jnp.sum(gates_own * gate_grad, axis=1, keepdims=True))
    logits_grad = jnp.sum(jnp.where(picked_own, chosen_grad[:, :, None], 0.0), axis=1)
    second_grad = expert_back + jnp.dot(logits_grad, w_router.T, precision=lax.Precision.HIGHEST)
    hidden_back, ffn_gain_grad = norm_backward(second_grad, unit_second, scale_second, ffn_gain)
    hidden_grad = out_f32 + hidden_back
    attn_grad = spread_rows((residual_scale * hidden_grad).astype(jnp.bfloat16))
    mixed_grad = jnp.dot(attn_grad, full_out, preferred_element_type=jnp.float32).astype(
        jnp.bfloat16
    )
    out_w_grad = dot_f32(attn_grad, mixed_out, ((0,), (0,)))
    dquery, key_grad, dvalues = attend_back(
        query_heads, key_heads, value_heads, allowed, log_total, mixed_grad
    )
    query_grad = (
        unrotate(dquery, cosine, sine_table)
        .astype(jnp.bfloat16)
        .reshape(row_count, heads_here * HEAD_DIM)
    )
    keys_grad = (
        unrotate(key_grad, cosine, sine_table)
        .astype(jnp.bfloat16)
        .reshape(row_count, kv_here * HEAD_DIM)
    )
    value_grad = dvalues.astype(jnp.bfloat16).reshape(row_count, kv_here * HEAD_DIM)
    qkv_grad = jnp.concatenate([query_grad, keys_grad, value_grad], axis=1)
    qkv_w_grad = dot_f32(wide_first, qkv_grad, ((0,), (0,)))
    packed_grad = scatter_weights(
        jnp.concatenate([qkv_w_grad, out_w_grad], axis=1).astype(jnp.bfloat16)
    ).astype(jnp.float32)
    first_grad = narrow(dot_f32(qkv_grad, full_qkv, ((1,), (1,))))
    tokens_back, attn_gain_grad = norm_backward(first_grad, unit_first, scale_first, attn_gain)
    tokens_grad = hidden_grad + tokens_back
    attn_gain_total, ffn_gain_total, router_total = lax.psum(
        (
            attn_gain_grad,
            ffn_gain_grad,
            exact_dot(normed_second, logits_grad, ((0,), (0,))),
        ),
        ("dp", "tensor"),
    )
    return (
        block_rows,
        tokens_grad,
        attn_gain_total,
        packed_grad[:, : cuts[0]],
        packed_grad[:, cuts[0] : cuts[1]],
        packed_grad[:, cuts[1] : cuts[2]],
        packed_grad[:, cuts[2] :],
        ffn_gain_total,
        router_total,
        send_home(0),
        send_home(1),
        send_home(2),
    )


def solution(mesh):
    placed = (
        P(("dp", "tensor"), None),
        P(("dp", "tensor"), None),
        P("dp", None),
        P("dp", None),
        P(),
        P("dp", "tensor"),
        P("dp", "tensor"),
        P("dp", "tensor"),
        P("dp", "tensor"),
        P(),
        P(),
        P(None, "dp", "tensor"),
        P(None, "dp", "tensor"),
        P(None, "dp", "tensor"),
    )
    near = mesh.shape["dp"] == 16 and mesh.shape["tensor"] == 2
    return jax.shard_map(
        local_near if near else local_far,
        mesh=mesh,
        in_specs=placed,
        out_specs=(
            P(("dp", "tensor"), None),
            P(("dp", "tensor"), None),
            P(),
            P("dp", "tensor"),
            P("dp", "tensor"),
            P("dp", "tensor"),
            P("dp", "tensor"),
            P(),
            P(),
            P(None, "dp", "tensor"),
            P(None, "dp", "tensor"),
            P(None, "dp", "tensor"),
        ),
        check_vma=False,
    )
```

```python
import functools

import jax
import jax.numpy as jnp
from jax import lax
from jax.experimental import pallas as pl
from jax.experimental.pallas import tpu as pltpu
from jax.sharding import PartitionSpec as P

EXPERTS = 32
TOPK = 8
HEAD_DIM = 64


eps_norm = 1e-06
residual_scale = 0.22
score_scale = 0.015625
rope_base = 10000.0
masked_score = -1e30


def norm_forward(row_block, gain_vec):
    rscale = lax.rsqrt(jnp.mean(row_block * row_block, axis=1, keepdims=True) + eps_norm)
    unit_rows = row_block * rscale
    return (unit_rows, rscale, (unit_rows * gain_vec).astype(jnp.bfloat16))


def norm_backward(gradient, unit_rows, rscale, gain_vec):
    unit_grad = gradient * gain_vec
    back_rows = rscale * (
        unit_grad - unit_rows * jnp.mean(unit_grad * unit_rows, axis=1, keepdims=True)
    )
    return (back_rows, jnp.sum(gradient * unit_rows, axis=0))


def seq_layout(seq_lengths, row_count):
    order = jnp.arange(seq_lengths.shape[0], dtype=jnp.int32)
    seq_ends = jnp.sum(jnp.where(order[:, None] <= order[None, :], seq_lengths[:, None], 0), axis=0)
    starts = seq_ends - seq_lengths
    places = jnp.arange(row_count, dtype=jnp.int32)
    segment = jnp.sum((places[:, None] >= seq_ends[None, :]).astype(jnp.int32), axis=1)
    member = segment[:, None] == jnp.arange(seq_lengths.shape[0], dtype=jnp.int32)[None, :]
    offset = jnp.sum(jnp.where(member, starts[None, :], 0), axis=1)
    allowed = (segment[:, None] == segment[None, :]) & (places[None, :] <= places[:, None])
    return (places - offset, allowed)


def rope_tables(position, head_width):
    frequency = rope_base ** (-(jnp.arange(head_width // 2, dtype=jnp.float32) * 2.0) / head_width)
    angles = position.astype(jnp.float32)[:, None] * frequency[None, :]
    cosine = jnp.concatenate([jnp.cos(angles), jnp.cos(angles)], axis=1)[:, None, :]
    sine_table = jnp.concatenate([jnp.sin(angles), jnp.sin(angles)], axis=1)[:, None, :]
    return (cosine, sine_table)


def rotate(vectors, cosine, sine_table):
    half_width = vectors.shape[-1] // 2
    first_half = vectors[..., :half_width]
    second_half = vectors[..., half_width:]
    return vectors * cosine + jnp.concatenate([-second_half, first_half], axis=-1) * sine_table


def unrotate(gradient, cosine, sine_table):
    half_width = gradient.shape[-1] // 2
    first_half = gradient[..., :half_width]
    second_half = gradient[..., half_width:]
    return gradient * cosine + jnp.concatenate([second_half, -first_half], axis=-1) * sine_table


def score_block(query_heads, key_heads, allowed):
    row_count, head_count, head_width = query_heads.shape
    kv_count = key_heads.shape[1]
    grouped = query_heads.reshape(row_count, kv_count, head_count // kv_count, head_width)
    scores = (
        jnp.einsum("igrd,jgd->grij", grouped, key_heads, preferred_element_type=jnp.float32)
        * score_scale
    )
    return (grouped, jnp.where(allowed[None, None], scores, masked_score))


def attend(query_heads, key_heads, value_heads, allowed):
    row_count, head_count, head_width = query_heads.shape
    grouped, scores = score_block(query_heads, key_heads, allowed)
    row_max = jnp.max(scores, axis=-1, keepdims=True)
    log_total = row_max + jnp.log(jnp.sum(jnp.exp(scores - row_max), axis=-1, keepdims=True))
    prob_bf = jnp.exp(scores - log_total).astype(jnp.bfloat16)
    mixed_out = jnp.einsum(
        "grij,jgd->igrd", prob_bf, value_heads, preferred_element_type=jnp.float32
    )
    return (mixed_out.reshape(row_count, head_count * head_width).astype(jnp.bfloat16), log_total)


def attend_back(query_heads, key_heads, value_heads, allowed, log_total, mixed_grad):
    row_count, head_count, head_width = query_heads.shape
    kv_count = key_heads.shape[1]
    grouped, scores = score_block(query_heads, key_heads, allowed)
    prob_full = jnp.exp(scores - log_total)
    grad_heads = mixed_grad.reshape(row_count, kv_count, head_count // kv_count, head_width)
    dprobs = jnp.einsum(
        "igrd,jgd->grij", grad_heads, value_heads, preferred_element_type=jnp.float32
    )
    row_delta = jnp.sum(prob_full * dprobs, axis=-1, keepdims=True)
    dscores = (prob_full * (dprobs - row_delta)).astype(jnp.bfloat16)
    dquery = (
        jnp.einsum("grij,jgd->igrd", dscores, key_heads, preferred_element_type=jnp.float32)
        * score_scale
    )
    key_grad = (
        jnp.einsum("grij,igrd->jgd", dscores, grouped, preferred_element_type=jnp.float32)
        * score_scale
    )
    dvalues = jnp.einsum(
        "grij,igrd->jgd",
        prob_full.astype(jnp.bfloat16),
        grad_heads,
        preferred_element_type=jnp.float32,
    )
    return (dquery.reshape(row_count, head_count, head_width), key_grad, dvalues)


def spread_rows(row_block):
    return lax.all_gather(row_block, "tensor", axis=0, tiled=True)


def narrow(partial_rows):
    if lax.axis_size("tensor") != 2:
        return lax.psum_scatter(partial_rows, "tensor", scatter_dimension=0, tiled=True)
    half = partial_rows.shape[0] // 2
    mine = lax.axis_index("tensor")
    away = lax.dynamic_slice_in_dim(partial_rows, (1 - mine) * half, half, 0)
    kept = lax.dynamic_slice_in_dim(partial_rows, mine * half, half, 0)
    return kept + lax.ppermute(away, "tensor", [(0, 1), (1, 0)])


def split_three(values):
    high = lax.reduce_precision(values, 8, 7)
    rest = values - high
    middle = lax.reduce_precision(rest, 8, 7)
    return [part.astype(jnp.bfloat16) for part in (high, middle, rest - middle)]


def dot_f32(left, right, dims):
    return lax.dot_general(left, right, (dims, ((), ())), preferred_element_type=jnp.float32)


def exact_dot(rows_bf, values, dims):
    width = values.shape[1]
    product = dot_f32(rows_bf, jnp.concatenate(split_three(values), axis=1), dims)
    return product[:, :width] + (product[:, width : 2 * width] + product[:, 2 * width :])


def gather_dp(rows, groups):
    return lax.all_gather(rows, "dp", axis=0, tiled=True, axis_index_groups=groups)


def scatter_dp(rows, groups):
    return lax.psum_scatter(
        rows, "dp", scatter_dimension=0, tiled=True, axis_index_groups=groups
    )


def gather_weights(packed):
    return lax.all_gather(packed, "dp", axis=0, tiled=True)


def scatter_weights(packed):
    return lax.psum_scatter(packed, "dp", scatter_dimension=0, tiled=True)


MESH = pl.DeviceIdType.MESH
WEIGHT = {"core": 1, "x": 2, "z0": 4, "z1": 8}
DIMS = ("z1", "z0", "x", "t")
ORDERS = (("x", "t", "z0", "z1"), ("t", "z0", "x", "z1"), ("z0", "x", "z1", "t"))


def bit_of(me, weight):
    return lax.rem(lax.div(me, weight), 2)


def partner(name):
    me, side = lax.axis_index("dp"), lax.axis_index("tensor")
    if name == "t":
        return (me, 1 - side)
    return (me + WEIGHT[name] * (1 - 2 * bit_of(me, WEIGHT[name])), side)


def greet_plane(count, others=()):
    me, side = lax.axis_index("dp"), lax.axis_index("tensor")
    barrier = pltpu.get_barrier_semaphore()

    def greet(k, carry):
        pl.semaphore_signal(
            barrier, inc=1, device_id=(lax.rem(me + k, count), side), device_id_type=MESH
        )
        return carry

    lax.fori_loop(1, count, greet, 0)
    for place in others:
        pl.semaphore_signal(barrier, inc=1, device_id=place, device_id_type=MESH)
    pl.semaphore_wait(barrier, count - 1 + len(others))


def far_first(i, count):
    return count // 2 + (1 - 2 * lax.rem(i, 2)) * lax.div(i + 1, 2)


class Fetch:
    def __init__(self, count, which, ins, outs, send_sem, recv_sem, own_sem):
        self.count, self.which = count, which
        self.ins, self.outs = ins, outs
        self.sems = (send_sem, recv_sem, own_sem)
        self.holders, self.rows = ins[0].shape[0] // count, ins[0].shape[1]
        self.issued = 0

    def ends(self, w, peer, owner):
        at = pl.ds(pl.multiple_of(owner * self.rows, self.rows), self.rows)
        return self.ins[w].at[peer * self.holders + self.which], self.outs[w].at[at]

    def copy(self, w, k, owner):
        me, side = lax.axis_index("dp"), lax.axis_index("tensor")
        peer = lax.rem(me + k, self.count)
        src, dst = self.ends(w, peer, owner)
        return pltpu.make_async_remote_copy(
            src_ref=src,
            dst_ref=dst,
            send_sem=self.sems[0].at[w, k],
            recv_sem=self.sems[1].at[w, k],
            device_id=(peer, side),
            device_id_type=MESH,
        )

    def own(self, w):
        me = lax.axis_index("dp")
        return pltpu.make_async_copy(*self.ends(w, me, me), self.sems[2].at[w])

    def start(self):
        def step(i, carry):
            for w in range(3):
                self.copy(w, far_first(i, self.count), lax.axis_index("dp")).start()
            return carry

        lax.fori_loop(0, self.count - 1, step, 0)
        for w in range(3):
            self.own(w).start()

    def some(self, amount):
        for _ in range(amount):
            if self.issued < 3 * (self.count - 1):
                i, w = divmod(self.issued, 3)
                k = self.count // 2 + (1 - 2 * (i % 2)) * ((i + 1) // 2)
                self.copy(w, k, lax.axis_index("dp")).start()
                self.issued += 1

    def rest(self):
        self.some(3 * self.count)
        for w in range(3):
            self.own(w).start()

    def finish(self):
        me = lax.axis_index("dp")

        def step(i, carry):
            k = far_first(i, self.count)
            for w in range(3):
                self.copy(w, k, me).wait_send()
                self.copy(w, k, lax.rem(me - k + self.count, self.count)).wait_recv()
            return carry

        lax.fori_loop(0, self.count - 1, step, 0)
        for w in range(3):
            self.own(w).wait()

    @staticmethod
    def semaphores(count):
        return [
            pltpu.SemaphoreType.DMA((3, count)),
            pltpu.SemaphoreType.DMA((3, count)),
            pltpu.SemaphoreType.DMA((3,)),
        ]


class Sum:
    def __init__(
        self,
        pieces,
        ins,
        outs,
        accs,
        bufs,
        send_sem,
        recv_sem,
        firsts=None,
        first_s=None,
        first_r=None,
    ):
        me, side = lax.axis_index("dp"), lax.axis_index("tensor")
        self.pieces, self.ins, self.outs, self.accs, self.bufs = pieces, ins, outs, accs, bufs
        self.send_sem, self.recv_sem = send_sem, recv_sem
        self.firsts, self.first_s, self.first_r = firsts, first_s, first_r
        self.core = bit_of(me, 1)
        self.whole = "t" in pieces[0][3]
        self.last = len(pieces[0][3])
        self.mine = {
            "z1": bit_of(me, 8),
            "z0": bit_of(me, 4),
            "x": bit_of(me, 2),
            "t": side if self.whole else 0,
        }

    def buf(self, i, s):
        if self.firsts is not None:
            return self.bufs[i * self.last + s - 1] if s else None
        return self.bufs[i * (self.last + 1) + s]

    def first_copy(self, which, z):
        z1, z0 = (z // 2, z % 2) if isinstance(z, int) else (lax.div(z, 2), lax.rem(z, 2))
        return pltpu.make_async_remote_copy(
            src_ref=self.ins[which].at[z1, z0, :, 1 - self.core],
            dst_ref=self.firsts[which].at[z1, z0],
            send_sem=self.first_s.at[which, z],
            recv_sem=self.first_r.at[which, z],
            device_id=partner("core"),
            device_id_type=MESH,
        )

    def send_first(self, which, z):
        self.first_copy(which, z).start()

    def exchange(self, i, s):
        which, first, width, order = self.pieces[i]
        columns = pl.ds(first, width)
        if s == 0:
            src = self.ins[which].at[:, :, :, 1 - self.core, :, :, columns]
            place = partner("core")
        else:
            done, now = order[: s - 1], order[s - 1]
            index = []
            for d in DIMS:
                if d in done:
                    index.append(pl.ds(self.mine[d], 1))
                elif d == now:
                    index.append(pl.ds(1 - self.mine[d], 1))
                else:
                    index.append(slice(None))
            src = self.accs[which].at[tuple(index) + (slice(None), columns)]
            place = partner(now)
        return pltpu.make_async_remote_copy(
            src_ref=src,
            dst_ref=self.buf(i, s),
            send_sem=self.send_sem.at[i, s],
            recv_sem=self.recv_sem.at[i, s],
            device_id=place,
            device_id_type=MESH,
        )

    def add(self, i, s):
        which, first, width, order = self.pieces[i]
        buf = self.buf(i, s)
        columns = pl.ds(first, width)
        if s == self.last:
            at = tuple(self.mine[d] for d in DIMS) + (slice(None), columns)
            self.outs[which][:, columns] = self.accs[which][at].astype(jnp.float32) + buf[
                0, 0, 0, 0
            ].astype(jnp.float32)
            return
        free = [d for d in DIMS if d in order[s:]]

        def step(b, carry):
            at, frm = dict(self.mine), {d: 0 for d in DIMS}
            left = b
            for d in reversed(free):
                at[d] = frm[d] = lax.rem(left, 2)
                left = lax.div(left, 2)
            at = tuple(at[d] for d in DIMS)
            if s == 0:
                have = self.ins[which][at[:3] + (self.core, at[3], slice(None), columns)]
            else:
                have = self.accs[which][at + (slice(None), columns)]
            frm = tuple(frm[d] for d in DIMS)
            if s == 0 and self.firsts is not None:
                got = self.firsts[which][frm + (slice(None), columns)]
            else:
                got = buf[frm]
            self.accs[which][at + (slice(None), columns)] = (
                have.astype(jnp.float32) + got.astype(jnp.float32)
            ).astype(jnp.bfloat16)
            return carry

        lax.fori_loop(0, 2 ** len(free), step, 0)

    def start(self):
        for i in range(len(self.pieces)):
            self.exchange(i, 0).start()

    def run(self, between=lambda: None):
        n = len(self.pieces)
        early = self.firsts is not None
        if early:
            for which in range(len(self.ins)):
                for z in range(4):
                    self.first_copy(which, z).wait_recv()
        for s in range(self.last + 1):
            for i in range(n):
                if s or not early:
                    self.exchange(i, s).wait_recv()
                self.add(i, s)
                if s < self.last:
                    self.exchange(i, s + 1).start()
                between()
        if early:
            for which in range(len(self.ins)):
                for z in range(4):
                    self.first_copy(which, z).wait_send()
        for s in range(int(early), self.last + 1):
            for i in range(n):
                self.exchange(i, s).wait_send()

    @staticmethod
    def scratch(pieces, rows, widths, begin=0):
        whole = 2 if "t" in pieces[0][3] else 1
        stages = len(pieces[0][3]) + 1
        bufs = []
        for _, _, width, order in pieces:
            for s in range(begin, stages):
                free = tuple(2 if d in order[s:] else 1 for d in DIMS)
                bufs.append(pltpu.VMEM(free + (rows, width), jnp.bfloat16))
        accs = [pltpu.VMEM((2, 2, 2, whole, rows, w), jnp.bfloat16) for w in widths]
        sems = [pltpu.SemaphoreType.DMA((len(pieces), stages))] * 2
        return accs, bufs, sems

    @staticmethod
    def view(array, whole):
        blocks = 32 if whole else 16
        return array.reshape(
            2, 2, 2, 2, 2 if whole else 1, array.shape[0] // blocks, array.shape[1]
        )


def home_pieces(wide, thin):
    cut = wide * 3 // 4
    return (
        (0, 0, cut, ORDERS[0]),
        (2, 0, cut, ORDERS[1]),
        (0, cut, wide - cut, ORDERS[2]),
        (2, cut, wide - cut, ORDERS[2]),
        (1, 0, thin, ORDERS[2]),
    )


def last_pieces(width):
    cut = width // 2
    return ((0, 0, cut, ("x", "z0", "z1")), (0, cut, width - cut, ("z0", "x", "z1")))


class Gather:
    def __init__(self, src, out, sides, sems):
        me, side = lax.axis_index("dp"), lax.axis_index("tensor")
        self.src, self.out, self.sides, self.sems = src, out, sides, sems
        self.rows = src.shape[0]
        self.me, self.t = me, side
        self.z, self.x, self.core = lax.div(me, 4), bit_of(me, 2), bit_of(me, 1)

    def at(self, z, x, t, core):
        place = z * 4 + x * 2 + core
        if self.sides:
            place = place * 2 + t
        return self.out.at[pl.ds(pl.multiple_of(place * self.rows, self.rows), self.rows)]

    def copy(self, pair, index, src, dst, device):
        return pltpu.make_async_remote_copy(
            src_ref=src,
            dst_ref=dst,
            send_sem=self.sems[pair].at[index],
            recv_sem=self.sems[pair + 1].at[index],
            device_id=device,
            device_id_type=MESH,
        )

    def line(self, up, z, src=None):
        block = self.at(z, self.x, self.t, self.core)
        step = 4 if up else -4
        device = (lax.rem(self.me + step + 16, 16), self.t)
        return self.copy(0, (int(up), z), block if src is None else src, block, device)

    def over_x(self, diag, z, x, t, src=None):
        block = self.at(z, x, t, self.core)
        return self.copy(
            2, (int(diag), z), block if src is None else src, block, partner("x")
        )

    def over_t(self, diag, z, x, t, src=None):
        block = self.at(z, x, t, self.core)
        return self.copy(
            4, (int(diag), z), block if src is None else src, block, partner("t")
        )

    def over_core(self, z, x, t, core, src=None):
        block = self.at(z, x, t, core)
        return self.copy(6, (t, x, z), block if src is None else src, block, partner("core"))

    def own(self):
        return pltpu.make_async_copy(
            self.src, self.at(self.z, self.x, self.t, self.core), self.sems[8]
        )

    def sideways(self, z, src=None):
        self.over_x(False, z, self.x, self.t, src).start()
        if self.sides:
            self.over_t(False, z, self.x, self.t, src).start()
        self.over_core(z, self.x, self.t, self.core, src).start()

    def start(self):
        @pl.when(self.z < 3)
        def _():
            self.line(True, self.z, self.src).start()

        @pl.when(self.z > 0)
        def _():
            self.line(False, self.z, self.src).start()

        self.sideways(self.z, self.src)
        self.own().start()

    def pass_line(self, s):
        @pl.when(self.z >= s)
        def _():
            z = self.z - s
            self.line(True, z).wait_recv()

            @pl.when(self.z < 3)
            def _():
                self.line(True, z).start()

            self.sideways(z)

        @pl.when(self.z + s <= 3)
        def _():
            z = self.z + s
            self.line(False, z).wait_recv()

            @pl.when(self.z > 0)
            def _():
                self.line(False, z).start()

            self.sideways(z)

    def second(self, z):
        x, t = self.x, self.t
        self.over_x(False, z, 1 - x, t).wait_recv()
        if self.sides:

            @pl.when(z >= 2)
            def _():
                self.over_t(True, z, 1 - x, t).start()

        self.over_core(z, 1 - x, t, self.core).start()
        if self.sides:
            self.over_t(False, z, x, 1 - t).wait_recv()

            @pl.when(z < 2)
            def _():
                self.over_x(True, z, x, 1 - t).start()

            self.over_core(z, x, 1 - t, self.core).start()

    def pass_second(self, s):
        @pl.when(self.z >= s)
        def _():
            self.second(self.z - s)

        if s:

            @pl.when(self.z + s <= 3)
            def _():
                self.second(self.z + s)

    def third(self, z):
        block = (z, 1 - self.x, 1 - self.t)
        (self.over_x if z < 2 else self.over_t)(True, *block).wait_recv()
        self.over_core(*block, self.core).start()

    def steps(self):
        line, second = self.pass_line, self.pass_second
        order = (line, 1), (second, 0), (line, 2), (second, 1), (line, 3), (second, 2), (second, 3)
        steps = [functools.partial(*each) for each in order]
        if self.sides:
            steps += [functools.partial(self.third, z) for z in range(4)]
        return steps + [self.arrived]

    def arrived(self):
        for z in range(4):
            for x in range(2):
                for t in range(2) if self.sides else [self.t]:
                    self.over_core(z, x, t, 1 - self.core).wait_recv()
        self.own().wait()

    def finish(self):
        x, t = self.x, self.t
        for z in range(4):

            @pl.when((z <= self.z) & (self.z < 3))
            def _():
                self.line(True, z).wait_send()

            @pl.when((z >= self.z) & (self.z > 0))
            def _():
                self.line(False, z).wait_send()

            self.over_x(False, z, x, t).wait_send()
            if self.sides:
                self.over_t(False, z, x, t).wait_send()
                if z < 2:
                    self.over_x(True, z, x, 1 - t).wait_send()
                else:
                    self.over_t(True, z, 1 - x, t).wait_send()
            for xb in range(2):
                for tb in range(2) if self.sides else [t]:
                    self.over_core(z, xb, tb, self.core).wait_send()

    @staticmethod
    def semaphores():
        dma = pltpu.SemaphoreType.DMA
        return [dma((2, 4))] * 6 + [dma((2, 2, 4))] * 2 + [dma]


def lanes_of(shape):
    return lax.broadcasted_iota(jnp.int32, shape, 1)


def turn(values, cosine, sine_table, back):
    width = values.shape[1]
    low = lax.rem(lanes_of(values.shape), HEAD_DIM) < HEAD_DIM // 2
    later = pltpu.roll(values, width - HEAD_DIM // 2, 1)
    earlier = pltpu.roll(values, HEAD_DIM // 2, 1)
    moved = jnp.where(low, later, -earlier) if back else jnp.where(low, -later, earlier)
    return values * cosine + moved * sine_table


def twice(pair, second):
    wide = pair.astype(jnp.float32)
    other = pltpu.roll(wide, HEAD_DIM, 1)
    low = lanes_of(wide.shape) < HEAD_DIM
    both = jnp.where(low, other, wide) if second else jnp.where(low, wide, other)
    return both.astype(jnp.bfloat16)


def stack_heads(pair):
    wide = pair.astype(jnp.float32)
    low = lanes_of(wide.shape) < HEAD_DIM
    return jnp.concatenate(
        [jnp.where(low, wide, 0.0), jnp.where(low, 0.0, wide)], axis=0
    ).astype(jnp.bfloat16)


def unstack_heads(stacked):
    rows = stacked.shape[0] // 2
    low = lanes_of((rows, stacked.shape[1])) < HEAD_DIM
    return jnp.where(low, stacked[:rows], stacked[rows:])


def probabilities(query, keys, mask):
    scores = dot_f32(query, keys, ((1,), (1,))) * score_scale
    scores = jnp.where(jnp.concatenate([mask, mask], axis=0) > 0.0, scores, masked_score)
    row_max = jnp.max(scores, axis=1, keepdims=True)
    log_total = row_max + jnp.log(jnp.sum(jnp.exp(scores - row_max), axis=1, keepdims=True))
    return jnp.exp(scores - log_total)


def chunk(ref, i, width):
    return ref[:, i * width : (i + 1) * width]


PLAN = (2, 2, 2, 2, 2)


def front_kernel(count, *refs):
    attn_ref, gate_ref, up_ref, down_ref, first_ref, tokens_ref = refs[:6]
    cos_ref, sin_ref, mask_ref, gain_ref = refs[6:10]
    gate_o, up_o, down_o, rows_o, attn_o, wide_o = refs[10:16]
    q_o, k_o, v_o, mixed_o, hidden_o, normed_o = refs[16:22]
    part, got, pair_sem = refs[22:25]
    swap = Fetch(count, 0, [gate_ref, up_ref, down_ref], [gate_o, up_o, down_o], *refs[25:28])
    attn = Gather(attn_ref, attn_o, False, refs[28:37])
    rows_job = Gather(normed_o, rows_o, True, refs[37:46])
    side = lax.axis_index("tensor")
    rows = first_ref.shape[0]

    def half(which):
        return pl.ds(pl.multiple_of(which * rows, rows), rows)

    spread = pltpu.make_async_remote_copy(
        src_ref=first_ref,
        dst_ref=wide_o.at[half(side)],
        send_sem=pair_sem.at[0, 0],
        recv_sem=pair_sem.at[0, 1],
        device_id=partner("t"),
        device_id_type=MESH,
    )
    narrowed = pltpu.make_async_remote_copy(
        src_ref=part.at[half(1 - side)],
        dst_ref=got,
        send_sem=pair_sem.at[1, 0],
        recv_sem=pair_sem.at[1, 1],
        device_id=partner("t"),
        device_id_type=MESH,
    )
    greet_plane(count, [partner("t")])
    attn.start()
    spread.start()
    wide_o[half(side), :] = first_ref[...]
    swap.some(PLAN[0])
    for each in attn.steps():
        each()
        swap.some(PLAN[1])
    spread.wait()
    swap.some(PLAN[2])
    q_cols, k_cols = q_o.shape[1], k_o.shape[1]
    step = 256
    for i in range((q_cols + 2 * k_cols) // step):
        at = i * step
        made = dot_f32(wide_o[...], chunk(attn_o, i, step), ((1,), (0,)))
        if at < q_cols + k_cols:
            made = turn(made, cos_ref[...], sin_ref[...], False)
        made = made.astype(jnp.bfloat16)
        if at < q_cols:
            q_o[:, at : at + step] = made
        elif at < q_cols + k_cols:
            k_o[:, at - q_cols : at - q_cols + step] = made
        else:
            v_o[:, at - q_cols - k_cols : at - q_cols - k_cols + step] = made
        swap.some(PLAN[2])
    pair_width = 2 * HEAD_DIM
    for g in range(q_cols // pair_width):
        query = stack_heads(chunk(q_o, g, pair_width))
        keys = twice(chunk(k_o, g // 2, pair_width), g % 2)
        values = twice(chunk(v_o, g // 2, pair_width), g % 2)
        probs = probabilities(query, keys, mask_ref[...]).astype(jnp.bfloat16)
        mixed = unstack_heads(dot_f32(probs, values, ((1,), (0,))))
        mixed_o[:, g * pair_width : (g + 1) * pair_width] = mixed.astype(jnp.bfloat16)
        swap.some(PLAN[2])
    base = q_cols + 2 * k_cols
    for i in range(attn_o.shape[0] // step):
        part[:, i * step : (i + 1) * step] = dot_f32(
            mixed_o[...], attn_o[i * step : (i + 1) * step, base:], ((1,), (1,))
        )
    narrowed.start()
    swap.some(PLAN[3])
    narrowed.wait()
    hidden = tokens_ref[...].astype(jnp.float32) + residual_scale * (
        part[half(side), :] + got[...]
    )
    hidden_o[...] = hidden
    rscale = lax.rsqrt(jnp.mean(hidden * hidden, axis=1, keepdims=True) + eps_norm)
    normed_o[...] = (hidden * rscale * gain_ref[...]).astype(jnp.bfloat16)
    rows_job.start()
    for each in rows_job.steps():
        swap.some(PLAN[4])
        each()
    swap.rest()
    attn.finish()
    rows_job.finish()
    swap.finish()


def front(packed, experts, first, tokens, cosine, sine_table, mask, gain, q_cols, k_cols):
    count = lax.axis_size("dp")
    rows, width = tokens.shape
    total = rows * count * 2
    wide_rows = 2 * rows
    _, expert_rows, half_ff = experts[0].shape
    bf16, f32 = jnp.bfloat16, jnp.float32
    shape = jax.ShapeDtypeStruct
    vmem, anywhere = pl.BlockSpec(memory_space=pltpu.VMEM), pl.BlockSpec(memory_space=pl.ANY)
    return pl.pallas_call(
        functools.partial(front_kernel, count),
        out_shape=[
            shape((expert_rows * count, half_ff), bf16) for _ in range(3)
        ]
        + [
            shape((total, width), bf16),
            shape((packed.shape[0] * count, packed.shape[1]), bf16),
            shape((wide_rows, width), bf16),
            shape((wide_rows, q_cols), bf16),
            shape((wide_rows, k_cols), bf16),
            shape((wide_rows, k_cols), bf16),
            shape((wide_rows, q_cols), bf16),
            shape((rows, width), f32),
            shape((rows, width), bf16),
        ],
        in_specs=[vmem] + [anywhere] * 3 + [vmem] * 6,
        out_specs=[anywhere] * 4 + [vmem] * 8,
        scratch_shapes=[
            pltpu.VMEM((wide_rows, width), f32),
            pltpu.VMEM((rows, width), f32),
            pltpu.SemaphoreType.DMA((2, 2)),
        ]
        + Fetch.semaphores(count)
        + Gather.semaphores() * 2,
        compiler_params=pltpu.CompilerParams(
            collective_id=1, has_side_effects=True, vmem_limit_bytes=40 << 20
        ),
        name="front",
    )(packed, *experts, first, tokens, cosine, sine_table, mask, gain)


def gates_of(rows_bf, routes, router):
    lane = lanes_of(routes.shape).astype(jnp.float32)
    split = dot_f32(rows_bf, router, ((1,), (1,)))
    logits = split + (pltpu.roll(split, 128 - EXPERTS, 1) + pltpu.roll(split, 128 - 2 * EXPERTS, 1))
    named = jnp.zeros(routes.shape, jnp.float32)
    for k in range(TOPK):
        named = jnp.where(routes[:, k : k + 1] == lane, 1.0, named)
    masked = jnp.where(named > 0.0, logits, -jnp.inf)
    raised = jnp.exp(masked - jnp.max(masked, axis=1, keepdims=True))
    return lane, named, raised / jnp.sum(raised, axis=1, keepdims=True)


class GradMoves:
    def __init__(self, count, grads, outs, send_sem, recv_sem, own_sem):
        self.count, self.grads, self.outs = count, grads, outs
        self.send_sem, self.recv_sem, self.own_sem = send_sem, recv_sem, own_sem
        self.holders = grads.shape[1]
        self.rows = grads.shape[2] // count
        self.issued = 0

    def copy(self, h, w, k, owner):
        me, side = lax.axis_index("dp"), lax.axis_index("tensor")
        peer = lax.rem(me + k, self.count)
        return pltpu.make_async_remote_copy(
            src_ref=self.grads.at[w, h, pl.ds(pl.multiple_of(peer * self.rows, self.rows), self.rows)],
            dst_ref=self.outs[w].at[owner * self.holders + h],
            send_sem=self.send_sem.at[h, w, k],
            recv_sem=self.recv_sem.at[h, w, k],
            device_id=(peer, side),
            device_id_type=MESH,
        )

    def own(self, h, w):
        me = lax.axis_index("dp")
        return pltpu.make_async_copy(
            self.grads.at[w, h, pl.ds(pl.multiple_of(me * self.rows, self.rows), self.rows)],
            self.outs[w].at[me * self.holders + h],
            self.own_sem.at[h, w],
        )

    def send(self, h):
        def step(i, carry):
            for w in range(3):
                self.copy(h, w, far_first(i, self.count), lax.axis_index("dp")).start()
            return carry

        lax.fori_loop(0, self.count - 1, step, 0)

    def some(self, h, amount):
        for _ in range(amount):
            if self.issued < self.count - 1:
                i = self.issued
                k = self.count // 2 + (1 - 2 * (i % 2)) * ((i + 1) // 2)
                for w in range(3):
                    self.copy(h, w, k, lax.axis_index("dp")).start()
                self.issued += 1

    def finish(self):
        me = lax.axis_index("dp")
        for h in range(self.holders):

            def step(k, carry):
                for w in range(3):
                    self.copy(h, w, k, me).wait_send()
                    self.copy(h, w, k, lax.rem(me - k + self.count, self.count)).wait_recv()
                return carry

            lax.fori_loop(1, self.count, step, 0)
            for w in range(3):
                self.own(h, w).wait()


def rms(values):
    return lax.rsqrt(jnp.mean(values * values, axis=1, keepdims=True) + eps_norm)


def back_norm(gradient, unit, scale, gain):
    inner = gradient * gain
    rows = scale * (inner - unit * jnp.mean(inner * unit, axis=1, keepdims=True))
    return rows, jnp.sum(gradient * unit, axis=0, keepdims=True)


SPREAD = (0, 1)


def back_kernel(count, sides, home, late, *refs):
    refs = list(refs)

    def take(n):
        taken = refs[:n]
        del refs[:n]
        return taken

    rows_hbm, tag_hbm = take(2)
    held_in, owned_in = take(3), take(3)
    router_ref, router_t = take(2)
    attn_ref, wide_first, q_ref, k_ref, v_ref, mixed_ref, hidden_ref, normed_ref, own_tag = take(9)
    grad_ref, tokens_ref, gain1_ref, gain2_ref, cos_ref, sin_ref, mask_ref = take(7)
    block_o, tokens_o, weights_o, logits_o, gains_o = take(5)
    moved_o = take(3)
    row_buf, tag_buf, load_sem, acc, grads = take(5)
    parts, firsts, home_out = take(3), take(3), take(3)
    sum_bufs = take(len(home) * 4)
    first_s, first_r, sum_s, sum_r = take(4)
    late_in, late_acc = take(2)
    late_bufs = take(len(late) * 4)
    late_s, late_r = take(2)
    moves = GradMoves(count, grads, moved_o, *take(3))
    weights, held_sem = take(3), take(1)[0]
    fetch = Fetch(count, 1, owned_in, [w.at[1] for w in weights], *take(3))
    lg_ref, gain_blk, wide_attn, mixed_grad, qkv_grad, part, got, pair_sem = take(8)
    spread_logits = Gather(lg_ref, logits_o, True, take(9))
    share_s, share_r, share_own = take(3)
    sums = Sum(home, parts, home_out, firsts, sum_bufs, sum_s, sum_r, firsts, first_s, first_r)
    last = Sum(late, [late_in], [weights_o], [late_acc], late_bufs, late_s, late_r)
    dp, side = lax.axis_index("dp"), lax.axis_index("tensor")
    rows = hidden_ref.shape[0]
    width = hidden_ref.shape[1]
    holders = weights[0].shape[0]
    tile = row_buf.shape[1]
    tiles = rows_hbm.shape[0] // tile
    total = count * sides
    me = dp * sides + side

    def place(k):
        peer = lax.rem(me + k, total)
        return (lax.div(peer, sides), lax.rem(peer, sides))

    def load(step):
        at = pl.ds(pl.multiple_of(lax.rem(step, tiles) * tile, tile), tile)
        slot = lax.rem(step, 2)
        return [
            pltpu.make_async_copy(rows_hbm.at[at], row_buf.at[slot], load_sem.at[0, slot]),
            pltpu.make_async_copy(tag_hbm.at[at], tag_buf.at[slot], load_sem.at[1, slot]),
        ]

    held = [pltpu.make_async_copy(held_in[w], weights[w].at[0], held_sem.at[w]) for w in range(3)]
    for each in load(0) + held:
        each.start()
    barrier = pltpu.get_barrier_semaphore()

    def greet(k, carry):
        pl.semaphore_signal(barrier, inc=1, device_id=place(k), device_id_type=MESH)
        return carry

    lax.fori_loop(1, total, greet, 0)
    pl.semaphore_wait(barrier, total - 1)
    fetch.start()
    for each in held:
        each.wait()

    def expert_step(step, carry):
        h, z = lax.div(step, tiles), lax.rem(step, tiles)
        slot = lax.rem(step, 2)

        @pl.when(step + 1 < holders * tiles)
        def _():
            for each in load(step + 1):
                each.start()

        @pl.when(step == tiles)
        def _():
            fetch.finish()

        for each in load(step):
            each.wait()
        rows_bf = row_buf[slot]
        moe = tag_buf[slot, :, :width].astype(jnp.float32)
        routes = tag_buf[slot, :, width:].astype(jnp.float32)
        lane, named, gates = gates_of(rows_bf, routes, router_ref[...])
        at = (lane == (dp * holders + h).astype(jnp.float32)) & (named > 0.0)
        gate = jnp.sum(jnp.where(at, gates, 0.0), axis=1, keepdims=True)
        gate_w, up_w, down_w = (ref[h] for ref in weights)
        gate_pre = dot_f32(rows_bf, gate_w, ((1,), (0,)))
        up_pre = dot_f32(rows_bf, up_w, ((1,), (0,)))
        route_grad = (gate * moe).astype(jnp.bfloat16)
        inner_grad = dot_f32(route_grad, down_w, ((1,), (0,)))
        sigmoid_gate = jax.nn.sigmoid(gate_pre)
        activated = gate_pre * sigmoid_gate
        inner_act = (activated * up_pre).astype(jnp.bfloat16)
        gate_pre_grad = (
            inner_grad * up_pre * sigmoid_gate * (1.0 + gate_pre * (1.0 - sigmoid_gate))
        ).astype(jnp.bfloat16)
        up_pre_grad = (inner_grad * activated).astype(jnp.bfloat16)
        produced = dot_f32(inner_act, down_w, ((1,), (1,))).astype(jnp.bfloat16)
        produced = produced.astype(jnp.float32)
        gate_part = jnp.sum(moe * produced, axis=1, keepdims=True)
        slots = jnp.where(at, gate_part, 0.0)
        high = slots.astype(jnp.bfloat16).astype(jnp.float32)
        rest = slots - high
        middle = rest.astype(jnp.bfloat16).astype(jnp.float32)
        low = (rest - middle).astype(jnp.bfloat16).astype(jnp.float32)
        slots = high + (pltpu.roll(middle, EXPERTS, 1) + pltpu.roll(low, 2 * EXPERTS, 1))
        back = dot_f32(gate_pre_grad, gate_w, ((1,), (1,))) + dot_f32(
            up_pre_grad, up_w, ((1,), (1,))
        )
        made = (
            back.astype(jnp.bfloat16),
            slots.astype(jnp.bfloat16),
            (gate * produced).astype(jnp.bfloat16),
        )
        z1, z0 = lax.div(z, 2), lax.rem(z, 2)
        for which in range(3):
            ref = parts[which].at[z1, z0]
            block = made[which].reshape(2, 2, 2, rows, made[which].shape[1])

            @pl.when(h == 0)
            def _():
                ref[...] = block

            @pl.when(h > 0)
            def _():
                ref[...] = (ref[...].astype(jnp.float32) + block.astype(jnp.float32)).astype(
                    jnp.bfloat16
                )

        for w, (left, right) in enumerate(
            ((rows_bf, gate_pre_grad), (rows_bf, up_pre_grad), (route_grad, inner_act))
        ):
            product = dot_f32(right, left, ((0,), (0,)))

            @pl.when(z == 0)
            def _():
                acc[w] = product

            @pl.when(z > 0)
            def _():
                acc[w] += product

        @pl.when(h == holders - 1)
        def _():
            for which in range(3):
                sums.send_first(which, z)

        @pl.when(z == tiles - 1)
        def _():
            for w in range(3):
                grads[w, h] = acc[w].T.astype(jnp.bfloat16)
                moves.own(h, w).start()

            @pl.when(h < holders - 1)
            def _():
                moves.send(h)

        return carry

    lax.fori_loop(0, holders * tiles, expert_step, 0)
    final = holders - 1
    sums.run(lambda: moves.some(final, SPREAD[0]))

    def half(which):
        return pl.ds(pl.multiple_of(which * rows, rows), rows)

    routes = own_tag[:, width:].astype(jnp.float32)
    _, _, gates = gates_of(normed_ref[...], routes, router_ref[...])
    slots = home_out[1][...]
    gate_grad = slots + (pltpu.roll(slots, 128 - EXPERTS, 1) + pltpu.roll(slots, 128 - 2 * EXPERTS, 1))
    logits_grad = gates * (gate_grad - jnp.sum(gates * gate_grad, axis=1, keepdims=True))
    lg_ref[...] = logits_grad
    second_grad = home_out[0][...] + jnp.dot(
        logits_grad[:, :EXPERTS],
        router_t[...],
        precision=lax.Precision.HIGHEST,
        preferred_element_type=jnp.float32,
    )
    hidden = hidden_ref[...]
    scale_second = rms(hidden)
    hidden_back, ffn_gain_grad = back_norm(
        second_grad, hidden * scale_second, scale_second, gain2_ref[...]
    )
    hidden_grad = grad_ref[...].astype(jnp.float32) + hidden_back
    tokens_o[...] = hidden_grad
    wide_attn[half(side), :] = (residual_scale * hidden_grad).astype(jnp.bfloat16)
    spread = pltpu.make_async_remote_copy(
        src_ref=wide_attn.at[half(side)],
        dst_ref=wide_attn.at[half(side)],
        send_sem=pair_sem.at[0, 0],
        recv_sem=pair_sem.at[0, 1],
        device_id=partner("t"),
        device_id_type=MESH,
    )
    spread.start()
    spread_logits.start()
    later = spread_logits.steps()

    def meanwhile():
        moves.some(final, SPREAD[1])
        if later:
            later.pop(0)()

    block_o[...] = (hidden + residual_scale * home_out[2][...]).astype(jnp.bfloat16)
    for j in range(width // 128):
        gain_blk[width // 128 + j : width // 128 + j + 1, :] = chunk(ffn_gain_grad, j, 128)
    meanwhile()
    spread.wait()
    q_cols, k_cols = q_ref.shape[1], k_ref.shape[1]
    base = q_cols + 2 * k_cols
    pair_width = 2 * HEAD_DIM
    mixed_grad[...] = dot_f32(wide_attn[...], attn_ref[:, base:], ((1,), (0,))).astype(jnp.bfloat16)
    step = 256

    def keep(at, value):
        late_in[:, :, :, :, :, :, at : at + value.shape[1]] = value.astype(jnp.bfloat16).reshape(
            late_in.shape[:-1] + (value.shape[1],)
        )

    for i in range(q_cols // step):
        keep(
            base + i * step,
            dot_f32(wide_attn[...], chunk(mixed_ref, i, step), ((0,), (0,))),
        )
    meanwhile()
    cosine, sine = cos_ref[:, :pair_width], sin_ref[:, :pair_width]
    low = lanes_of((2 * rows, pair_width)) < HEAD_DIM
    held = None
    for g in range(q_cols // pair_width):
        query = stack_heads(chunk(q_ref, g, pair_width))
        keys = twice(chunk(k_ref, g // 2, pair_width), g % 2)
        values = twice(chunk(v_ref, g // 2, pair_width), g % 2)
        grad_heads = stack_heads(chunk(mixed_grad, g, pair_width))
        probs = probabilities(query, keys, mask_ref[...])
        dprobs = dot_f32(grad_heads, values, ((1,), (1,)))
        delta = jnp.sum(probs * dprobs, axis=1, keepdims=True)
        dscores = (probs * (dprobs - delta)).astype(jnp.bfloat16)
        dquery = unstack_heads(dot_f32(dscores, keys, ((1,), (0,)))) * score_scale
        qkv_grad[:, g * pair_width : (g + 1) * pair_width] = turn(
            dquery, cosine, sine, True
        ).astype(jnp.bfloat16)
        dkeys = dot_f32(dscores, query, ((0,), (0,)))
        dvalues = dot_f32(probs.astype(jnp.bfloat16), grad_heads, ((0,), (0,)))
        dkeys = dkeys + pltpu.roll(dkeys, HEAD_DIM, 1)
        dvalues = dvalues + pltpu.roll(dvalues, HEAD_DIM, 1)
        if g % 2 == 0:
            held = (dkeys, dvalues)
        else:
            j = g // 2 * pair_width
            dkeys = jnp.where(low, held[0], dkeys) * score_scale
            dvalues = jnp.where(low, held[1], dvalues)
            qkv_grad[:, q_cols + j : q_cols + j + pair_width] = turn(
                dkeys, cosine, sine, True
            ).astype(jnp.bfloat16)
            qkv_grad[:, q_cols + k_cols + j : q_cols + k_cols + j + pair_width] = dvalues.astype(
                jnp.bfloat16
            )
        meanwhile()
    for i in range(attn_ref.shape[0] // step):
        part[:, i * step : (i + 1) * step] = dot_f32(
            qkv_grad[...], attn_ref[i * step : (i + 1) * step, :base], ((1,), (1,))
        )
    narrowed = pltpu.make_async_remote_copy(
        src_ref=part.at[half(1 - side)],
        dst_ref=got,
        send_sem=pair_sem.at[1, 0],
        recv_sem=pair_sem.at[1, 1],
        device_id=partner("t"),
        device_id_type=MESH,
    )
    narrowed.start()
    meanwhile()
    for i in range(base // step):
        keep(i * step, dot_f32(wide_first[...], chunk(qkv_grad, i, step), ((0,), (0,))))
    last.start()
    moves.some(final, count)
    narrowed.wait()
    first_grad = part[half(side), :] + got[...]
    tokens = tokens_ref[...].astype(jnp.float32)
    scale_first = rms(tokens)
    tokens_back, attn_gain_grad = back_norm(
        first_grad, tokens * scale_first, scale_first, gain1_ref[...]
    )
    tokens_o[...] = tokens_o[...] + tokens_back
    for j in range(width // 128):
        gain_blk[j : j + 1, :] = chunk(attn_gain_grad, j, 128)

    def share(k, slot):
        return pltpu.make_async_remote_copy(
            src_ref=gain_blk,
            dst_ref=gains_o.at[slot],
            send_sem=share_s.at[k],
            recv_sem=share_r.at[k],
            device_id=place(k),
            device_id_type=MESH,
        )

    def share_start(k, carry):
        share(k, me).start()
        return carry

    def share_finish(k, carry):
        share(k, me).wait_send()
        share(k, lax.rem(me - k + total, total)).wait_recv()
        return carry

    lax.fori_loop(1, total, share_start, 0)
    own_gain = pltpu.make_async_copy(gain_blk, gains_o.at[me], share_own)
    own_gain.start()
    while later:
        later.pop(0)()
    last.run()
    spread_logits.finish()
    lax.fori_loop(1, total, share_finish, 0)
    own_gain.wait()
    moves.finish()


def back(rows_all, tagged_all, held, owned, router, router_t, attention, own_tag, own, tables):
    count, sides = lax.axis_size("dp"), lax.axis_size("tensor")
    attn_all, wide_first, query, key, value, mixed, hidden, normed = attention
    rows, width = hidden.shape
    total = rows_all.shape[0]
    columns = attn_all.shape[1]
    late_rows = attn_all.shape[0] // count
    holders = owned[0].shape[0] // count
    tall, half_ff = held[0].shape
    tile = total // 4
    bf16, f32 = jnp.bfloat16, jnp.float32
    shape = jax.ShapeDtypeStruct
    vmem, anywhere = pl.BlockSpec(memory_space=pltpu.VMEM), pl.BlockSpec(memory_space=pl.ANY)
    dma = pltpu.SemaphoreType.DMA
    home, late = home_pieces(width, 128), last_pieces(columns)
    widths = (width, 128, width)
    _, home_bufs, home_sems = Sum.scratch(home, rows, widths, 1)
    late_accs, late_bufs, late_sems = Sum.scratch(late, late_rows, (columns,))
    gain_rows = 2 * width // 128
    scratch = [
        pltpu.VMEM((2, tile, width), bf16),
        pltpu.VMEM((2, tile, tagged_all.shape[1]), bf16),
        dma((2, 2)),
        pltpu.VMEM((3, half_ff, tall), f32),
        pltpu.VMEM((3, holders, tall, half_ff), bf16),
    ]
    scratch += [pltpu.VMEM((2, 2, 2, 2, 2, rows, w), bf16) for w in widths]
    scratch += [pltpu.VMEM((2, 2, 2, 2, rows, w), bf16) for w in widths]
    scratch += [pltpu.VMEM((rows, w), f32) for w in widths] + home_bufs
    scratch += [dma((3, 4)), dma((3, 4))] + home_sems
    scratch += [pltpu.VMEM((2, 2, 2, 2, 1, late_rows, columns), bf16)] + late_accs + late_bufs
    scratch += late_sems
    scratch += [dma((holders, 3, count)), dma((holders, 3, count)), dma((holders, 3))]
    scratch += [pltpu.VMEM((holders, tall, half_ff), bf16) for _ in range(3)] + [dma((3,))]
    scratch += Fetch.semaphores(count)
    scratch += [
        pltpu.VMEM((rows, 128), f32),
        pltpu.VMEM((gain_rows, 128), f32),
        pltpu.VMEM((2 * rows, width), bf16),
        pltpu.VMEM((2 * rows, query.shape[1]), bf16),
        pltpu.VMEM((2 * rows, columns - query.shape[1]), bf16),
        pltpu.VMEM((2 * rows, width), f32),
        pltpu.VMEM((rows, width), f32),
        dma((2, 2)),
    ]
    scratch += Gather.semaphores()
    scratch += [dma((count * sides,)), dma((count * sides,)), dma]
    return pl.pallas_call(
        functools.partial(back_kernel, count, sides, home, late),
        out_shape=[
            shape((rows, width), bf16),
            shape((rows, width), f32),
            shape((late_rows, columns), f32),
            shape((total, 128), f32),
            shape((count * sides, gain_rows, 128), f32),
        ]
        + [shape((holders * count, tall // count, half_ff), bf16) for _ in range(3)],
        in_specs=[anywhere] * 8 + [vmem] * 18,
        out_specs=[vmem] * 5 + [anywhere] * 3,
        scratch_shapes=scratch,
        compiler_params=pltpu.CompilerParams(
            collective_id=2, has_side_effects=True, vmem_limit_bytes=60 << 20
        ),
        name="back",
    )(
        rows_all,
        tagged_all,
        *held,
        *owned,
        router,
        router_t,
        *attention,
        own_tag,
        *own,
        *tables,
    )


def local_near(
    tokens,
    out_grad,
    lengths,
    routes,
    attn_gain,
    w_query,
    w_key,
    w_value,
    w_out,
    ffn_gain,
    w_router,
    w_gate,
    w_up,
    w_down,
):
    local_rows = tokens.shape[0]
    row_count = routes.shape[0]
    model_width = tokens.shape[1]
    own_row = lax.axis_index("tensor") * local_rows
    q_cols, k_cols = w_query.shape[1], w_key.shape[1]
    cuts = (q_cols, q_cols + k_cols, q_cols + 2 * k_cols)
    tokens_f32 = tokens.astype(jnp.float32)
    out_f32 = out_grad.astype(jnp.float32)
    own_routes = lax.dynamic_slice_in_dim(routes, own_row, local_rows, 0)
    position, allowed = seq_layout(lengths[0], row_count)
    places = jnp.arange(256, dtype=jnp.int32) % (HEAD_DIM // 2)
    frequency = rope_base ** (-(places.astype(jnp.float32) * 2.0) / HEAD_DIM)
    angles = position.astype(jnp.float32)[:, None] * frequency[None, :]
    tables = [jnp.cos(angles), jnp.sin(angles), allowed.astype(jnp.float32)]
    _, _, normed_first = norm_forward(tokens_f32, attn_gain)
    tagged = jnp.concatenate(
        [
            (residual_scale * out_f32).astype(jnp.bfloat16),
            jnp.pad(own_routes.astype(jnp.bfloat16), ((0, 0), (0, 128 - TOPK))),
        ],
        axis=1,
    )
    tagged_all = lax.all_gather(tagged, ("dp", "tensor"), axis=0, tiled=True)
    (
        local_gate,
        local_up,
        local_down,
        rows_all,
        full_attn,
        wide_first,
        query_flat,
        key_flat,
        value_flat,
        mixed_out,
        hidden,
        normed_second,
    ) = front(
        jnp.concatenate([w_query, w_key, w_value, w_out], axis=1),
        [w_gate, w_up, w_down],
        normed_first,
        tokens,
        *tables,
        ffn_gain[None, :],
        q_cols,
        k_cols,
    )
    router_t = w_router.T
    router_parts = jnp.pad(
        jnp.concatenate(split_three(router_t), axis=0), ((0, 128 - 3 * EXPERTS), (0, 0))
    )
    block_rows, tokens_grad, packed_grad, logits_all, shared, *expert_grads = back(
        rows_all,
        tagged_all,
        [local_gate, local_up, local_down],
        [w_gate, w_up, w_down],
        router_parts,
        router_t,
        [
            full_attn,
            wide_first,
            query_flat,
            key_flat,
            value_flat,
            mixed_out,
            hidden,
            normed_second,
        ],
        tagged,
        [out_grad, tokens, attn_gain[None, :], ffn_gain[None, :]],
        tables,
    )
    router_total = exact_dot(rows_all, logits_all[:, :EXPERTS], ((0,), (0,)))
    gains = jnp.sum(shared, axis=0).reshape(2, model_width)
    return (
        block_rows,
        tokens_grad,
        gains[0],
        packed_grad[:, : cuts[0]],
        packed_grad[:, cuts[0] : cuts[1]],
        packed_grad[:, cuts[1] : cuts[2]],
        packed_grad[:, cuts[2] :],
        gains[1],
        router_total,
        *[g.astype(jnp.float32) for g in expert_grads],
    )


def local_far(
    tokens,
    out_grad,
    lengths,
    routes,
    attn_gain,
    w_query,
    w_key,
    w_value,
    w_out,
    ffn_gain,
    w_router,
    w_gate,
    w_up,
    w_down,
):
    local_rows = tokens.shape[0]
    row_count = routes.shape[0]
    model_width = tokens.shape[1]
    dp_count = lax.axis_size("dp")
    replicas = max(1, dp_count // EXPERTS)
    holders = max(1, EXPERTS // dp_count)
    clusters = EXPERTS // holders
    half_ff = w_gate.shape[2]
    heads_here = w_query.shape[1] // HEAD_DIM
    kv_here = w_key.shape[1] // HEAD_DIM
    own_row = lax.axis_index("tensor") * local_rows
    groups = (
        None
        if replicas == 1
        else [[r * clusters + c for c in range(clusters)] for r in range(replicas)]
    )
    q_cols, k_cols = w_query.shape[1], w_key.shape[1]
    cuts = (q_cols, q_cols + k_cols, q_cols + 2 * k_cols)
    packed_attn = gather_weights(jnp.concatenate([w_query, w_key, w_value, w_out], axis=1))
    full_qkv = packed_attn[:, : cuts[2]]
    full_out = packed_attn[:, cuts[2] :]

    def spread_out(weight):
        grouped = weight.reshape(clusters, holders, weight.shape[1], half_ff)
        return jnp.broadcast_to(grouped[None], (replicas,) + grouped.shape).reshape(
            dp_count, holders, weight.shape[1], half_ff
        )

    def fetch(weight):
        moved = lax.all_to_all(spread_out(weight), "dp", split_axis=0, concat_axis=2, tiled=True)
        return moved.reshape(holders, model_width, half_ff)

    local_gate, local_up, local_down = fetch(w_gate), fetch(w_up), fetch(w_down)
    tokens_f32 = tokens.astype(jnp.float32)
    out_f32 = out_grad.astype(jnp.float32)
    position, allowed = seq_layout(lengths[0], row_count)
    cosine, sine_table = rope_tables(position, HEAD_DIM)
    unit_first, scale_first, normed_first = norm_forward(tokens_f32, attn_gain)
    both = spread_rows(
        jnp.concatenate(
            [normed_first, (residual_scale * out_f32).astype(jnp.bfloat16)], axis=1
        )
    )
    wide_first = both[:, :model_width]
    tagged = jnp.concatenate(
        [
            both[:, model_width:],
            jnp.pad(routes.astype(jnp.bfloat16), ((0, 0), (0, 128 - TOPK))),
        ],
        axis=1,
    )
    tagged_all = gather_dp(tagged, groups)
    moe_all = tagged_all[:, :model_width]
    routes_all = tagged_all[:, model_width : model_width + TOPK].astype(jnp.int32)
    qkv = jnp.dot(wide_first, full_qkv, preferred_element_type=jnp.float32)
    query_heads = rotate(
        qkv[:, : cuts[0]].reshape(row_count, heads_here, HEAD_DIM), cosine, sine_table
    ).astype(jnp.bfloat16)
    key_heads = rotate(
        qkv[:, cuts[0] : cuts[1]].reshape(row_count, kv_here, HEAD_DIM), cosine, sine_table
    ).astype(jnp.bfloat16)
    value_heads = qkv[:, cuts[1] :].astype(jnp.bfloat16).reshape(row_count, kv_here, HEAD_DIM)
    mixed_out, log_total = attend(query_heads, key_heads, value_heads, allowed)
    hidden = tokens_f32 + residual_scale * narrow(dot_f32(mixed_out, full_out, ((1,), (1,))))
    unit_second, scale_second, normed_second = norm_forward(hidden, ffn_gain)
    rows_all = gather_dp(spread_rows(normed_second), groups)

    expert_ids = jnp.arange(EXPERTS, dtype=jnp.int32)

    def gate_of(rows_bf, row_routes):
        picked = row_routes[:, :, None] == expert_ids[None, None, :]
        logits = exact_dot(rows_bf, w_router, ((1,), (0,)))
        named = jnp.any(picked, axis=1)
        masked = jnp.where(named, logits, -jnp.inf)
        raised = jnp.exp(masked - jnp.max(masked, axis=1, keepdims=True))
        return picked, named, raised / jnp.sum(raised, axis=1, keepdims=True)

    _, named_all, gates_all = gate_of(rows_all, routes_all)
    first_expert = lax.axis_index("dp") % clusters * holders
    out_part = back_part = gate_slots = 0.0
    grads = []
    for h in range(holders):
        gate = lax.dynamic_slice_in_dim(gates_all, first_expert + h, 1, 1)
        here = lax.dynamic_slice_in_dim(named_all, first_expert + h, 1, 1)
        gate_pre = dot_f32(rows_all, local_gate[h], ((1,), (0,)))
        up_pre = dot_f32(rows_all, local_up[h], ((1,), (0,)))
        sigmoid_gate = jax.nn.sigmoid(gate_pre)
        activated = gate_pre * sigmoid_gate
        inner_act = (activated * up_pre).astype(jnp.bfloat16)
        produced = dot_f32(inner_act, local_down[h], ((1,), (1,))).astype(jnp.bfloat16)
        produced = produced.astype(jnp.float32)
        out_part = out_part + jnp.where(here, gate * produced, 0.0)
        moe_f32 = moe_all.astype(jnp.float32)
        gate_part = jnp.sum(moe_f32 * produced, axis=1, keepdims=True)
        gate_slots = gate_slots + jnp.where(routes_all == first_expert + h, gate_part, 0.0)
        route_grad = jnp.where(here, gate * moe_f32, 0.0).astype(jnp.bfloat16)
        inner_grad = dot_f32(route_grad, local_down[h], ((1,), (0,)))
        gate_pre_grad = (
            inner_grad * up_pre * sigmoid_gate * (1.0 + gate_pre * (1.0 - sigmoid_gate))
        ).astype(jnp.bfloat16)
        up_pre_grad = (inner_grad * activated).astype(jnp.bfloat16)
        back = dot_f32(gate_pre_grad, local_gate[h], ((1,), (1,))) + dot_f32(
            up_pre_grad, local_up[h], ((1,), (1,))
        )
        back_part = back_part + back.astype(jnp.bfloat16).astype(jnp.float32)
        grads.append(
            (
                dot_f32(rows_all, gate_pre_grad, ((0,), (0,))).astype(jnp.bfloat16),
                dot_f32(rows_all, up_pre_grad, ((0,), (0,))).astype(jnp.bfloat16),
                dot_f32(route_grad, inner_act, ((0,), (0,))).astype(jnp.bfloat16),
            )
        )
    slot_parts = split_three(gate_slots)
    pad = jnp.zeros((rows_all.shape[0], 128 - 3 * TOPK), jnp.bfloat16)
    home = scatter_dp(
        jnp.concatenate(
            [back_part.astype(jnp.bfloat16)] + slot_parts + [pad, out_part.astype(jnp.bfloat16)],
            axis=1,
        ),
        groups,
    ).astype(jnp.float32)
    back_home = home[:, : model_width + 128]
    out_home = home[:, model_width + 128 :]
    slots = back_home[:, model_width:]
    gate_half = slots[:, :TOPK] + slots[:, TOPK : 2 * TOPK] + slots[:, 2 * TOPK : 3 * TOPK]
    own_back = narrow(
        jnp.concatenate(
            [back_home[:, :model_width], jnp.pad(gate_half, ((0, 0), (0, 128 - TOPK)))], axis=1
        )
    )
    expert_back = own_back[:, :model_width]
    gate_grad = own_back[:, model_width : model_width + TOPK]
    block_rows = (hidden + residual_scale * narrow(out_home)).astype(jnp.bfloat16)

    def send_home(index):
        stacked = jnp.stack([grads[h][index] for h in range(holders)])
        moved = lax.all_to_all(stacked[None], "dp", split_axis=2, concat_axis=0, tiled=True)
        return jnp.sum(
            moved.astype(jnp.float32).reshape(
                replicas, clusters * holders, moved.shape[2], half_ff
            ),
            axis=0,
        )

    own_routes = lax.dynamic_slice_in_dim(routes, own_row, local_rows, 0)
    picked_own, _, gates_dense = gate_of(normed_second, own_routes)
    gates_own = jnp.sum(jnp.where(picked_own, gates_dense[:, None, :], 0.0), axis=2)
    chosen_grad = gates_own * (gate_grad - jnp.sum(gates_own * gate_grad, axis=1, keepdims=True))
    logits_grad = jnp.sum(jnp.where(picked_own, chosen_grad[:, :, None], 0.0), axis=1)
    second_grad = expert_back + jnp.dot(logits_grad, w_router.T, precision=lax.Precision.HIGHEST)
    hidden_back, ffn_gain_grad = norm_backward(second_grad, unit_second, scale_second, ffn_gain)
    hidden_grad = out_f32 + hidden_back
    attn_grad = spread_rows((residual_scale * hidden_grad).astype(jnp.bfloat16))
    mixed_grad = jnp.dot(attn_grad, full_out, preferred_element_type=jnp.float32).astype(
        jnp.bfloat16
    )
    out_w_grad = dot_f32(attn_grad, mixed_out, ((0,), (0,)))
    dquery, key_grad, dvalues = attend_back(
        query_heads, key_heads, value_heads, allowed, log_total, mixed_grad
    )
    query_grad = (
        unrotate(dquery, cosine, sine_table)
        .astype(jnp.bfloat16)
        .reshape(row_count, heads_here * HEAD_DIM)
    )
    keys_grad = (
        unrotate(key_grad, cosine, sine_table)
        .astype(jnp.bfloat16)
        .reshape(row_count, kv_here * HEAD_DIM)
    )
    value_grad = dvalues.astype(jnp.bfloat16).reshape(row_count, kv_here * HEAD_DIM)
    qkv_grad = jnp.concatenate([query_grad, keys_grad, value_grad], axis=1)
    qkv_w_grad = dot_f32(wide_first, qkv_grad, ((0,), (0,)))
    packed_grad = scatter_weights(
        jnp.concatenate([qkv_w_grad, out_w_grad], axis=1).astype(jnp.bfloat16)
    ).astype(jnp.float32)
    first_grad = narrow(dot_f32(qkv_grad, full_qkv, ((1,), (1,))))
    tokens_back, attn_gain_grad = norm_backward(first_grad, unit_first, scale_first, attn_gain)
    tokens_grad = hidden_grad + tokens_back
    attn_gain_total, ffn_gain_total, router_total = lax.psum(
        (
            attn_gain_grad,
            ffn_gain_grad,
            exact_dot(normed_second, logits_grad, ((0,), (0,))),
        ),
        ("dp", "tensor"),
    )
    return (
        block_rows,
        tokens_grad,
        attn_gain_total,
        packed_grad[:, : cuts[0]],
        packed_grad[:, cuts[0] : cuts[1]],
        packed_grad[:, cuts[1] : cuts[2]],
        packed_grad[:, cuts[2] :],
        ffn_gain_total,
        router_total,
        send_home(0),
        send_home(1),
        send_home(2),
    )


def solution(mesh):
    placed = (
        P(("dp", "tensor"), None),
        P(("dp", "tensor"), None),
        P("dp", None),
        P("dp", None),
        P(),
        P("dp", "tensor"),
        P("dp", "tensor"),
        P("dp", "tensor"),
        P("dp", "tensor"),
        P(),
        P(),
        P(None, "dp", "tensor"),
        P(None, "dp", "tensor"),
        P(None, "dp", "tensor"),
    )
    near = mesh.shape["dp"] == 16 and mesh.shape["tensor"] == 2
    return jax.shard_map(
        local_near if near else local_far,
        mesh=mesh,
        in_specs=placed,
        out_specs=(
            P(("dp", "tensor"), None),
            P(("dp", "tensor"), None),
            P(),
            P("dp", "tensor"),
            P("dp", "tensor"),
            P("dp", "tensor"),
            P("dp", "tensor"),
            P(),
            P(),
            P(None, "dp", "tensor"),
            P(None, "dp", "tensor"),
            P(None, "dp", "tensor"),
        ),
        check_vma=False,
    )
```

```python
import functools

import jax
import jax.numpy as jnp
from jax import lax
from jax.experimental import pallas as pl
from jax.experimental.pallas import tpu as pltpu
from jax.sharding import PartitionSpec as P

EXPERTS = 32
TOPK = 8
HEAD_DIM = 64


eps_norm = 1e-06
residual_scale = 0.22
score_scale = 0.015625
rope_base = 10000.0
masked_score = -1e30


def norm_forward(row_block, gain_vec):
    rscale = lax.rsqrt(jnp.mean(row_block * row_block, axis=1, keepdims=True) + eps_norm)
    unit_rows = row_block * rscale
    return (unit_rows, rscale, (unit_rows * gain_vec).astype(jnp.bfloat16))


def norm_backward(gradient, unit_rows, rscale, gain_vec):
    unit_grad = gradient * gain_vec
    back_rows = rscale * (
        unit_grad - unit_rows * jnp.mean(unit_grad * unit_rows, axis=1, keepdims=True)
    )
    return (back_rows, jnp.sum(gradient * unit_rows, axis=0))


def seq_layout(seq_lengths, row_count):
    order = jnp.arange(seq_lengths.shape[0], dtype=jnp.int32)
    seq_ends = jnp.sum(jnp.where(order[:, None] <= order[None, :], seq_lengths[:, None], 0), axis=0)
    starts = seq_ends - seq_lengths
    places = jnp.arange(row_count, dtype=jnp.int32)
    segment = jnp.sum((places[:, None] >= seq_ends[None, :]).astype(jnp.int32), axis=1)
    member = segment[:, None] == jnp.arange(seq_lengths.shape[0], dtype=jnp.int32)[None, :]
    offset = jnp.sum(jnp.where(member, starts[None, :], 0), axis=1)
    allowed = (segment[:, None] == segment[None, :]) & (places[None, :] <= places[:, None])
    return (places - offset, allowed)


def rope_tables(position, head_width):
    frequency = rope_base ** (-(jnp.arange(head_width // 2, dtype=jnp.float32) * 2.0) / head_width)
    angles = position.astype(jnp.float32)[:, None] * frequency[None, :]
    cosine = jnp.concatenate([jnp.cos(angles), jnp.cos(angles)], axis=1)[:, None, :]
    sine_table = jnp.concatenate([jnp.sin(angles), jnp.sin(angles)], axis=1)[:, None, :]
    return (cosine, sine_table)


def rotate(vectors, cosine, sine_table):
    half_width = vectors.shape[-1] // 2
    first_half = vectors[..., :half_width]
    second_half = vectors[..., half_width:]
    return vectors * cosine + jnp.concatenate([-second_half, first_half], axis=-1) * sine_table


def unrotate(gradient, cosine, sine_table):
    half_width = gradient.shape[-1] // 2
    first_half = gradient[..., :half_width]
    second_half = gradient[..., half_width:]
    return gradient * cosine + jnp.concatenate([second_half, -first_half], axis=-1) * sine_table


def score_block(query_heads, key_heads, allowed):
    row_count, head_count, head_width = query_heads.shape
    kv_count = key_heads.shape[1]
    grouped = query_heads.reshape(row_count, kv_count, head_count // kv_count, head_width)
    scores = (
        jnp.einsum("igrd,jgd->grij", grouped, key_heads, preferred_element_type=jnp.float32)
        * score_scale
    )
    return (grouped, jnp.where(allowed[None, None], scores, masked_score))


def attend(query_heads, key_heads, value_heads, allowed):
    row_count, head_count, head_width = query_heads.shape
    grouped, scores = score_block(query_heads, key_heads, allowed)
    row_max = jnp.max(scores, axis=-1, keepdims=True)
    log_total = row_max + jnp.log(jnp.sum(jnp.exp(scores - row_max), axis=-1, keepdims=True))
    prob_bf = jnp.exp(scores - log_total).astype(jnp.bfloat16)
    mixed_out = jnp.einsum(
        "grij,jgd->igrd", prob_bf, value_heads, preferred_element_type=jnp.float32
    )
    return (mixed_out.reshape(row_count, head_count * head_width).astype(jnp.bfloat16), log_total)


def attend_back(query_heads, key_heads, value_heads, allowed, log_total, mixed_grad):
    row_count, head_count, head_width = query_heads.shape
    kv_count = key_heads.shape[1]
    grouped, scores = score_block(query_heads, key_heads, allowed)
    prob_full = jnp.exp(scores - log_total)
    grad_heads = mixed_grad.reshape(row_count, kv_count, head_count // kv_count, head_width)
    dprobs = jnp.einsum(
        "igrd,jgd->grij", grad_heads, value_heads, preferred_element_type=jnp.float32
    )
    row_delta = jnp.sum(prob_full * dprobs, axis=-1, keepdims=True)
    dscores = (prob_full * (dprobs - row_delta)).astype(jnp.bfloat16)
    dquery = (
        jnp.einsum("grij,jgd->igrd", dscores, key_heads, preferred_element_type=jnp.float32)
        * score_scale
    )
    key_grad = (
        jnp.einsum("grij,igrd->jgd", dscores, grouped, preferred_element_type=jnp.float32)
        * score_scale
    )
    dvalues = jnp.einsum(
        "grij,igrd->jgd",
        prob_full.astype(jnp.bfloat16),
        grad_heads,
        preferred_element_type=jnp.float32,
    )
    return (dquery.reshape(row_count, head_count, head_width), key_grad, dvalues)


def spread_rows(row_block):
    return lax.all_gather(row_block, "tensor", axis=0, tiled=True)


def narrow(partial_rows):
    if lax.axis_size("tensor") != 2:
        return lax.psum_scatter(partial_rows, "tensor", scatter_dimension=0, tiled=True)
    half = partial_rows.shape[0] // 2
    mine = lax.axis_index("tensor")
    away = lax.dynamic_slice_in_dim(partial_rows, (1 - mine) * half, half, 0)
    kept = lax.dynamic_slice_in_dim(partial_rows, mine * half, half, 0)
    return kept + lax.ppermute(away, "tensor", [(0, 1), (1, 0)])


def split_three(values):
    high = lax.reduce_precision(values, 8, 7)
    rest = values - high
    middle = lax.reduce_precision(rest, 8, 7)
    return [part.astype(jnp.bfloat16) for part in (high, middle, rest - middle)]


def dot_f32(left, right, dims):
    return lax.dot_general(left, right, (dims, ((), ())), preferred_element_type=jnp.float32)


def exact_dot(rows_bf, values, dims):
    width = values.shape[1]
    product = dot_f32(rows_bf, jnp.concatenate(split_three(values), axis=1), dims)
    return product[:, :width] + (product[:, width : 2 * width] + product[:, 2 * width :])


def gather_dp(rows, groups):
    return lax.all_gather(rows, "dp", axis=0, tiled=True, axis_index_groups=groups)


def scatter_dp(rows, groups):
    return lax.psum_scatter(
        rows, "dp", scatter_dimension=0, tiled=True, axis_index_groups=groups
    )


def gather_weights(packed):
    return lax.all_gather(packed, "dp", axis=0, tiled=True)


def scatter_weights(packed):
    return lax.psum_scatter(packed, "dp", scatter_dimension=0, tiled=True)


MESH = pl.DeviceIdType.MESH
WEIGHT = {"core": 1, "x": 2, "z0": 4, "z1": 8}
DIMS = ("z1", "z0", "x", "t")
ORDERS = (("x", "t", "z0", "z1"), ("t", "z0", "x", "z1"), ("z0", "x", "z1", "t"))


def bit_of(me, weight):
    return lax.rem(lax.div(me, weight), 2)


def partner(name):
    me, side = lax.axis_index("dp"), lax.axis_index("tensor")
    if name == "t":
        return (me, 1 - side)
    return (me + WEIGHT[name] * (1 - 2 * bit_of(me, WEIGHT[name])), side)


def greet_plane(count, others=()):
    me, side = lax.axis_index("dp"), lax.axis_index("tensor")
    barrier = pltpu.get_barrier_semaphore()

    def greet(k, carry):
        pl.semaphore_signal(
            barrier, inc=1, device_id=(lax.rem(me + k, count), side), device_id_type=MESH
        )
        return carry

    lax.fori_loop(1, count, greet, 0)
    for place in others:
        pl.semaphore_signal(barrier, inc=1, device_id=place, device_id_type=MESH)
    pl.semaphore_wait(barrier, count - 1 + len(others))


def far_first(i, count):
    return count // 2 + (1 - 2 * lax.rem(i, 2)) * lax.div(i + 1, 2)


class Fetch:
    def __init__(self, count, which, ins, outs, send_sem, recv_sem, own_sem):
        self.count, self.which = count, which
        self.ins, self.outs = ins, outs
        self.sems = (send_sem, recv_sem, own_sem)
        self.holders, self.rows = ins[0].shape[0] // count, ins[0].shape[1]
        self.issued = 0

    def ends(self, w, peer, owner):
        at = pl.ds(pl.multiple_of(owner * self.rows, self.rows), self.rows)
        return self.ins[w].at[peer * self.holders + self.which], self.outs[w].at[at]

    def copy(self, w, k, owner):
        me, side = lax.axis_index("dp"), lax.axis_index("tensor")
        peer = lax.rem(me + k, self.count)
        src, dst = self.ends(w, peer, owner)
        return pltpu.make_async_remote_copy(
            src_ref=src,
            dst_ref=dst,
            send_sem=self.sems[0].at[w, k],
            recv_sem=self.sems[1].at[w, k],
            device_id=(peer, side),
            device_id_type=MESH,
        )

    def own(self, w):
        me = lax.axis_index("dp")
        return pltpu.make_async_copy(*self.ends(w, me, me), self.sems[2].at[w])

    def start(self):
        def step(i, carry):
            for w in range(3):
                self.copy(w, far_first(i, self.count), lax.axis_index("dp")).start()
            return carry

        lax.fori_loop(0, self.count - 1, step, 0)
        for w in range(3):
            self.own(w).start()

    def some(self, amount):
        for _ in range(amount):
            if self.issued < 3 * (self.count - 1):
                i, w = divmod(self.issued, 3)
                k = self.count // 2 + (1 - 2 * (i % 2)) * ((i + 1) // 2)
                self.copy(w, k, lax.axis_index("dp")).start()
                self.issued += 1

    def rest(self):
        self.some(3 * self.count)
        for w in range(3):
            self.own(w).start()

    def finish(self):
        me = lax.axis_index("dp")

        def step(i, carry):
            k = far_first(i, self.count)
            for w in range(3):
                self.copy(w, k, me).wait_send()
                self.copy(w, k, lax.rem(me - k + self.count, self.count)).wait_recv()
            return carry

        lax.fori_loop(0, self.count - 1, step, 0)
        for w in range(3):
            self.own(w).wait()

    @staticmethod
    def semaphores(count):
        return [
            pltpu.SemaphoreType.DMA((3, count)),
            pltpu.SemaphoreType.DMA((3, count)),
            pltpu.SemaphoreType.DMA((3,)),
        ]


class Sum:
    def __init__(
        self,
        pieces,
        ins,
        outs,
        accs,
        bufs,
        send_sem,
        recv_sem,
        firsts=None,
        first_s=None,
        first_r=None,
    ):
        me, side = lax.axis_index("dp"), lax.axis_index("tensor")
        self.pieces, self.ins, self.outs, self.accs, self.bufs = pieces, ins, outs, accs, bufs
        self.send_sem, self.recv_sem = send_sem, recv_sem
        self.firsts, self.first_s, self.first_r = firsts, first_s, first_r
        self.core = bit_of(me, 1)
        self.whole = "t" in pieces[0][3]
        self.last = len(pieces[0][3])
        self.mine = {
            "z1": bit_of(me, 8),
            "z0": bit_of(me, 4),
            "x": bit_of(me, 2),
            "t": side if self.whole else 0,
        }

    def buf(self, i, s):
        if self.firsts is not None:
            return self.bufs[i * self.last + s - 1] if s else None
        return self.bufs[i * (self.last + 1) + s]

    def first_copy(self, which, z):
        z1, z0 = (z // 2, z % 2) if isinstance(z, int) else (lax.div(z, 2), lax.rem(z, 2))
        return pltpu.make_async_remote_copy(
            src_ref=self.ins[which].at[z1, z0, :, 1 - self.core],
            dst_ref=self.firsts[which].at[z1, z0],
            send_sem=self.first_s.at[which, z],
            recv_sem=self.first_r.at[which, z],
            device_id=partner("core"),
            device_id_type=MESH,
        )

    def send_first(self, which, z):
        self.first_copy(which, z).start()

    def exchange(self, i, s):
        which, first, width, order = self.pieces[i]
        columns = pl.ds(first, width)
        if s == 0:
            src = self.ins[which].at[:, :, :, 1 - self.core, :, :, columns]
            place = partner("core")
        else:
            done, now = order[: s - 1], order[s - 1]
            index = []
            for d in DIMS:
                if d in done:
                    index.append(pl.ds(self.mine[d], 1))
                elif d == now:
                    index.append(pl.ds(1 - self.mine[d], 1))
                else:
                    index.append(slice(None))
            src = self.accs[which].at[tuple(index) + (slice(None), columns)]
            place = partner(now)
        return pltpu.make_async_remote_copy(
            src_ref=src,
            dst_ref=self.buf(i, s),
            send_sem=self.send_sem.at[i, s],
            recv_sem=self.recv_sem.at[i, s],
            device_id=place,
            device_id_type=MESH,
        )

    def add(self, i, s):
        which, first, width, order = self.pieces[i]
        buf = self.buf(i, s)
        columns = pl.ds(first, width)
        if s == self.last:
            at = tuple(self.mine[d] for d in DIMS) + (slice(None), columns)
            self.outs[which][:, columns] = self.accs[which][at].astype(jnp.float32) + buf[
                0, 0, 0, 0
            ].astype(jnp.float32)
            return
        free = [d for d in DIMS if d in order[s:]]

        def step(b, carry):
            at, frm = dict(self.mine), {d: 0 for d in DIMS}
            left = b
            for d in reversed(free):
                at[d] = frm[d] = lax.rem(left, 2)
                left = lax.div(left, 2)
            at = tuple(at[d] for d in DIMS)
            if s == 0:
                have = self.ins[which][at[:3] + (self.core, at[3], slice(None), columns)]
            else:
                have = self.accs[which][at + (slice(None), columns)]
            frm = tuple(frm[d] for d in DIMS)
            if s == 0 and self.firsts is not None:
                got = self.firsts[which][frm + (slice(None), columns)]
            else:
                got = buf[frm]
            self.accs[which][at + (slice(None), columns)] = (
                have.astype(jnp.float32) + got.astype(jnp.float32)
            ).astype(jnp.bfloat16)
            return carry

        lax.fori_loop(0, 2 ** len(free), step, 0)

    def start(self):
        for i in range(len(self.pieces)):
            self.exchange(i, 0).start()

    def run(self, between=lambda: None):
        n = len(self.pieces)
        early = self.firsts is not None
        if early:
            for which in range(len(self.ins)):
                for z in range(4):
                    self.first_copy(which, z).wait_recv()
        for s in range(self.last + 1):
            for i in range(n):
                if s or not early:
                    self.exchange(i, s).wait_recv()
                self.add(i, s)
                if s < self.last:
                    self.exchange(i, s + 1).start()
                between()
        if early:
            for which in range(len(self.ins)):
                for z in range(4):
                    self.first_copy(which, z).wait_send()
        for s in range(int(early), self.last + 1):
            for i in range(n):
                self.exchange(i, s).wait_send()

    @staticmethod
    def scratch(pieces, rows, widths, begin=0):
        whole = 2 if "t" in pieces[0][3] else 1
        stages = len(pieces[0][3]) + 1
        bufs = []
        for _, _, width, order in pieces:
            for s in range(begin, stages):
                free = tuple(2 if d in order[s:] else 1 for d in DIMS)
                bufs.append(pltpu.VMEM(free + (rows, width), jnp.bfloat16))
        accs = [pltpu.VMEM((2, 2, 2, whole, rows, w), jnp.bfloat16) for w in widths]
        sems = [pltpu.SemaphoreType.DMA((len(pieces), stages))] * 2
        return accs, bufs, sems

    @staticmethod
    def view(array, whole):
        blocks = 32 if whole else 16
        return array.reshape(
            2, 2, 2, 2, 2 if whole else 1, array.shape[0] // blocks, array.shape[1]
        )


def home_pieces(wide, thin):
    cut = wide * 3 // 4
    return (
        (0, 0, cut, ORDERS[0]),
        (2, 0, cut, ORDERS[1]),
        (0, cut, wide - cut, ORDERS[2]),
        (2, cut, wide - cut, ORDERS[2]),
        (1, 0, thin, ORDERS[2]),
    )


def last_pieces(width):
    cut = width // 2
    return ((0, 0, cut, ("x", "z0", "z1")), (0, cut, width - cut, ("z0", "x", "z1")))


class Gather:
    def __init__(self, src, out, sides, sems):
        me, side = lax.axis_index("dp"), lax.axis_index("tensor")
        self.src, self.out, self.sides, self.sems = src, out, sides, sems
        self.rows = src.shape[0]
        self.me, self.t = me, side
        self.z, self.x, self.core = lax.div(me, 4), bit_of(me, 2), bit_of(me, 1)

    def at(self, z, x, t, core):
        place = z * 4 + x * 2 + core
        if self.sides:
            place = place * 2 + t
        return self.out.at[pl.ds(pl.multiple_of(place * self.rows, self.rows), self.rows)]

    def copy(self, pair, index, src, dst, device):
        return pltpu.make_async_remote_copy(
            src_ref=src,
            dst_ref=dst,
            send_sem=self.sems[pair].at[index],
            recv_sem=self.sems[pair + 1].at[index],
            device_id=device,
            device_id_type=MESH,
        )

    def line(self, up, z, src=None):
        block = self.at(z, self.x, self.t, self.core)
        step = 4 if up else -4
        device = (lax.rem(self.me + step + 16, 16), self.t)
        return self.copy(0, (int(up), z), block if src is None else src, block, device)

    def over_x(self, diag, z, x, t, src=None):
        block = self.at(z, x, t, self.core)
        return self.copy(
            2, (int(diag), z), block if src is None else src, block, partner("x")
        )

    def over_t(self, diag, z, x, t, src=None):
        block = self.at(z, x, t, self.core)
        return self.copy(
            4, (int(diag), z), block if src is None else src, block, partner("t")
        )

    def over_core(self, z, x, t, core, src=None):
        block = self.at(z, x, t, core)
        return self.copy(6, (t, x, z), block if src is None else src, block, partner("core"))

    def own(self):
        return pltpu.make_async_copy(
            self.src, self.at(self.z, self.x, self.t, self.core), self.sems[8]
        )

    def sideways(self, z, src=None):
        self.over_x(False, z, self.x, self.t, src).start()
        if self.sides:
            self.over_t(False, z, self.x, self.t, src).start()
        self.over_core(z, self.x, self.t, self.core, src).start()

    def start(self):
        @pl.when(self.z < 3)
        def _():
            self.line(True, self.z, self.src).start()

        @pl.when(self.z > 0)
        def _():
            self.line(False, self.z, self.src).start()

        self.sideways(self.z, self.src)
        self.own().start()

    def pass_line(self, s):
        @pl.when(self.z >= s)
        def _():
            z = self.z - s
            self.line(True, z).wait_recv()

            @pl.when(self.z < 3)
            def _():
                self.line(True, z).start()

            self.sideways(z)

        @pl.when(self.z + s <= 3)
        def _():
            z = self.z + s
            self.line(False, z).wait_recv()

            @pl.when(self.z > 0)
            def _():
                self.line(False, z).start()

            self.sideways(z)

    def second(self, z):
        x, t = self.x, self.t
        self.over_x(False, z, 1 - x, t).wait_recv()
        if self.sides:

            @pl.when(z >= 2)
            def _():
                self.over_t(True, z, 1 - x, t).start()

        self.over_core(z, 1 - x, t, self.core).start()
        if self.sides:
            self.over_t(False, z, x, 1 - t).wait_recv()

            @pl.when(z < 2)
            def _():
                self.over_x(True, z, x, 1 - t).start()

            self.over_core(z, x, 1 - t, self.core).start()

    def pass_second(self, s):
        @pl.when(self.z >= s)
        def _():
            self.second(self.z - s)

        if s:

            @pl.when(self.z + s <= 3)
            def _():
                self.second(self.z + s)

    def third(self, z):
        block = (z, 1 - self.x, 1 - self.t)
        (self.over_x if z < 2 else self.over_t)(True, *block).wait_recv()
        self.over_core(*block, self.core).start()

    def steps(self):
        line, second = self.pass_line, self.pass_second
        order = (line, 1), (second, 0), (line, 2), (second, 1), (line, 3), (second, 2), (second, 3)
        steps = [functools.partial(*each) for each in order]
        if self.sides:
            steps += [functools.partial(self.third, z) for z in range(4)]
        return steps + [self.arrived]

    def arrived(self):
        for z in range(4):
            for x in range(2):
                for t in range(2) if self.sides else [self.t]:
                    self.over_core(z, x, t, 1 - self.core).wait_recv()
        self.own().wait()

    def finish(self):
        x, t = self.x, self.t
        for z in range(4):

            @pl.when((z <= self.z) & (self.z < 3))
            def _():
                self.line(True, z).wait_send()

            @pl.when((z >= self.z) & (self.z > 0))
            def _():
                self.line(False, z).wait_send()

            self.over_x(False, z, x, t).wait_send()
            if self.sides:
                self.over_t(False, z, x, t).wait_send()
                if z < 2:
                    self.over_x(True, z, x, 1 - t).wait_send()
                else:
                    self.over_t(True, z, 1 - x, t).wait_send()
            for xb in range(2):
                for tb in range(2) if self.sides else [t]:
                    self.over_core(z, xb, tb, self.core).wait_send()

    @staticmethod
    def semaphores():
        dma = pltpu.SemaphoreType.DMA
        return [dma((2, 4))] * 6 + [dma((2, 2, 4))] * 2 + [dma]


def lanes_of(shape):
    return lax.broadcasted_iota(jnp.int32, shape, 1)


def turn(values, cosine, sine_table, back):
    width = values.shape[1]
    low = lax.rem(lanes_of(values.shape), HEAD_DIM) < HEAD_DIM // 2
    later = pltpu.roll(values, width - HEAD_DIM // 2, 1)
    earlier = pltpu.roll(values, HEAD_DIM // 2, 1)
    moved = jnp.where(low, later, -earlier) if back else jnp.where(low, -later, earlier)
    return values * cosine + moved * sine_table


def twice(pair, second):
    wide = pair.astype(jnp.float32)
    other = pltpu.roll(wide, HEAD_DIM, 1)
    low = lanes_of(wide.shape) < HEAD_DIM
    both = jnp.where(low, other, wide) if second else jnp.where(low, wide, other)
    return both.astype(jnp.bfloat16)


def stack_heads(pair):
    wide = pair.astype(jnp.float32)
    low = lanes_of(wide.shape) < HEAD_DIM
    return jnp.concatenate(
        [jnp.where(low, wide, 0.0), jnp.where(low, 0.0, wide)], axis=0
    ).astype(jnp.bfloat16)


def unstack_heads(stacked):
    rows = stacked.shape[0] // 2
    low = lanes_of((rows, stacked.shape[1])) < HEAD_DIM
    return jnp.where(low, stacked[:rows], stacked[rows:])


def probabilities(query, keys, mask):
    scores = dot_f32(query, keys, ((1,), (1,))) * score_scale
    scores = jnp.where(jnp.concatenate([mask, mask], axis=0) > 0.0, scores, masked_score)
    row_max = jnp.max(scores, axis=1, keepdims=True)
    log_total = row_max + jnp.log(jnp.sum(jnp.exp(scores - row_max), axis=1, keepdims=True))
    return jnp.exp(scores - log_total)


def chunk(ref, i, width):
    return ref[:, i * width : (i + 1) * width]


PLAN = (2, 2, 2, 2, 2)


def front_kernel(count, *refs):
    attn_ref, gate_ref, up_ref, down_ref, first_ref, tokens_ref = refs[:6]
    cos_ref, sin_ref, mask_ref, gain_ref = refs[6:10]
    gate_o, up_o, down_o, rows_o, attn_o, wide_o = refs[10:16]
    q_o, k_o, v_o, mixed_o, hidden_o, normed_o = refs[16:22]
    part, got, pair_sem = refs[22:25]
    swap = Fetch(count, 0, [gate_ref, up_ref, down_ref], [gate_o, up_o, down_o], *refs[25:28])
    attn = Gather(attn_ref, attn_o, False, refs[28:37])
    rows_job = Gather(normed_o, rows_o, True, refs[37:46])
    side = lax.axis_index("tensor")
    rows = first_ref.shape[0]

    def half(which):
        return pl.ds(pl.multiple_of(which * rows, rows), rows)

    spread = pltpu.make_async_remote_copy(
        src_ref=first_ref,
        dst_ref=wide_o.at[half(side)],
        send_sem=pair_sem.at[0, 0],
        recv_sem=pair_sem.at[0, 1],
        device_id=partner("t"),
        device_id_type=MESH,
    )
    narrowed = pltpu.make_async_remote_copy(
        src_ref=part.at[half(1 - side)],
        dst_ref=got,
        send_sem=pair_sem.at[1, 0],
        recv_sem=pair_sem.at[1, 1],
        device_id=partner("t"),
        device_id_type=MESH,
    )
    greet_plane(count, [partner("t")])
    attn.start()
    spread.start()
    wide_o[half(side), :] = first_ref[...]
    swap.some(PLAN[0])
    for each in attn.steps():
        each()
        swap.some(PLAN[1])
    spread.wait()
    swap.some(PLAN[2])
    q_cols, k_cols = q_o.shape[1], k_o.shape[1]
    step = 256
    for i in range((q_cols + 2 * k_cols) // step):
        at = i * step
        made = dot_f32(wide_o[...], chunk(attn_o, i, step), ((1,), (0,)))
        if at < q_cols + k_cols:
            made = turn(made, cos_ref[...], sin_ref[...], False)
        made = made.astype(jnp.bfloat16)
        if at < q_cols:
            q_o[:, at : at + step] = made
        elif at < q_cols + k_cols:
            k_o[:, at - q_cols : at - q_cols + step] = made
        else:
            v_o[:, at - q_cols - k_cols : at - q_cols - k_cols + step] = made
        swap.some(PLAN[2])
    pair_width = 2 * HEAD_DIM
    for g in range(q_cols // pair_width):
        query = stack_heads(chunk(q_o, g, pair_width))
        keys = twice(chunk(k_o, g // 2, pair_width), g % 2)
        values = twice(chunk(v_o, g // 2, pair_width), g % 2)
        probs = probabilities(query, keys, mask_ref[...]).astype(jnp.bfloat16)
        mixed = unstack_heads(dot_f32(probs, values, ((1,), (0,))))
        mixed_o[:, g * pair_width : (g + 1) * pair_width] = mixed.astype(jnp.bfloat16)
        swap.some(PLAN[2])
    base = q_cols + 2 * k_cols
    for i in range(attn_o.shape[0] // step):
        part[:, i * step : (i + 1) * step] = dot_f32(
            mixed_o[...], attn_o[i * step : (i + 1) * step, base:], ((1,), (1,))
        )
    narrowed.start()
    swap.some(PLAN[3])
    narrowed.wait()
    hidden = tokens_ref[...].astype(jnp.float32) + residual_scale * (
        part[half(side), :] + got[...]
    )
    hidden_o[...] = hidden
    rscale = lax.rsqrt(jnp.mean(hidden * hidden, axis=1, keepdims=True) + eps_norm)
    normed_o[...] = (hidden * rscale * gain_ref[...]).astype(jnp.bfloat16)
    rows_job.start()
    for each in rows_job.steps():
        swap.some(PLAN[4])
        each()
    swap.rest()
    attn.finish()
    rows_job.finish()
    swap.finish()


def front(packed, experts, first, tokens, cosine, sine_table, mask, gain, q_cols, k_cols):
    count = lax.axis_size("dp")
    rows, width = tokens.shape
    total = rows * count * 2
    wide_rows = 2 * rows
    _, expert_rows, half_ff = experts[0].shape
    bf16, f32 = jnp.bfloat16, jnp.float32
    shape = jax.ShapeDtypeStruct
    vmem, anywhere = pl.BlockSpec(memory_space=pltpu.VMEM), pl.BlockSpec(memory_space=pl.ANY)
    return pl.pallas_call(
        functools.partial(front_kernel, count),
        out_shape=[
            shape((expert_rows * count, half_ff), bf16) for _ in range(3)
        ]
        + [
            shape((total, width), bf16),
            shape((packed.shape[0] * count, packed.shape[1]), bf16),
            shape((wide_rows, width), bf16),
            shape((wide_rows, q_cols), bf16),
            shape((wide_rows, k_cols), bf16),
            shape((wide_rows, k_cols), bf16),
            shape((wide_rows, q_cols), bf16),
            shape((rows, width), f32),
            shape((rows, width), bf16),
        ],
        in_specs=[vmem] + [anywhere] * 3 + [vmem] * 6,
        out_specs=[anywhere] * 4 + [vmem] * 8,
        scratch_shapes=[
            pltpu.VMEM((wide_rows, width), f32),
            pltpu.VMEM((rows, width), f32),
            pltpu.SemaphoreType.DMA((2, 2)),
        ]
        + Fetch.semaphores(count)
        + Gather.semaphores() * 2,
        compiler_params=pltpu.CompilerParams(
            collective_id=1, has_side_effects=True, vmem_limit_bytes=60 << 20
        ),
        name="front",
    )(packed, *experts, first, tokens, cosine, sine_table, mask, gain)


def gates_of(rows_bf, routes, router):
    lane = lanes_of(routes.shape).astype(jnp.float32)
    split = dot_f32(rows_bf, router, ((1,), (1,)))
    logits = split + (pltpu.roll(split, 128 - EXPERTS, 1) + pltpu.roll(split, 128 - 2 * EXPERTS, 1))
    named = jnp.zeros(routes.shape, jnp.float32)
    for k in range(TOPK):
        named = jnp.where(routes[:, k : k + 1] == lane, 1.0, named)
    masked = jnp.where(named > 0.0, logits, -jnp.inf)
    raised = jnp.exp(masked - jnp.max(masked, axis=1, keepdims=True))
    return raised / jnp.sum(raised, axis=1, keepdims=True)


class GradMoves:
    def __init__(self, count, grads, outs, send_sem, recv_sem, own_sem):
        self.count, self.grads, self.outs = count, grads, outs
        self.send_sem, self.recv_sem, self.own_sem = send_sem, recv_sem, own_sem
        self.holders = grads.shape[1]
        self.rows = grads.shape[2] // count
        self.issued = 0

    def copy(self, h, w, k, owner):
        me, side = lax.axis_index("dp"), lax.axis_index("tensor")
        peer = lax.rem(me + k, self.count)
        return pltpu.make_async_remote_copy(
            src_ref=self.grads.at[w, h, pl.ds(pl.multiple_of(peer * self.rows, self.rows), self.rows)],
            dst_ref=self.outs[w].at[owner * self.holders + h],
            send_sem=self.send_sem.at[h, w, k],
            recv_sem=self.recv_sem.at[h, w, k],
            device_id=(peer, side),
            device_id_type=MESH,
        )

    def own(self, h, w):
        me = lax.axis_index("dp")
        return pltpu.make_async_copy(
            self.grads.at[w, h, pl.ds(pl.multiple_of(me * self.rows, self.rows), self.rows)],
            self.outs[w].at[me * self.holders + h],
            self.own_sem.at[h, w],
        )

    def send(self, h):
        def step(i, carry):
            for w in range(3):
                self.copy(h, w, far_first(i, self.count), lax.axis_index("dp")).start()
            return carry

        lax.fori_loop(0, self.count - 1, step, 0)

    def some(self, h, amount):
        for _ in range(amount):
            if self.issued < self.count - 1:
                i = self.issued
                k = self.count // 2 + (1 - 2 * (i % 2)) * ((i + 1) // 2)
                for w in range(3):
                    self.copy(h, w, k, lax.axis_index("dp")).start()
                self.issued += 1

    def finish(self):
        me = lax.axis_index("dp")
        for h in range(self.holders):

            def step(k, carry):
                for w in range(3):
                    self.copy(h, w, k, me).wait_send()
                    self.copy(h, w, k, lax.rem(me - k + self.count, self.count)).wait_recv()
                return carry

            lax.fori_loop(1, self.count, step, 0)
            for w in range(3):
                self.own(h, w).wait()


def rms(values):
    return lax.rsqrt(jnp.mean(values * values, axis=1, keepdims=True) + eps_norm)


def back_norm(gradient, unit, scale, gain):
    inner = gradient * gain
    rows = scale * (inner - unit * jnp.mean(inner * unit, axis=1, keepdims=True))
    return rows, jnp.sum(gradient * unit, axis=0, keepdims=True)


SPREAD = (0, 1)


def back_kernel(count, sides, home, late, *refs):
    refs = list(refs)

    def take(n):
        taken = refs[:n]
        del refs[:n]
        return taken

    rows_hbm, tag_hbm = take(2)
    held_in, owned_in = take(3), take(3)
    router_ref, router_t = take(2)
    attn_ref, wide_first, q_ref, k_ref, v_ref, mixed_ref, hidden_ref, normed_ref, own_tag = take(9)
    grad_ref, tokens_ref, gain1_ref, gain2_ref, cos_ref, sin_ref, mask_ref = take(7)
    block_o, tokens_o, weights_o, logits_o, gains_o = take(5)
    moved_o = take(3)
    row_buf, tag_buf, load_sem, tile_gates, acc, grads = take(6)
    parts, firsts, home_out = take(3), take(3), take(3)
    sum_bufs = take(len(home) * 4)
    first_s, first_r, sum_s, sum_r = take(4)
    late_in, late_acc = take(2)
    late_bufs = take(len(late) * 4)
    late_s, late_r = take(2)
    moves = GradMoves(count, grads, moved_o, *take(3))
    weights, held_sem = take(3), take(1)[0]
    fetch = Fetch(count, 1, owned_in, [w.at[1] for w in weights], *take(3))
    lg_ref, gain_blk, wide_attn, mixed_grad, qkv_grad, part, got, pair_sem = take(8)
    spread_logits = Gather(lg_ref, logits_o, True, take(9))
    share_s, share_r, share_own = take(3)
    sums = Sum(home, parts, home_out, firsts, sum_bufs, sum_s, sum_r, firsts, first_s, first_r)
    last = Sum(late, [late_in], [weights_o], [late_acc], late_bufs, late_s, late_r)
    dp, side = lax.axis_index("dp"), lax.axis_index("tensor")
    rows = hidden_ref.shape[0]
    width = hidden_ref.shape[1]
    holders = weights[0].shape[0]
    tile = row_buf.shape[1]
    tiles = rows_hbm.shape[0] // tile
    total = count * sides
    me = dp * sides + side

    def place(k):
        peer = lax.rem(me + k, total)
        return (lax.div(peer, sides), lax.rem(peer, sides))

    def load(step):
        at = pl.ds(pl.multiple_of(lax.rem(step, tiles) * tile, tile), tile)
        slot = lax.rem(step, 2)
        return [
            pltpu.make_async_copy(rows_hbm.at[at], row_buf.at[slot], load_sem.at[0, slot]),
            pltpu.make_async_copy(tag_hbm.at[at], tag_buf.at[slot], load_sem.at[1, slot]),
        ]

    held = [pltpu.make_async_copy(held_in[w], weights[w].at[0], held_sem.at[w]) for w in range(3)]
    for each in load(0) + held:
        each.start()
    barrier = pltpu.get_barrier_semaphore()

    def greet(k, carry):
        pl.semaphore_signal(barrier, inc=1, device_id=place(k), device_id_type=MESH)
        return carry

    lax.fori_loop(1, total, greet, 0)
    pl.semaphore_wait(barrier, total - 1)
    fetch.start()
    for each in held:
        each.wait()

    def expert_step(step, carry):
        h, z = lax.div(step, tiles), lax.rem(step, tiles)
        slot = lax.rem(step, 2)

        @pl.when(step + 1 < holders * tiles)
        def _():
            for each in load(step + 1):
                each.start()

        @pl.when(step == tiles)
        def _():
            fetch.finish()

        for each in load(step):
            each.wait()
        rows_bf = row_buf[slot]
        moe = tag_buf[slot, :, :width].astype(jnp.float32)

        @pl.when(h == 0)
        def _():
            routes = tag_buf[slot, :, width:].astype(jnp.float32)
            tile_gates[z] = gates_of(rows_bf, routes, router_ref[...])

        gates = tile_gates[z]
        at = lanes_of(gates.shape) == dp * holders + h
        gate = jnp.sum(jnp.where(at, gates, 0.0), axis=1, keepdims=True)
        gate_w, up_w, down_w = (ref[h] for ref in weights)
        gate_pre = dot_f32(rows_bf, gate_w, ((1,), (0,)))
        up_pre = dot_f32(rows_bf, up_w, ((1,), (0,)))
        route_grad = (gate * moe).astype(jnp.bfloat16)
        inner_grad = dot_f32(route_grad, down_w, ((1,), (0,)))
        sigmoid_gate = jax.nn.sigmoid(gate_pre)
        activated = gate_pre * sigmoid_gate
        inner_act = (activated * up_pre).astype(jnp.bfloat16)
        gate_pre_grad = (
            inner_grad * up_pre * sigmoid_gate * (1.0 + gate_pre * (1.0 - sigmoid_gate))
        ).astype(jnp.bfloat16)
        up_pre_grad = (inner_grad * activated).astype(jnp.bfloat16)
        produced = dot_f32(inner_act, down_w, ((1,), (1,))).astype(jnp.bfloat16)
        produced = produced.astype(jnp.float32)
        gate_part = jnp.sum(moe * produced, axis=1, keepdims=True)
        slots = jnp.where(at, gate_part, 0.0)
        high = slots.astype(jnp.bfloat16).astype(jnp.float32)
        rest = slots - high
        middle = rest.astype(jnp.bfloat16).astype(jnp.float32)
        low = (rest - middle).astype(jnp.bfloat16).astype(jnp.float32)
        slots = high + (pltpu.roll(middle, EXPERTS, 1) + pltpu.roll(low, 2 * EXPERTS, 1))
        back = dot_f32(gate_pre_grad, gate_w, ((1,), (1,))) + dot_f32(
            up_pre_grad, up_w, ((1,), (1,))
        )
        made = (
            back.astype(jnp.bfloat16),
            slots.astype(jnp.bfloat16),
            (gate * produced).astype(jnp.bfloat16),
        )
        z1, z0 = lax.div(z, 2), lax.rem(z, 2)
        for which in range(3):
            ref = parts[which].at[z1, z0]
            block = made[which].reshape(2, 2, 2, rows, made[which].shape[1])

            @pl.when(h == 0)
            def _():
                ref[...] = block

            @pl.when(h > 0)
            def _():
                ref[...] = (ref[...].astype(jnp.float32) + block.astype(jnp.float32)).astype(
                    jnp.bfloat16
                )

        for w, (left, right) in enumerate(
            ((rows_bf, gate_pre_grad), (rows_bf, up_pre_grad), (route_grad, inner_act))
        ):
            product = dot_f32(right, left, ((0,), (0,)))

            @pl.when(z == 0)
            def _():
                acc[w] = product

            @pl.when(z > 0)
            def _():
                acc[w] += product

        @pl.when(h == holders - 1)
        def _():
            for which in range(3):
                sums.send_first(which, z)

        @pl.when(z == tiles - 1)
        def _():
            for w in range(3):
                grads[w, h] = acc[w].T.astype(jnp.bfloat16)
                moves.own(h, w).start()

            @pl.when(h < holders - 1)
            def _():
                moves.send(h)

        return carry

    lax.fori_loop(0, holders * tiles, expert_step, 0)
    final = holders - 1
    sums.run(lambda: moves.some(final, SPREAD[0]))

    def half(which):
        return pl.ds(pl.multiple_of(which * rows, rows), rows)

    routes = own_tag[:, width:].astype(jnp.float32)
    gates = gates_of(normed_ref[...], routes, router_ref[...])
    slots = home_out[1][...]
    gate_grad = slots + (pltpu.roll(slots, 128 - EXPERTS, 1) + pltpu.roll(slots, 128 - 2 * EXPERTS, 1))
    logits_grad = gates * (gate_grad - jnp.sum(gates * gate_grad, axis=1, keepdims=True))
    lg_ref[...] = logits_grad
    second_grad = home_out[0][...] + jnp.dot(
        logits_grad[:, :EXPERTS],
        router_t[...],
        precision=lax.Precision.HIGHEST,
        preferred_element_type=jnp.float32,
    )
    hidden = hidden_ref[...]
    scale_second = rms(hidden)
    hidden_back, ffn_gain_grad = back_norm(
        second_grad, hidden * scale_second, scale_second, gain2_ref[...]
    )
    hidden_grad = grad_ref[...].astype(jnp.float32) + hidden_back
    tokens_o[...] = hidden_grad
    wide_attn[half(side), :] = (residual_scale * hidden_grad).astype(jnp.bfloat16)
    spread = pltpu.make_async_remote_copy(
        src_ref=wide_attn.at[half(side)],
        dst_ref=wide_attn.at[half(side)],
        send_sem=pair_sem.at[0, 0],
        recv_sem=pair_sem.at[0, 1],
        device_id=partner("t"),
        device_id_type=MESH,
    )
    spread.start()
    spread_logits.start()
    later = spread_logits.steps()

    def meanwhile():
        moves.some(final, SPREAD[1])
        if later:
            later.pop(0)()

    block_o[...] = (hidden + residual_scale * home_out[2][...]).astype(jnp.bfloat16)
    for j in range(width // 128):
        gain_blk[width // 128 + j : width // 128 + j + 1, :] = chunk(ffn_gain_grad, j, 128)
    meanwhile()
    spread.wait()
    q_cols, k_cols = q_ref.shape[1], k_ref.shape[1]
    base = q_cols + 2 * k_cols
    pair_width = 2 * HEAD_DIM
    mixed_grad[...] = dot_f32(wide_attn[...], attn_ref[:, base:], ((1,), (0,))).astype(jnp.bfloat16)
    step = 256

    def keep(at, value):
        late_in[:, :, :, :, :, :, at : at + value.shape[1]] = value.astype(jnp.bfloat16).reshape(
            late_in.shape[:-1] + (value.shape[1],)
        )

    for i in range(q_cols // step):
        keep(
            base + i * step,
            dot_f32(wide_attn[...], chunk(mixed_ref, i, step), ((0,), (0,))),
        )
    meanwhile()
    cosine, sine = cos_ref[:, :pair_width], sin_ref[:, :pair_width]
    low = lanes_of((2 * rows, pair_width)) < HEAD_DIM
    held = None
    for g in range(q_cols // pair_width):
        query = stack_heads(chunk(q_ref, g, pair_width))
        keys = twice(chunk(k_ref, g // 2, pair_width), g % 2)
        values = twice(chunk(v_ref, g // 2, pair_width), g % 2)
        grad_heads = stack_heads(chunk(mixed_grad, g, pair_width))
        probs = probabilities(query, keys, mask_ref[...])
        dprobs = dot_f32(grad_heads, values, ((1,), (1,)))
        delta = jnp.sum(probs * dprobs, axis=1, keepdims=True)
        dscores = (probs * (dprobs - delta)).astype(jnp.bfloat16)
        dquery = unstack_heads(dot_f32(dscores, keys, ((1,), (0,)))) * score_scale
        qkv_grad[:, g * pair_width : (g + 1) * pair_width] = turn(
            dquery, cosine, sine, True
        ).astype(jnp.bfloat16)
        dkeys = dot_f32(dscores, query, ((0,), (0,)))
        dvalues = dot_f32(probs.astype(jnp.bfloat16), grad_heads, ((0,), (0,)))
        dkeys = dkeys + pltpu.roll(dkeys, HEAD_DIM, 1)
        dvalues = dvalues + pltpu.roll(dvalues, HEAD_DIM, 1)
        if g % 2 == 0:
            held = (dkeys, dvalues)
        else:
            j = g // 2 * pair_width
            dkeys = jnp.where(low, held[0], dkeys) * score_scale
            dvalues = jnp.where(low, held[1], dvalues)
            qkv_grad[:, q_cols + j : q_cols + j + pair_width] = turn(
                dkeys, cosine, sine, True
            ).astype(jnp.bfloat16)
            qkv_grad[:, q_cols + k_cols + j : q_cols + k_cols + j + pair_width] = dvalues.astype(
                jnp.bfloat16
            )
        meanwhile()
    for i in range(attn_ref.shape[0] // step):
        part[:, i * step : (i + 1) * step] = dot_f32(
            qkv_grad[...], attn_ref[i * step : (i + 1) * step, :base], ((1,), (1,))
        )
    narrowed = pltpu.make_async_remote_copy(
        src_ref=part.at[half(1 - side)],
        dst_ref=got,
        send_sem=pair_sem.at[1, 0],
        recv_sem=pair_sem.at[1, 1],
        device_id=partner("t"),
        device_id_type=MESH,
    )
    narrowed.start()
    meanwhile()
    for i in range(base // step):
        keep(i * step, dot_f32(wide_first[...], chunk(qkv_grad, i, step), ((0,), (0,))))
    last.start()
    moves.some(final, count)
    narrowed.wait()
    first_grad = part[half(side), :] + got[...]
    tokens = tokens_ref[...].astype(jnp.float32)
    scale_first = rms(tokens)
    tokens_back, attn_gain_grad = back_norm(
        first_grad, tokens * scale_first, scale_first, gain1_ref[...]
    )
    tokens_o[...] = tokens_o[...] + tokens_back
    for j in range(width // 128):
        gain_blk[j : j + 1, :] = chunk(attn_gain_grad, j, 128)

    def share(k, slot):
        return pltpu.make_async_remote_copy(
            src_ref=gain_blk,
            dst_ref=gains_o.at[slot],
            send_sem=share_s.at[k],
            recv_sem=share_r.at[k],
            device_id=place(k),
            device_id_type=MESH,
        )

    def share_start(k, carry):
        share(k, me).start()
        return carry

    def share_finish(k, carry):
        share(k, me).wait_send()
        share(k, lax.rem(me - k + total, total)).wait_recv()
        return carry

    lax.fori_loop(1, total, share_start, 0)
    own_gain = pltpu.make_async_copy(gain_blk, gains_o.at[me], share_own)
    own_gain.start()
    while later:
        later.pop(0)()
    last.run()
    spread_logits.finish()
    lax.fori_loop(1, total, share_finish, 0)
    own_gain.wait()
    moves.finish()


def back(rows_all, tagged_all, held, owned, router, router_t, attention, own_tag, own, tables):
    count, sides = lax.axis_size("dp"), lax.axis_size("tensor")
    attn_all, wide_first, query, key, value, mixed, hidden, normed = attention
    rows, width = hidden.shape
    total = rows_all.shape[0]
    columns = attn_all.shape[1]
    late_rows = attn_all.shape[0] // count
    holders = owned[0].shape[0] // count
    tall, half_ff = held[0].shape
    tile = total // 4
    bf16, f32 = jnp.bfloat16, jnp.float32
    shape = jax.ShapeDtypeStruct
    vmem, anywhere = pl.BlockSpec(memory_space=pltpu.VMEM), pl.BlockSpec(memory_space=pl.ANY)
    dma = pltpu.SemaphoreType.DMA
    home, late = home_pieces(width, 128), last_pieces(columns)
    widths = (width, 128, width)
    _, home_bufs, home_sems = Sum.scratch(home, rows, widths, 1)
    late_accs, late_bufs, late_sems = Sum.scratch(late, late_rows, (columns,))
    gain_rows = 2 * width // 128
    scratch = [
        pltpu.VMEM((2, tile, width), bf16),
        pltpu.VMEM((2, tile, tagged_all.shape[1]), bf16),
        dma((2, 2)),
        pltpu.VMEM((4, tile, 128), f32),
        pltpu.VMEM((3, half_ff, tall), f32),
        pltpu.VMEM((3, holders, tall, half_ff), bf16),
    ]
    scratch += [pltpu.VMEM((2, 2, 2, 2, 2, rows, w), bf16) for w in widths]
    scratch += [pltpu.VMEM((2, 2, 2, 2, rows, w), bf16) for w in widths]
    scratch += [pltpu.VMEM((rows, w), f32) for w in widths] + home_bufs
    scratch += [dma((3, 4)), dma((3, 4))] + home_sems
    scratch += [pltpu.VMEM((2, 2, 2, 2, 1, late_rows, columns), bf16)] + late_accs + late_bufs
    scratch += late_sems
    scratch += [dma((holders, 3, count)), dma((holders, 3, count)), dma((holders, 3))]
    scratch += [pltpu.VMEM((holders, tall, half_ff), bf16) for _ in range(3)] + [dma((3,))]
    scratch += Fetch.semaphores(count)
    scratch += [
        pltpu.VMEM((rows, 128), f32),
        pltpu.VMEM((gain_rows, 128), f32),
        pltpu.VMEM((2 * rows, width), bf16),
        pltpu.VMEM((2 * rows, query.shape[1]), bf16),
        pltpu.VMEM((2 * rows, columns - query.shape[1]), bf16),
        pltpu.VMEM((2 * rows, width), f32),
        pltpu.VMEM((rows, width), f32),
        dma((2, 2)),
    ]
    scratch += Gather.semaphores()
    scratch += [dma((count * sides,)), dma((count * sides,)), dma]
    return pl.pallas_call(
        functools.partial(back_kernel, count, sides, home, late),
        out_shape=[
            shape((rows, width), bf16),
            shape((rows, width), f32),
            shape((late_rows, columns), f32),
            shape((total, 128), f32),
            shape((count * sides, gain_rows, 128), f32),
        ]
        + [shape((holders * count, tall // count, half_ff), bf16) for _ in range(3)],
        in_specs=[anywhere] * 8 + [vmem] * 18,
        out_specs=[vmem] * 5 + [anywhere] * 3,
        scratch_shapes=scratch,
        compiler_params=pltpu.CompilerParams(
            collective_id=2, has_side_effects=True, vmem_limit_bytes=60 << 20
        ),
        name="back",
    )(
        rows_all,
        tagged_all,
        *held,
        *owned,
        router,
        router_t,
        *attention,
        own_tag,
        *own,
        *tables,
    )


def local_near(
    tokens,
    out_grad,
    lengths,
    routes,
    attn_gain,
    w_query,
    w_key,
    w_value,
    w_out,
    ffn_gain,
    w_router,
    w_gate,
    w_up,
    w_down,
):
    local_rows = tokens.shape[0]
    row_count = routes.shape[0]
    model_width = tokens.shape[1]
    own_row = lax.axis_index("tensor") * local_rows
    q_cols, k_cols = w_query.shape[1], w_key.shape[1]
    cuts = (q_cols, q_cols + k_cols, q_cols + 2 * k_cols)
    tokens_f32 = tokens.astype(jnp.float32)
    out_f32 = out_grad.astype(jnp.float32)
    own_routes = lax.dynamic_slice_in_dim(routes, own_row, local_rows, 0)
    position, allowed = seq_layout(lengths[0], row_count)
    places = jnp.arange(256, dtype=jnp.int32) % (HEAD_DIM // 2)
    frequency = rope_base ** (-(places.astype(jnp.float32) * 2.0) / HEAD_DIM)
    angles = position.astype(jnp.float32)[:, None] * frequency[None, :]
    tables = [jnp.cos(angles), jnp.sin(angles), allowed.astype(jnp.float32)]
    _, _, normed_first = norm_forward(tokens_f32, attn_gain)
    tagged = jnp.concatenate(
        [
            (residual_scale * out_f32).astype(jnp.bfloat16),
            jnp.pad(own_routes.astype(jnp.bfloat16), ((0, 0), (0, 128 - TOPK))),
        ],
        axis=1,
    )
    tagged_all = lax.all_gather(tagged, ("dp", "tensor"), axis=0, tiled=True)
    (
        local_gate,
        local_up,
        local_down,
        rows_all,
        full_attn,
        wide_first,
        query_flat,
        key_flat,
        value_flat,
        mixed_out,
        hidden,
        normed_second,
    ) = front(
        jnp.concatenate([w_query, w_key, w_value, w_out], axis=1),
        [w_gate, w_up, w_down],
        normed_first,
        tokens,
        *tables,
        ffn_gain[None, :],
        q_cols,
        k_cols,
    )
    router_t = w_router.T
    router_parts = jnp.pad(
        jnp.concatenate(split_three(router_t), axis=0), ((0, 128 - 3 * EXPERTS), (0, 0))
    )
    block_rows, tokens_grad, packed_grad, logits_all, shared, *expert_grads = back(
        rows_all,
        tagged_all,
        [local_gate, local_up, local_down],
        [w_gate, w_up, w_down],
        router_parts,
        router_t,
        [
            full_attn,
            wide_first,
            query_flat,
            key_flat,
            value_flat,
            mixed_out,
            hidden,
            normed_second,
        ],
        tagged,
        [out_grad, tokens, attn_gain[None, :], ffn_gain[None, :]],
        tables,
    )
    router_total = exact_dot(rows_all, logits_all[:, :EXPERTS], ((0,), (0,)))
    gains = jnp.sum(shared, axis=0).reshape(2, model_width)
    return (
        block_rows,
        tokens_grad,
        gains[0],
        packed_grad[:, : cuts[0]],
        packed_grad[:, cuts[0] : cuts[1]],
        packed_grad[:, cuts[1] : cuts[2]],
        packed_grad[:, cuts[2] :],
        gains[1],
        router_total,
        *[g.astype(jnp.float32) for g in expert_grads],
    )


def local_far(
    tokens,
    out_grad,
    lengths,
    routes,
    attn_gain,
    w_query,
    w_key,
    w_value,
    w_out,
    ffn_gain,
    w_router,
    w_gate,
    w_up,
    w_down,
):
    local_rows = tokens.shape[0]
    row_count = routes.shape[0]
    model_width = tokens.shape[1]
    dp_count = lax.axis_size("dp")
    replicas = max(1, dp_count // EXPERTS)
    holders = max(1, EXPERTS // dp_count)
    clusters = EXPERTS // holders
    half_ff = w_gate.shape[2]
    heads_here = w_query.shape[1] // HEAD_DIM
    kv_here = w_key.shape[1] // HEAD_DIM
    own_row = lax.axis_index("tensor") * local_rows
    groups = (
        None
        if replicas == 1
        else [[r * clusters + c for c in range(clusters)] for r in range(replicas)]
    )
    q_cols, k_cols = w_query.shape[1], w_key.shape[1]
    cuts = (q_cols, q_cols + k_cols, q_cols + 2 * k_cols)
    packed_attn = gather_weights(jnp.concatenate([w_query, w_key, w_value, w_out], axis=1))
    full_qkv = packed_attn[:, : cuts[2]]
    full_out = packed_attn[:, cuts[2] :]

    def spread_out(weight):
        grouped = weight.reshape(clusters, holders, weight.shape[1], half_ff)
        return jnp.broadcast_to(grouped[None], (replicas,) + grouped.shape).reshape(
            dp_count, holders, weight.shape[1], half_ff
        )

    def fetch(weight):
        moved = lax.all_to_all(spread_out(weight), "dp", split_axis=0, concat_axis=2, tiled=True)
        return moved.reshape(holders, model_width, half_ff)

    local_gate, local_up, local_down = fetch(w_gate), fetch(w_up), fetch(w_down)
    tokens_f32 = tokens.astype(jnp.float32)
    out_f32 = out_grad.astype(jnp.float32)
    position, allowed = seq_layout(lengths[0], row_count)
    cosine, sine_table = rope_tables(position, HEAD_DIM)
    unit_first, scale_first, normed_first = norm_forward(tokens_f32, attn_gain)
    both = spread_rows(
        jnp.concatenate(
            [normed_first, (residual_scale * out_f32).astype(jnp.bfloat16)], axis=1
        )
    )
    wide_first = both[:, :model_width]
    tagged = jnp.concatenate(
        [
            both[:, model_width:],
            jnp.pad(routes.astype(jnp.bfloat16), ((0, 0), (0, 128 - TOPK))),
        ],
        axis=1,
    )
    tagged_all = gather_dp(tagged, groups)
    moe_all = tagged_all[:, :model_width]
    routes_all = tagged_all[:, model_width : model_width + TOPK].astype(jnp.int32)
    qkv = jnp.dot(wide_first, full_qkv, preferred_element_type=jnp.float32)
    query_heads = rotate(
        qkv[:, : cuts[0]].reshape(row_count, heads_here, HEAD_DIM), cosine, sine_table
    ).astype(jnp.bfloat16)
    key_heads = rotate(
        qkv[:, cuts[0] : cuts[1]].reshape(row_count, kv_here, HEAD_DIM), cosine, sine_table
    ).astype(jnp.bfloat16)
    value_heads = qkv[:, cuts[1] :].astype(jnp.bfloat16).reshape(row_count, kv_here, HEAD_DIM)
    mixed_out, log_total = attend(query_heads, key_heads, value_heads, allowed)
    hidden = tokens_f32 + residual_scale * narrow(dot_f32(mixed_out, full_out, ((1,), (1,))))
    unit_second, scale_second, normed_second = norm_forward(hidden, ffn_gain)
    rows_all = gather_dp(spread_rows(normed_second), groups)

    expert_ids = jnp.arange(EXPERTS, dtype=jnp.int32)

    def gate_of(rows_bf, row_routes):
        picked = row_routes[:, :, None] == expert_ids[None, None, :]
        logits = exact_dot(rows_bf, w_router, ((1,), (0,)))
        named = jnp.any(picked, axis=1)
        masked = jnp.where(named, logits, -jnp.inf)
        raised = jnp.exp(masked - jnp.max(masked, axis=1, keepdims=True))
        return picked, named, raised / jnp.sum(raised, axis=1, keepdims=True)

    _, named_all, gates_all = gate_of(rows_all, routes_all)
    first_expert = lax.axis_index("dp") % clusters * holders
    out_part = back_part = gate_slots = 0.0
    grads = []
    for h in range(holders):
        gate = lax.dynamic_slice_in_dim(gates_all, first_expert + h, 1, 1)
        here = lax.dynamic_slice_in_dim(named_all, first_expert + h, 1, 1)
        gate_pre = dot_f32(rows_all, local_gate[h], ((1,), (0,)))
        up_pre = dot_f32(rows_all, local_up[h], ((1,), (0,)))
        sigmoid_gate = jax.nn.sigmoid(gate_pre)
        activated = gate_pre * sigmoid_gate
        inner_act = (activated * up_pre).astype(jnp.bfloat16)
        produced = dot_f32(inner_act, local_down[h], ((1,), (1,))).astype(jnp.bfloat16)
        produced = produced.astype(jnp.float32)
        out_part = out_part + jnp.where(here, gate * produced, 0.0)
        moe_f32 = moe_all.astype(jnp.float32)
        gate_part = jnp.sum(moe_f32 * produced, axis=1, keepdims=True)
        gate_slots = gate_slots + jnp.where(routes_all == first_expert + h, gate_part, 0.0)
        route_grad = jnp.where(here, gate * moe_f32, 0.0).astype(jnp.bfloat16)
        inner_grad = dot_f32(route_grad, local_down[h], ((1,), (0,)))
        gate_pre_grad = (
            inner_grad * up_pre * sigmoid_gate * (1.0 + gate_pre * (1.0 - sigmoid_gate))
        ).astype(jnp.bfloat16)
        up_pre_grad = (inner_grad * activated).astype(jnp.bfloat16)
        back = dot_f32(gate_pre_grad, local_gate[h], ((1,), (1,))) + dot_f32(
            up_pre_grad, local_up[h], ((1,), (1,))
        )
        back_part = back_part + back.astype(jnp.bfloat16).astype(jnp.float32)
        grads.append(
            (
                dot_f32(rows_all, gate_pre_grad, ((0,), (0,))).astype(jnp.bfloat16),
                dot_f32(rows_all, up_pre_grad, ((0,), (0,))).astype(jnp.bfloat16),
                dot_f32(route_grad, inner_act, ((0,), (0,))).astype(jnp.bfloat16),
            )
        )
    slot_parts = split_three(gate_slots)
    pad = jnp.zeros((rows_all.shape[0], 128 - 3 * TOPK), jnp.bfloat16)
    home = scatter_dp(
        jnp.concatenate(
            [back_part.astype(jnp.bfloat16)] + slot_parts + [pad, out_part.astype(jnp.bfloat16)],
            axis=1,
        ),
        groups,
    ).astype(jnp.float32)
    back_home = home[:, : model_width + 128]
    out_home = home[:, model_width + 128 :]
    slots = back_home[:, model_width:]
    gate_half = slots[:, :TOPK] + slots[:, TOPK : 2 * TOPK] + slots[:, 2 * TOPK : 3 * TOPK]
    own_back = narrow(
        jnp.concatenate(
            [back_home[:, :model_width], jnp.pad(gate_half, ((0, 0), (0, 128 - TOPK)))], axis=1
        )
    )
    expert_back = own_back[:, :model_width]
    gate_grad = own_back[:, model_width : model_width + TOPK]
    block_rows = (hidden + residual_scale * narrow(out_home)).astype(jnp.bfloat16)

    def send_home(index):
        stacked = jnp.stack([grads[h][index] for h in range(holders)])
        moved = lax.all_to_all(stacked[None], "dp", split_axis=2, concat_axis=0, tiled=True)
        return jnp.sum(
            moved.astype(jnp.float32).reshape(
                replicas, clusters * holders, moved.shape[2], half_ff
            ),
            axis=0,
        )

    own_routes = lax.dynamic_slice_in_dim(routes, own_row, local_rows, 0)
    picked_own, _, gates_dense = gate_of(normed_second, own_routes)
    gates_own = jnp.sum(jnp.where(picked_own, gates_dense[:, None, :], 0.0), axis=2)
    chosen_grad = gates_own * (gate_grad - jnp.sum(gates_own * gate_grad, axis=1, keepdims=True))
    logits_grad = jnp.sum(jnp.where(picked_own, chosen_grad[:, :, None], 0.0), axis=1)
    second_grad = expert_back + jnp.dot(logits_grad, w_router.T, precision=lax.Precision.HIGHEST)
    hidden_back, ffn_gain_grad = norm_backward(second_grad, unit_second, scale_second, ffn_gain)
    hidden_grad = out_f32 + hidden_back
    attn_grad = spread_rows((residual_scale * hidden_grad).astype(jnp.bfloat16))
    mixed_grad = jnp.dot(attn_grad, full_out, preferred_element_type=jnp.float32).astype(
        jnp.bfloat16
    )
    out_w_grad = dot_f32(attn_grad, mixed_out, ((0,), (0,)))
    dquery, key_grad, dvalues = attend_back(
        query_heads, key_heads, value_heads, allowed, log_total, mixed_grad
    )
    query_grad = (
        unrotate(dquery, cosine, sine_table)
        .astype(jnp.bfloat16)
        .reshape(row_count, heads_here * HEAD_DIM)
    )
    keys_grad = (
        unrotate(key_grad, cosine, sine_table)
        .astype(jnp.bfloat16)
        .reshape(row_count, kv_here * HEAD_DIM)
    )
    value_grad = dvalues.astype(jnp.bfloat16).reshape(row_count, kv_here * HEAD_DIM)
    qkv_grad = jnp.concatenate([query_grad, keys_grad, value_grad], axis=1)
    qkv_w_grad = dot_f32(wide_first, qkv_grad, ((0,), (0,)))
    packed_grad = scatter_weights(
        jnp.concatenate([qkv_w_grad, out_w_grad], axis=1).astype(jnp.bfloat16)
    ).astype(jnp.float32)
    first_grad = narrow(dot_f32(qkv_grad, full_qkv, ((1,), (1,))))
    tokens_back, attn_gain_grad = norm_backward(first_grad, unit_first, scale_first, attn_gain)
    tokens_grad = hidden_grad + tokens_back
    attn_gain_total, ffn_gain_total, router_total = lax.psum(
        (
            attn_gain_grad,
            ffn_gain_grad,
            exact_dot(normed_second, logits_grad, ((0,), (0,))),
        ),
        ("dp", "tensor"),
    )
    return (
        block_rows,
        tokens_grad,
        attn_gain_total,
        packed_grad[:, : cuts[0]],
        packed_grad[:, cuts[0] : cuts[1]],
        packed_grad[:, cuts[1] : cuts[2]],
        packed_grad[:, cuts[2] :],
        ffn_gain_total,
        router_total,
        send_home(0),
        send_home(1),
        send_home(2),
    )


def solution(mesh):
    placed = (
        P(("dp", "tensor"), None),
        P(("dp", "tensor"), None),
        P("dp", None),
        P("dp", None),
        P(),
        P("dp", "tensor"),
        P("dp", "tensor"),
        P("dp", "tensor"),
        P("dp", "tensor"),
        P(),
        P(),
        P(None, "dp", "tensor"),
        P(None, "dp", "tensor"),
        P(None, "dp", "tensor"),
    )
    near = mesh.shape["dp"] == 16 and mesh.shape["tensor"] == 2
    return jax.shard_map(
        local_near if near else local_far,
        mesh=mesh,
        in_specs=placed,
        out_specs=(
            P(("dp", "tensor"), None),
            P(("dp", "tensor"), None),
            P(),
            P("dp", "tensor"),
            P("dp", "tensor"),
            P("dp", "tensor"),
            P("dp", "tensor"),
            P(),
            P(),
            P(None, "dp", "tensor"),
            P(None, "dp", "tensor"),
            P(None, "dp", "tensor"),
        ),
        check_vma=False,
    )
```
